128 devices in a mesh: gx: 8 (over z, x_lo), gy: 16 (over x_hi, y, core).
Axes of the slice: x: 4 (x_hi: 2, x_lo: 2; x = x_hi * 2 + x_lo), y: 4, z: 4, core: 2. Of those that a mesh axis runs over, the one named last changes fastest.
Arguments:
- cot_vort: float32 [3, 16, 1536, 1024], P(None, None, 'gy', 'gx'), may hold values from -6 to 6
- cot_vel: float32 [3, 16, 1536, 1024], P(None, None, 'gy', 'gx'), may hold values from -6 to 6
- vorticity: bfloat16 [3, 16, 1536, 1024], P(None, None, 'gy', 'gx'), may hold values from -6 to 6
- velocity: bfloat16 [3, 16, 1536, 1024], P(None, None, 'gy', 'gx'), may hold values from -6 to 6
Outputs:
- grad_vort: float32 [3, 16, 1536, 1024], P(None, None, 'gy', 'gx')
- grad_vel: float32 [3, 16, 1536, 1024], P(None, None, 'gy', 'gx')
The draws below stay inside these ranges and needn't reach their ends.
All inputs are finite; a program needn't handle non-finite values.
Results may differ from the reference program's by a relative error of at most 0.008.
Values may be sent and summed in bfloat16 or wider, within the bound.
A program may use at most 128 MiB of HBM per device.

```python
import math
import jax
import jax.numpy as jnp
from jax import lax

X = 1024
Y = 1536
Z = 16


def level_of(rng, dims, pieces, least, top_value):
    level = 1.0
    for position, parts in pieces:
        heights = jax.random.uniform(jax.random.fold_in(jax.random.fold_in(rng, 6), position), (parts,), jnp.float32, least / len(pieces), top_value / len(pieces))
        level = level * jnp.repeat(jnp.exp(heights), dims[position] // parts).reshape((-1,) + (1,) * (len(dims) - 1 - position))
    return level


def bell_draw(key, extent, spread, reach, pieces=(), kind=jnp.bfloat16):
    result = spread * jax.random.normal(key, extent, jnp.float32)
    if pieces:
        result = result * level_of(key, extent, pieces, -0.22, 0.18)
    return jnp.clip(result, -reach, reach).astype(kind)


def setup_inputs(seed: int = 0) -> dict:
    seeds = jax.random.split(jax.random.key(seed), 5)
    cot_vort = bell_draw(seeds[0], (3, Z, Y, X), 1.0, 6.0, ((2, 16), (3, 8)), jnp.float32)
    cot_vel = bell_draw(seeds[1], (3, Z, Y, X), 1.0, 6.0, ((2, 16), (3, 8)), jnp.float32)
    vorticity = bell_draw(seeds[2], (3, Z, Y, X), 1.0, 6.0, ((2, 16), (3, 8)))
    velocity = bell_draw(seeds[3], (3, Z, Y, X), 1.0, 6.0, ((2, 16), (3, 8)))
    return {"cot_vort": cot_vort, "cot_vel": cot_vel, "vorticity": vorticity, "velocity": velocity}


step_size = 0.5


def rounded(value):
    return lax.optimization_barrier(value.astype(jnp.bfloat16)).astype(jnp.float32)


def phase_tables(first_index, second, length):
    product = (first_index[:, None] * second[None, :]) % length
    angles = product.astype(jnp.float32) * (2.0 * math.pi / length)
    return jnp.cos(angles), jnp.sin(angles)


def wave_numbers(indices, length):
    signed = jnp.where(indices < length // 2, indices, indices - length)
    retained = jnp.where(indices == length // 2, 0.0, 1.0).astype(jnp.float32)
    return signed.astype(jnp.float32) * (2.0 * math.pi / length), retained


def along_depth(stacked, cosine, sine, sign):
    cos_part = jnp.einsum("zk,czrmx->ckrmx", cosine, stacked, precision=lax.Precision.HIGHEST)
    sin_part = jnp.einsum("zk,czrmx->ckrmx", sine, stacked, precision=lax.Precision.HIGHEST)
    real_part = cos_part[:, :, 0] + sign * sin_part[:, :, 1]
    imag_part = cos_part[:, :, 1] - sign * sin_part[:, :, 0]
    return rounded(jnp.stack([real_part, imag_part], 2))


def along_width(real_part, imag_part, cosine, sine, sign):
    high = lax.Precision.HIGHEST
    out_real = jnp.dot(real_part, cosine, precision=high) + sign * jnp.dot(imag_part, sine, precision=high)
    out_imag = jnp.dot(imag_part, cosine, precision=high) - sign * jnp.dot(real_part, sine, precision=high)
    return out_real, out_imag


def curl_solve(real_part, imag_part, wave_x, wave_y, wave_z, retained):
    square = wave_x * wave_x + wave_y * wave_y + wave_z * wave_z
    weight = jnp.where(square > 0, retained / jnp.where(square > 0, square, 1.0), 0.0)

    def cross(vector):
        return jnp.stack([wave_y * vector[2] - wave_z * vector[1], wave_z * vector[0] - wave_x * vector[2], wave_x * vector[1] - wave_y * vector[0]])

    return -cross(imag_part) * weight, cross(real_part) * weight


def slope_whole(values, axis_number):
    return (jnp.roll(values, -1, axis_number) - jnp.roll(values, 1, axis_number)) * 0.5


def reference(cot_vort, cot_vel, vorticity, velocity):
    half_modes = Y // 2
    packed = rounded(cot_vel)
    row_index = jnp.arange(Y, dtype=jnp.int32)
    mode_index = jnp.arange(half_modes, dtype=jnp.int32)
    cosine_y, sine_y = phase_tables(row_index, mode_index, Y)
    forward_y = rounded(jnp.concatenate([cosine_y, -sine_y], 1))
    yspectrum = rounded(jnp.einsum("czyx,ym->czmx", packed, forward_y, precision=lax.Precision.HIGHEST))
    yspectrum = yspectrum.reshape(3, Z, 2, half_modes, X)
    depth_index = jnp.arange(Z, dtype=jnp.int32)
    cosine_z, sine_z = phase_tables(depth_index, depth_index, Z)
    cosine_z = rounded(cosine_z)
    sine_z = rounded(sine_z)
    zspectrum = along_depth(yspectrum, cosine_z, sine_z, 1.0)
    width_index = jnp.arange(X, dtype=jnp.int32)
    cosine_x, sine_x = phase_tables(width_index, width_index, X)
    cosine_x = rounded(cosine_x)
    sine_x = rounded(sine_x)
    xreal, ximag = along_width(zspectrum[:, :, 0], zspectrum[:, :, 1], cosine_x, sine_x, 1.0)
    wave_x, keep_x = wave_numbers(width_index, X)
    wave_z, keep_z = wave_numbers(depth_index, Z)
    wave_y = mode_index.astype(jnp.float32) * (2.0 * math.pi / Y)
    filtered_real, filtered_imag = curl_solve(xreal, ximag, wave_x[None, None, :], wave_y[None, :, None], wave_z[:, None, None], keep_z[:, None, None] * keep_x[None, None, :])
    back_real, back_imag = along_width(rounded(filtered_real), rounded(filtered_imag), cosine_x, sine_x, -1.0)
    xback = rounded(jnp.stack([back_real, back_imag], 2))
    zback = along_depth(xback, cosine_z, sine_z, -1.0)
    cosine_b, sine_b = phase_tables(mode_index, row_index, Y)
    doubling = jnp.where(mode_index == 0, 1.0, 2.0).astype(jnp.float32)[:, None]
    inverse_y = rounded(jnp.stack([cosine_b * doubling, -sine_b * doubling], 0))
    spatial = jnp.einsum("czrmx,rmy->czyx", zback, inverse_y, precision=lax.Precision.HIGHEST)
    spectral = rounded(spatial * (1.0 / (X * Y * Z)))
    adjoint = cot_vort + spectral
    velocity_full = velocity.astype(jnp.float32)
    vorticity_full = vorticity.astype(jnp.float32)
    axes_order = (3, 2, 1)
    grad_vort = jnp.stack([adjoint[j] + step_size * jnp.sum(adjoint * slope_whole(velocity_full, axes_order[j]), 0) for j in range(3)])
    total = jnp.zeros_like(adjoint)
    for j in range(3):
        total = total + slope_whole(vorticity_full[j:j + 1] * adjoint, axes_order[j])
    grad_vel = -step_size * total
    return grad_vort, grad_vel
```

```python
import math

import jax
import jax.numpy as jnp
import numpy as np
from jax import lax
from jax.experimental import pallas as pl
from jax.experimental.pallas import tpu as pltpu
from jax.sharding import PartitionSpec as P

step_size = 0.5
F32 = jnp.float32
BF16 = jnp.bfloat16
LANES = 128
ROWS = 16
MESH = pl.DeviceIdType.MESH


def seed(alpha, beta, length):
    turns = np.concatenate([beta, alpha], 0) % length
    angles = turns * (2.0 * np.pi / length)
    return np.stack([np.cos(angles), np.sin(angles)]).astype(np.float32)


def y_modes(Y, chunks):
    half = chunks // 2
    per = (Y // 2) // chunks
    row = np.arange(Y)
    chunk, part, index = row // (2 * per), (row // per) % 2, row % per
    return 2 * ((chunk % half) * per + index) + chunk // half, part


def tables(X, Y, chunks):
    modes, part = y_modes(Y, chunks)
    quarter = Y // 4
    yy = np.arange(Y // 2)
    start = np.arange(0, Y, ROWS)
    forward_y = seed(
        modes[start][:, None] * yy + quarter * part[start][:, None],
        2 * np.arange(ROWS)[:, None] * yy,
        Y,
    )
    block = np.arange(0, Y // 2, ROWS)
    inverse_y = seed(
        block[:, None] * modes + quarter * part, np.arange(ROWS)[:, None] * modes, Y
    )
    Q = X // 4
    k = np.arange(Q)
    freq = np.concatenate([4 * k + r for r in range(4) for _ in range(2)])
    shift = np.concatenate([np.full(Q, s * (X // 4)) for _ in range(4) for s in range(2)])
    block = np.arange(0, Q, ROWS)
    forward_x = seed(block[:, None] * freq - shift, np.arange(ROWS)[:, None] * freq, X)
    xx = np.concatenate([k, k])
    shift = np.concatenate([np.zeros(Q), np.full(Q, X // 4)]).astype(np.int64)
    first = np.concatenate([4 * block + r for r in range(4)])
    inverse_x = seed(first[:, None] * xx - shift, 4 * np.arange(ROWS)[:, None] * xx, X)
    return forward_y, inverse_y, forward_x, inverse_x


def combine(terms):
    total = None
    for factor, value in terms:
        if abs(factor) < 1e-12:
            continue
        if total is None:
            total = value if factor == 1.0 else (-value if factor == -1.0 else value * factor)
        elif factor == 1.0:
            total = total + value
        elif factor == -1.0:
            total = total - value
        else:
            total = total + value * factor
    return total


def trig(kind, product, Z):
    value = (math.cos if kind == "c" else math.sin)(2.0 * math.pi * (product % Z) / Z)
    nearest = round(value)
    return float(nearest) if abs(value - nearest) < 1e-12 else value


def depth_forward(f, Z):
    H = Z // 2
    even = [f[0]] + [f[z] + f[Z - z] for z in range(1, H)] + [f[H]]
    odd = [None] + [f[z] - f[Z - z] for z in range(1, H)]
    real, imag = [None] * H, [None] * H
    for k in range(H // 2 + 1):
        a = combine([(trig("c", k * z, Z), even[z]) for z in range(0, H + 1, 2)])
        b = combine([(trig("c", k * z, Z), even[z]) for z in range(1, H + 1, 2)])
        total = a if b is None else (b if a is None else a + b)
        real[k] = total
        if 0 < k < H - k:
            real[H - k] = a if b is None else (-b if a is None else a - b)
        if k == 0:
            continue
        a = combine([(trig("s", k * z, Z), odd[z]) for z in range(2, H, 2)])
        b = combine([(trig("s", k * z, Z), odd[z]) for z in range(1, H, 2)])
        imag[k] = -(a if b is None else (b if a is None else a + b))
        if k < H - k:
            imag[H - k] = -b if a is None else (a if b is None else a - b)
    planes = []
    for k in range(H):
        planes += [real[k], jnp.zeros_like(real[0]) if k == 0 else imag[k]]
    return planes


def depth_inverse(planes, Z):
    H = Z // 2
    s = [planes[2 * k] for k in range(H)]
    d = [planes[2 * k + 1] for k in range(H)]
    even, odd = [None] * (H + 1), [None] * (H + 1)
    for z in range(H // 2 + 1):
        a = combine([((1.0 if k == 0 else 2.0 * trig("c", k * z, Z)), s[k]) for k in range(0, H, 2)])
        b = combine([(2.0 * trig("c", k * z, Z), s[k]) for k in range(1, H, 2)])
        even[z] = a if b is None else a + b
        even[H - z] = a if b is None else a - b
        if z == 0:
            continue
        a = combine([(2.0 * trig("s", k * z, Z), d[k]) for k in range(2, H, 2)])
        b = combine([(2.0 * trig("s", k * z, Z), d[k]) for k in range(1, H, 2)])
        odd[z] = a if b is None else (b if a is None else a + b)
        odd[H - z] = -a if b is None else (b if a is None else b - a)
    out = [None] * Z
    out[0], out[H] = even[0], even[H]
    for z in range(1, H):
        out[z] = even[z] + odd[z]
        out[Z - z] = even[z] - odd[z]
    return out


def make_spectral(C, Z, yl, NX, NY):
    X, Y = NX * LANES, NY * yl
    assert NY == Z
    chunks = NX * 2
    per = (Y // 2) // chunks
    pair = 2 * per
    half_y = Y // 2
    Q = X // 4
    wide = Q // LANES
    scale = 2.0 / (X * Y * Z)
    seeds = tables(X, Y, chunks)

    def kernel(
        cv,
        sfy_h,
        siy_h,
        sfx_h,
        six_h,
        out,
        sfy,
        siy,
        sfx,
        six,
        fwd_y,
        inv_y,
        fwd_x,
        inv_x,
        weights,
        zb,
        fy,
        ys,
        xr,
        lx,
        raw,
        filt,
        xb,
        yr,
        sp,
        zr,
        seed_sem,
        send_sem,
        recv_sem,
    ):
        gx = lax.axis_index("gx")
        gy = lax.axis_index("gy")
        core = lax.rem(gy, 2)
        base = gy - core
        mine = gx * 2 + core

        barrier = pltpu.get_barrier_semaphore()

        def greet_y(k, carry):
            pl.semaphore_signal(
                barrier, inc=1, device_id=(gx, lax.rem(gy + k, NY)), device_id_type=MESH
            )
            return carry

        lax.fori_loop(1, NY, greet_y, 0)

        def greet_x(k, carry):
            t = lax.rem(mine + k, chunks)
            pl.semaphore_signal(
                barrier, inc=1, device_id=(t // 2, base + lax.rem(t, 2)), device_id_type=MESH
            )
            return carry

        lax.fori_loop(1, chunks, greet_x, 0)

        loads = []
        for i, (src, dst) in enumerate(((sfy_h, sfy), (sfx_h, sfx), (siy_h, siy), (six_h, six))):
            loads.append(pltpu.make_async_copy(src, dst, seed_sem.at[i]))
            loads[-1].start()

        def z_block(c, b):
            rows = pl.ds(pl.multiple_of(b * ROWS, ROWS), ROWS)
            planes = depth_forward([cv[c, z, rows, :] for z in range(Z)], Z)
            for k in range(Z):
                zb[c, k, rows, :] = planes[k].astype(BF16)

        def send_planes(c):
            row = pl.ds(pl.multiple_of(gy * yl, yl), yl)

            def body(k, carry):
                dst = lax.rem(gy + k, NY)
                pltpu.make_async_remote_copy(
                    src_ref=zb.at[c, dst],
                    dst_ref=fy.at[c, row],
                    send_sem=send_sem.at[0, c],
                    recv_sem=recv_sem.at[0, c],
                    device_id=(gx, dst),
                    device_id_type=MESH,
                ).start()
                return carry

            lax.fori_loop(1, NY, body, 0)
            pltpu.make_async_copy(zb.at[c, gy], fy.at[c, row], recv_sem.at[0, c]).start()

        for c in range(C):
            lax.fori_loop(0, yl // ROWS, lambda b, carry, c=c: (z_block(c, b), carry)[1], 0)
            if c == 0:
                pl.semaphore_wait(barrier, NY - 1 + chunks - 1)
            send_planes(c)

        def build(dst, table, count, width):
            def body(a, carry):
                row = pl.ds(ROWS + a, 1)
                value = table[0, 0:ROWS, :] * table[0, row, :] - table[1, 0:ROWS, :] * table[1, row, :]
                dst[pl.ds(pl.multiple_of(a * ROWS, ROWS), ROWS), :] = value.astype(BF16)
                return carry

            lax.fori_loop(0, count, body, 0)

        loads[0].wait()
        build(fwd_y, sfy, Y // ROWS, half_y)

        def y_stage(c, carry):
            pltpu.make_async_copy(fy.at[c], fy.at[c], recv_sem.at[0, c]).wait()
            low = fy[c, 0:half_y, :].astype(F32)
            high = fy[c, half_y:Y, :].astype(F32)
            ys[c, 0:half_y, :] = jnp.dot(
                fwd_y[0:half_y, :], (low + high).astype(BF16), preferred_element_type=F32
            ).astype(BF16)
            ys[c, half_y:Y, :] = jnp.dot(
                fwd_y[half_y:Y, :], (low - high).astype(BF16), preferred_element_type=F32
            ).astype(BF16)

            def body(k, carry):
                t = lax.rem(mine + k, chunks)
                pltpu.make_async_remote_copy(
                    src_ref=ys.at[c, pl.ds(pl.multiple_of(t * pair, pair), pair)],
                    dst_ref=xr.at[c, core, gx],
                    send_sem=send_sem.at[1, c],
                    recv_sem=recv_sem.at[1, c],
                    device_id=(t // 2, base + lax.rem(t, 2)),
                    device_id_type=MESH,
                ).start()
                return carry

            lax.fori_loop(1, chunks, body, 0)
            pltpu.make_async_copy(
                ys.at[c, pl.ds(pl.multiple_of(mine * pair, pair), pair)],
                xr.at[c, core, gx],
                recv_sem.at[1, c],
            ).start()
            return carry

        lax.fori_loop(0, C, y_stage, 0)

        loads[1].wait()
        build(fwd_x, sfx, Q // ROWS, 8 * Q)
        loads[2].wait()
        build(inv_y, siy, half_y // ROWS, Y)
        loads[3].wait()
        build(inv_x, six, 4 * Q // ROWS, 2 * Q)

        depth_wave = (gy // 2).astype(F32) * (2.0 * math.pi / Z)
        chunk_half = mine // (chunks // 2)
        first_mode = 2 * lax.rem(mine, chunks // 2) * per + chunk_half
        mode = first_mode + 2 * lax.broadcasted_iota(jnp.int32, (per, Q), 0)
        wave_y = mode.astype(F32) * (2.0 * math.pi / Y)
        for r in range(4):
            kx = 4 * lax.broadcasted_iota(jnp.int32, (per, Q), 1) + r
            wave_x = jnp.where(kx < X // 2, kx, kx - X).astype(F32) * (2.0 * math.pi / X)
            square = wave_x * wave_x + wave_y * wave_y + depth_wave * depth_wave
            weight = jnp.where(square > 0, 1.0 / jnp.where(square > 0, square, 1.0), 0.0)
            weight = jnp.where(kx == X // 2, 0.0, weight)
            weight = jnp.where(mode == 0, 0.5 * weight, weight)
            weights[r, 0] = weight * wave_x
            weights[r, 1] = weight * wave_y
            weights[r, 2] = weight * depth_wave

        def x_stage(c, carry):
            pltpu.make_async_copy(xr.at[c], xr.at[c], recv_sem.at[1, c]).wait()
            for p in range(2):
                for b in range(per // ROWS):
                    for h in range(wide):
                        a = []
                        for part in range(2):
                            rows = slice(part * per + b * ROWS, part * per + (b + 1) * ROWS)
                            a.append([xr[c, p, j * wide + h, rows, :].astype(F32) for j in range(4)])
                        (r0, r1, r2, r3), (i0, i1, i2, i3) = a
                        sr, dr, tr, er = r0 + r2, r0 - r2, r1 + r3, r1 - r3
                        si, di, ti, ei = i0 + i2, i0 - i2, i1 + i3, i1 - i3
                        values = (
                            (sr + tr, si + ti),
                            (dr + ei, di - er),
                            (sr - tr, si - ti),
                            (dr - ei, di + er),
                        )
                        for r in range(4):
                            for part in range(2):
                                row = p * pair + part * per + b * ROWS
                                lx[r, row : row + ROWS, h * LANES : (h + 1) * LANES] = values[r][
                                    part
                                ].astype(BF16)
            for r in range(4):
                raw[c, r] = jnp.dot(
                    lx[r], fwd_x[:, r * 2 * Q : (r + 1) * 2 * Q], preferred_element_type=F32
                )
            return carry

        lax.fori_loop(0, C, x_stage, 0)

        def filter_block(r, carry):
            for b in range(per // ROWS):
                for h in range(wide):
                    cols = slice(h * LANES, (h + 1) * LANES)
                    sins = slice(Q + h * LANES, Q + (h + 1) * LANES)

                    def spectrum(c, p):
                        re = slice(p * pair + b * ROWS, p * pair + (b + 1) * ROWS)
                        im = slice(p * pair + per + b * ROWS, p * pair + per + (b + 1) * ROWS)
                        real = raw[c, r, re, cols] + raw[c, r, im, sins]
                        imag = raw[c, r, im, cols] - raw[c, r, re, sins]
                        return real, imag

                    wrow = slice(b * ROWS, (b + 1) * ROWS)
                    ax = weights[r, 0, wrow, cols]
                    ay = weights[r, 1, wrow, cols]
                    az = weights[r, 2, wrow, cols]
                    (rx, sx), (ry, sy), (rz, sz) = [spectrum(c, 0) for c in range(3)]
                    (ux, vx), (uy, vy), (uz, vz) = [spectrum(c, 1) for c in range(3)]
                    result = (
                        (
                            (az * uy - ay * sz, ay * rz + az * vy),
                            (ay * vz + az * ry, az * sy - ay * uz),
                        ),
                        (
                            (ax * sz - az * ux, -(ax * rz + az * vx)),
                            (-(ax * vz + az * rx), ax * uz - az * sx),
                        ),
                        (
                            (ay * sx - ax * sy, ax * ry - ay * rx),
                            (ax * vy - ay * vx, ay * ux - ax * uy),
                        ),
                    )
                    for c in range(3):
                        for p in range(2):
                            for part in range(2):
                                row = p * pair + part * per + b * ROWS
                                filt[c, r, row : row + ROWS, cols] = result[c][p][part].astype(BF16)
            return carry

        lax.fori_loop(0, 4, filter_block, 0)

        def x_back(c, carry):
            for r in range(4):
                raw[c, r] = jnp.dot(
                    filt[c, r], inv_x[r * Q : (r + 1) * Q, :], preferred_element_type=F32
                )
            for p in range(2):
                for b in range(per // ROWS):
                    for h in range(wide):
                        cols = slice(h * LANES, (h + 1) * LANES)
                        sins = slice(Q + h * LANES, Q + (h + 1) * LANES)
                        re = slice(p * pair + b * ROWS, p * pair + (b + 1) * ROWS)
                        im = slice(p * pair + per + b * ROWS, p * pair + per + (b + 1) * ROWS)
                        real = [raw[c, r, re, cols] - raw[c, r, im, sins] for r in range(4)]
                        imag = [raw[c, r, re, sins] + raw[c, r, im, cols] for r in range(4)]
                        sr, dr, tr, er = real[0] + real[2], real[0] - real[2], real[1] + real[3], real[1] - real[3]
                        si, di, ti, ei = imag[0] + imag[2], imag[0] - imag[2], imag[1] + imag[3], imag[1] - imag[3]
                        values = (
                            (sr + tr, si + ti),
                            (dr - ei, di + er),
                            (sr - tr, si - ti),
                            (dr + ei, di - er),
                        )
                        for j in range(4):
                            for part in range(2):
                                row = part * per + b * ROWS
                                xb[c, p, j * wide + h, row : row + ROWS, :] = values[j][part].astype(BF16)

            dst = pl.ds(pl.multiple_of(mine * pair, pair), pair)

            def body(k, carry):
                t = lax.rem(mine + k, chunks)
                pltpu.make_async_remote_copy(
                    src_ref=xb.at[c, lax.rem(t, 2), t // 2],
                    dst_ref=yr.at[c, dst],
                    send_sem=send_sem.at[2, c],
                    recv_sem=recv_sem.at[2, c],
                    device_id=(t // 2, base + lax.rem(t, 2)),
                    device_id_type=MESH,
                ).start()
                return carry

            lax.fori_loop(1, chunks, body, 0)
            pltpu.make_async_copy(xb.at[c, core, gx], yr.at[c, dst], recv_sem.at[2, c]).start()
            return carry

        lax.fori_loop(0, C, x_back, 0)

        def y_back(c, carry):
            pltpu.make_async_copy(yr.at[c], yr.at[c], recv_sem.at[2, c]).wait()
            even = jnp.dot(inv_y[:, 0:half_y], yr[c, 0:half_y, :], preferred_element_type=F32)
            odd = jnp.dot(inv_y[:, half_y:Y], yr[c, half_y:Y, :], preferred_element_type=F32)
            sp[c, 0:half_y, :] = (even + odd).astype(BF16)
            sp[c, half_y:Y, :] = (even - odd).astype(BF16)

            def body(k, carry):
                dst = lax.rem(gy + k, NY)
                pltpu.make_async_remote_copy(
                    src_ref=sp.at[c, pl.ds(pl.multiple_of(dst * yl, yl), yl)],
                    dst_ref=zr.at[c, gy],
                    send_sem=send_sem.at[3, c],
                    recv_sem=recv_sem.at[3, c],
                    device_id=(gx, dst),
                    device_id_type=MESH,
                ).start()
                return carry

            lax.fori_loop(1, NY, body, 0)
            pltpu.make_async_copy(
                sp.at[c, pl.ds(pl.multiple_of(gy * yl, yl), yl)], zr.at[c, gy], recv_sem.at[3, c]
            ).start()
            return carry

        lax.fori_loop(0, C, y_back, 0)

        def z_back(c, carry):
            pltpu.make_async_copy(zr.at[c], zr.at[c], recv_sem.at[3, c]).wait()

            def body(b, carry):
                rows = pl.ds(pl.multiple_of(b * ROWS, ROWS), ROWS)
                values = depth_inverse(
                    [zr[c, k, rows, :].astype(F32) * scale for k in range(Z)], Z
                )
                for z in range(Z):
                    out[c, z, rows, :] = values[z]
                return carry

            return lax.fori_loop(0, yl // ROWS, body, carry)

        lax.fori_loop(0, C, z_back, 0)

        for c in range(C):
            left = zb.at[c, 0 : NY - 1]
            pltpu.make_async_copy(left, left, send_sem.at[0, c]).wait()
            left = ys.at[c, 0 : (chunks - 1) * pair]
            pltpu.make_async_copy(left, left, send_sem.at[1, c]).wait()
            left = yr.at[c, 0 : (chunks - 1) * pair]
            pltpu.make_async_copy(left, left, send_sem.at[2, c]).wait()
            left = sp.at[c, 0 : (NY - 1) * yl]
            pltpu.make_async_copy(left, left, send_sem.at[3, c]).wait()

    def vmem(shape, dtype=BF16):
        return pltpu.VMEM(shape, dtype)

    scratch = [vmem(s.shape, F32) for s in seeds]
    scratch += [
        vmem((Y, half_y)),
        vmem((half_y, Y)),
        vmem((Q, 8 * Q)),
        vmem((4 * Q, 2 * Q)),
        vmem((4, 3, per, Q), F32),
        vmem((C, Z, yl, LANES)),
        vmem((C, Y, LANES)),
        vmem((C, Y, LANES)),
        vmem((C, 2, NX, pair, LANES)),
        vmem((4, 2 * pair, Q)),
        vmem((C, 4, 2 * pair, 2 * Q), F32),
        vmem((C, 4, 2 * pair, Q)),
        vmem((C, 2, NX, pair, LANES)),
        vmem((C, Y, LANES)),
        vmem((C, Y, LANES)),
        vmem((C, Z, yl, LANES)),
        pltpu.SemaphoreType.DMA((4,)),
        pltpu.SemaphoreType.DMA((4, C)),
        pltpu.SemaphoreType.DMA((4, C)),
    ]
    call = pl.pallas_call(
        kernel,
        out_shape=jax.ShapeDtypeStruct((C, Z, yl, LANES), F32),
        in_specs=[pl.BlockSpec(memory_space=pltpu.VMEM)] + [pl.BlockSpec(memory_space=pl.ANY)] * 4,
        out_specs=pl.BlockSpec(memory_space=pltpu.VMEM),
        scratch_shapes=scratch,
        compiler_params=pltpu.CompilerParams(
            collective_id=0, has_side_effects=True, vmem_limit_bytes=56 << 20
        ),
        name="spectral",
    )

    def run(cot_vel):
        return call(cot_vel, *[jnp.asarray(s) for s in seeds])

    return run


def extended(block, sides, width):
    for axis, dim in sides:
        count = lax.axis_size(axis)
        forward = [(i, i + 1) for i in range(count - 1)]
        forward.append((count - 1, 0))
        backward = [(target, source) for source, target in forward]
        low = lax.ppermute(
            lax.slice_in_dim(block, block.shape[dim] - width, None, axis=dim), axis, forward
        )
        high = lax.ppermute(lax.slice_in_dim(block, 0, width, axis=dim), axis, backward)
        block = jnp.concatenate([low, block, high], axis=dim)
    return block


def slope(padded, direction):
    if direction == 0:
        return (padded[:, :, 1:-1, 2:] - padded[:, :, 1:-1, :-2]) * 0.5
    if direction == 1:
        return (padded[:, :, 2:, 1:-1] - padded[:, :, :-2, 1:-1]) * 0.5
    inner = padded[:, :, 1:-1, 1:-1]
    return (jnp.roll(inner, -1, 1) - jnp.roll(inner, 1, 1)) * 0.5


def stretch_terms(adjoint, velocity_pad, vorticity_pad, adjoint_pad):
    grad_vort = jnp.stack(
        [adjoint[j] + step_size * jnp.sum(adjoint * slope(velocity_pad, j), 0) for j in range(3)]
    )
    total = jnp.zeros_like(adjoint)
    for j in range(3):
        total = total + slope(vorticity_pad[j : j + 1] * adjoint_pad, j)
    return (grad_vort, -step_size * total)


def local(cot_vort, cot_vel, vorticity, velocity):
    C, Z, yl, _ = cot_vel.shape
    spectral = make_spectral(C, Z, yl, lax.axis_size("gx"), lax.axis_size("gy"))(cot_vel)
    adjoint = cot_vort + spectral
    stacked = jnp.concatenate(
        [velocity.astype(jnp.float32), vorticity.astype(jnp.float32), adjoint], 0
    )
    padded = extended(stacked.astype(jnp.bfloat16), (("gx", 3), ("gy", 2)), 1).astype(stacked.dtype)
    return stretch_terms(adjoint, padded[:3], padded[3:6], padded[6:])


def solution(mesh):
    return jax.shard_map(
        local,
        mesh=mesh,
        in_specs=(
            P(None, None, "gy", "gx"),
            P(None, None, "gy", "gx"),
            P(None, None, "gy", "gx"),
            P(None, None, "gy", "gx"),
        ),
        out_specs=(P(None, None, "gy", "gx"), P(None, None, "gy", "gx")),
        check_vma=False,
    )
```

```python
import math

import jax
import jax.numpy as jnp
import numpy as np
from jax import lax
from jax.experimental import pallas as pl
from jax.experimental.pallas import tpu as pltpu
from jax.sharding import PartitionSpec as P

step_size = 0.5
F32 = jnp.float32
BF16 = jnp.bfloat16
LANES = 128
ROWS = 16
MESH = pl.DeviceIdType.MESH


def seed(alpha, beta, length):
    turns = np.concatenate([beta, alpha], 0) % length
    angles = turns * (2.0 * np.pi / length)
    return np.stack([np.cos(angles), np.sin(angles)]).astype(np.float32)


def y_modes(Y, chunks):
    half = chunks // 2
    per = (Y // 2) // chunks
    row = np.arange(Y)
    chunk, part, index = row // (2 * per), (row // per) % 2, row % per
    return 2 * ((chunk % half) * per + index) + chunk // half, part


def tables(X, Y, chunks):
    modes, part = y_modes(Y, chunks)
    quarter = Y // 4
    yy = np.arange(Y // 2)
    start = np.arange(0, Y, ROWS)
    forward_y = seed(
        modes[start][:, None] * yy + quarter * part[start][:, None],
        2 * np.arange(ROWS)[:, None] * yy,
        Y,
    )
    block = np.arange(0, Y // 2, ROWS)
    inverse_y = seed(
        block[:, None] * modes + quarter * part, np.arange(ROWS)[:, None] * modes, Y
    )
    Q = X // 4
    k = np.arange(Q)
    freq = np.concatenate([4 * k + r for r in range(4) for _ in range(2)])
    shift = np.concatenate([np.full(Q, s * (X // 4)) for _ in range(4) for s in range(2)])
    block = np.arange(0, Q, ROWS)
    forward_x = seed(block[:, None] * freq - shift, np.arange(ROWS)[:, None] * freq, X)
    xx = np.concatenate([k, k])
    shift = np.concatenate([np.zeros(Q), np.full(Q, X // 4)]).astype(np.int64)
    first = np.concatenate([4 * block + r for r in range(4)])
    inverse_x = seed(first[:, None] * xx - shift, 4 * np.arange(ROWS)[:, None] * xx, X)
    return forward_y, inverse_y, forward_x, inverse_x


def combine(terms):
    total = None
    for factor, value in terms:
        if abs(factor) < 1e-12:
            continue
        if total is None:
            total = value if factor == 1.0 else (-value if factor == -1.0 else value * factor)
        elif factor == 1.0:
            total = total + value
        elif factor == -1.0:
            total = total - value
        else:
            total = total + value * factor
    return total


def trig(kind, product, Z):
    value = (math.cos if kind == "c" else math.sin)(2.0 * math.pi * (product % Z) / Z)
    nearest = round(value)
    return float(nearest) if abs(value - nearest) < 1e-12 else value


def depth_forward(f, Z):
    H = Z // 2
    even = [f[0]] + [f[z] + f[Z - z] for z in range(1, H)] + [f[H]]
    odd = [None] + [f[z] - f[Z - z] for z in range(1, H)]
    real, imag = [None] * H, [None] * H
    for k in range(H // 2 + 1):
        a = combine([(trig("c", k * z, Z), even[z]) for z in range(0, H + 1, 2)])
        b = combine([(trig("c", k * z, Z), even[z]) for z in range(1, H + 1, 2)])
        total = a if b is None else (b if a is None else a + b)
        real[k] = total
        if 0 < k < H - k:
            real[H - k] = a if b is None else (-b if a is None else a - b)
        if k == 0:
            continue
        a = combine([(trig("s", k * z, Z), odd[z]) for z in range(2, H, 2)])
        b = combine([(trig("s", k * z, Z), odd[z]) for z in range(1, H, 2)])
        imag[k] = -(a if b is None else (b if a is None else a + b))
        if k < H - k:
            imag[H - k] = -b if a is None else (a if b is None else a - b)
    planes = []
    for k in range(H):
        planes += [real[k], jnp.zeros_like(real[0]) if k == 0 else imag[k]]
    return planes


def depth_inverse(planes, Z):
    H = Z // 2
    s = [planes[2 * k] for k in range(H)]
    d = [planes[2 * k + 1] for k in range(H)]
    even, odd = [None] * (H + 1), [None] * (H + 1)
    for z in range(H // 2 + 1):
        a = combine([((1.0 if k == 0 else 2.0 * trig("c", k * z, Z)), s[k]) for k in range(0, H, 2)])
        b = combine([(2.0 * trig("c", k * z, Z), s[k]) for k in range(1, H, 2)])
        even[z] = a if b is None else a + b
        even[H - z] = a if b is None else a - b
        if z == 0:
            continue
        a = combine([(2.0 * trig("s", k * z, Z), d[k]) for k in range(2, H, 2)])
        b = combine([(2.0 * trig("s", k * z, Z), d[k]) for k in range(1, H, 2)])
        odd[z] = a if b is None else (b if a is None else a + b)
        odd[H - z] = -a if b is None else (b if a is None else b - a)
    out = [None] * Z
    out[0], out[H] = even[0], even[H]
    for z in range(1, H):
        out[z] = even[z] + odd[z]
        out[Z - z] = even[z] - odd[z]
    return out


def make_spectral(C, Z, yl, NX, NY):
    X, Y = NX * LANES, NY * yl
    assert NY == Z
    chunks = NX * 2
    per = (Y // 2) // chunks
    pair = 2 * per
    half_y = Y // 2
    Q = X // 4
    wide = Q // LANES
    scale = 2.0 / (X * Y * Z)
    seeds = tables(X, Y, chunks)

    def kernel(
        cv_h,
        cw_h,
        ve_h,
        vo_h,
        sfy_h,
        siy_h,
        sfx_h,
        six_h,
        adj_h,
        halo_rows,
        halo_cols,
        cv,
        adj,
        ve,
        vo,
        rows_f,
        cols_f,
        rows_out,
        cols_out,
        rows_in,
        cols_in,
        sfy,
        siy,
        sfx,
        six,
        fwd_y,
        inv_y,
        fwd_x,
        inv_x,
        weights,
        zb,
        fy,
        ys,
        xr,
        lx,
        raw,
        filt,
        xb,
        yr,
        sp,
        zr,
        load_sem,
        store_sem,
        seed_sem,
        send_sem,
        recv_sem,
        halo_send,
        halo_recv,
    ):
        gx = lax.axis_index("gx")
        gy = lax.axis_index("gy")
        core = lax.rem(gy, 2)
        base = gy - core
        mine = gx * 2 + core

        cv_loads = []
        for c in range(C):
            cv_loads.append(pltpu.make_async_copy(cv_h.at[c], cv.at[c], load_sem.at[c]))
            cv_loads[-1].start()
        field_loads = []
        for i, (src, dst) in enumerate(((ve_h, ve), (vo_h, vo), (cw_h, adj))):
            field_loads.append(pltpu.make_async_copy(src, dst, load_sem.at[C + i]))
            field_loads[-1].start()

        barrier = pltpu.get_barrier_semaphore()
        right, left = (lax.rem(gx + 1, NX), gy), (lax.rem(gx + NX - 1, NX), gy)
        after, before = (gx, lax.rem(gy + 1, NY)), (gx, lax.rem(gy + NY - 1, NY))

        def greet_y(k, carry):
            pl.semaphore_signal(
                barrier, inc=1, device_id=(gx, lax.rem(gy + k, NY)), device_id_type=MESH
            )
            return carry

        lax.fori_loop(1, NY, greet_y, 0)

        def greet_x(k, carry):
            t = lax.rem(mine + k, chunks)
            pl.semaphore_signal(
                barrier, inc=1, device_id=(t // 2, base + lax.rem(t, 2)), device_id_type=MESH
            )
            return carry

        lax.fori_loop(1, chunks, greet_x, 0)

        loads = []
        for i, (src, dst) in enumerate(((sfy_h, sfy), (sfx_h, sfx), (siy_h, siy), (six_h, six))):
            loads.append(pltpu.make_async_copy(src, dst, seed_sem.at[i]))
            loads[-1].start()

        def z_block(c, b):
            rows = pl.ds(pl.multiple_of(b * ROWS, ROWS), ROWS)
            planes = depth_forward([cv[c, z, rows, :] for z in range(Z)], Z)
            for k in range(Z):
                zb[c, k, rows, :] = planes[k].astype(BF16)

        def send_planes(c):
            row = pl.ds(pl.multiple_of(gy * yl, yl), yl)

            def body(k, carry):
                dst = lax.rem(gy + k, NY)
                pltpu.make_async_remote_copy(
                    src_ref=zb.at[c, dst],
                    dst_ref=fy.at[c, row],
                    send_sem=send_sem.at[0, c],
                    recv_sem=recv_sem.at[0, c],
                    device_id=(gx, dst),
                    device_id_type=MESH,
                ).start()
                return carry

            lax.fori_loop(1, NY, body, 0)
            pltpu.make_async_copy(zb.at[c, gy], fy.at[c, row], recv_sem.at[0, c]).start()

        for c in range(C):
            cv_loads[c].wait()
            lax.fori_loop(0, yl // ROWS, lambda b, carry, c=c: (z_block(c, b), carry)[1], 0)
            if c == 0:
                pl.semaphore_wait(barrier, NY - 1 + chunks - 1)
            send_planes(c)

        lane = lax.broadcasted_iota(jnp.int32, (yl, LANES), 1)

        def send_halo(stage, count):
            first = 4 * stage
            copies = []
            for i, (src, dst, device) in enumerate(
                (
                    (rows_out.at[1, first : first + count], rows_in.at[0, first : first + count], after),
                    (rows_out.at[0, first : first + count], rows_in.at[1, first : first + count], before),
                    (cols_out.at[stage], cols_in.at[0, stage], right),
                    (cols_out.at[stage], cols_in.at[1, stage], left),
                )
            ):
                copies.append(
                    pltpu.make_async_remote_copy(
                        src_ref=src,
                        dst_ref=dst,
                        send_sem=halo_send.at[stage, i],
                        recv_sem=halo_recv.at[stage, i],
                        device_id=device,
                        device_id_type=MESH,
                    )
                )
                copies[-1].start()
            return copies

        field_loads[0].wait()
        field_loads[1].wait()

        def pack_plane(z, acc):
            for i in range(C + 1):
                plane = (ve[i, z] if i < C else vo[0, z]).astype(F32)
                acc = jnp.where(lane // 2 == i * Z + z, pltpu.roll(plane, 2 * (i * Z + z) + 1, 1), acc)
                edge = plane if i < C else vo[1, z].astype(F32)
                rows_f[0, i, pl.ds(z, 1), :] = edge[0:1]
                rows_f[1, i, pl.ds(z, 1), :] = edge[yl - 1 : yl]
            return acc

        cols_out[0] = lax.fori_loop(0, Z, pack_plane, jnp.zeros((yl, LANES), F32)).astype(BF16)
        rows_out[:, 0 : C + 1] = rows_f[:, 0 : C + 1].astype(BF16)
        halo_copies = send_halo(0, C + 1)

        def build(dst, table, count, width):
            def body(a, carry):
                row = pl.ds(ROWS + a, 1)
                value = table[0, 0:ROWS, :] * table[0, row, :] - table[1, 0:ROWS, :] * table[1, row, :]
                dst[pl.ds(pl.multiple_of(a * ROWS, ROWS), ROWS), :] = value.astype(BF16)
                return carry

            lax.fori_loop(0, count, body, 0)

        loads[0].wait()
        build(fwd_y, sfy, Y // ROWS, half_y)

        def y_stage(c, carry):
            pltpu.make_async_copy(fy.at[c], fy.at[c], recv_sem.at[0, c]).wait()
            low = fy[c, 0:half_y, :].astype(F32)
            high = fy[c, half_y:Y, :].astype(F32)
            ys[c, 0:half_y, :] = jnp.dot(
                fwd_y[0:half_y, :], (low + high).astype(BF16), preferred_element_type=F32
            ).astype(BF16)
            ys[c, half_y:Y, :] = jnp.dot(
                fwd_y[half_y:Y, :], (low - high).astype(BF16), preferred_element_type=F32
            ).astype(BF16)

            def body(k, carry):
                t = lax.rem(mine + k, chunks)
                pltpu.make_async_remote_copy(
                    src_ref=ys.at[c, pl.ds(pl.multiple_of(t * pair, pair), pair)],
                    dst_ref=xr.at[c, core, gx],
                    send_sem=send_sem.at[1, c],
                    recv_sem=recv_sem.at[1, c],
                    device_id=(t // 2, base + lax.rem(t, 2)),
                    device_id_type=MESH,
                ).start()
                return carry

            lax.fori_loop(1, chunks, body, 0)
            pltpu.make_async_copy(
                ys.at[c, pl.ds(pl.multiple_of(mine * pair, pair), pair)],
                xr.at[c, core, gx],
                recv_sem.at[1, c],
            ).start()
            return carry

        lax.fori_loop(0, C, y_stage, 0)

        loads[1].wait()
        build(fwd_x, sfx, Q // ROWS, 8 * Q)
        loads[2].wait()
        build(inv_y, siy, half_y // ROWS, Y)
        loads[3].wait()
        build(inv_x, six, 4 * Q // ROWS, 2 * Q)

        depth_wave = (gy // 2).astype(F32) * (2.0 * math.pi / Z)
        chunk_half = mine // (chunks // 2)
        first_mode = 2 * lax.rem(mine, chunks // 2) * per + chunk_half
        mode = first_mode + 2 * lax.broadcasted_iota(jnp.int32, (per, Q), 0)
        wave_y = mode.astype(F32) * (2.0 * math.pi / Y)
        for r in range(4):
            kx = 4 * lax.broadcasted_iota(jnp.int32, (per, Q), 1) + r
            wave_x = jnp.where(kx < X // 2, kx, kx - X).astype(F32) * (2.0 * math.pi / X)
            square = wave_x * wave_x + wave_y * wave_y + depth_wave * depth_wave
            weight = jnp.where(square > 0, 1.0 / jnp.where(square > 0, square, 1.0), 0.0)
            weight = jnp.where(kx == X // 2, 0.0, weight)
            weight = jnp.where(mode == 0, 0.5 * weight, weight)
            weights[r, 0] = weight * wave_x
            weights[r, 1] = weight * wave_y
            weights[r, 2] = weight * depth_wave

        def x_stage(c, carry):
            pltpu.make_async_copy(xr.at[c], xr.at[c], recv_sem.at[1, c]).wait()
            for p in range(2):
                for b in range(per // ROWS):
                    for h in range(wide):
                        a = []
                        for part in range(2):
                            rows = slice(part * per + b * ROWS, part * per + (b + 1) * ROWS)
                            a.append([xr[c, p, j * wide + h, rows, :].astype(F32) for j in range(4)])
                        (r0, r1, r2, r3), (i0, i1, i2, i3) = a
                        sr, dr, tr, er = r0 + r2, r0 - r2, r1 + r3, r1 - r3
                        si, di, ti, ei = i0 + i2, i0 - i2, i1 + i3, i1 - i3
                        values = (
                            (sr + tr, si + ti),
                            (dr + ei, di - er),
                            (sr - tr, si - ti),
                            (dr - ei, di + er),
                        )
                        for r in range(4):
                            for part in range(2):
                                row = p * pair + part * per + b * ROWS
                                lx[r, row : row + ROWS, h * LANES : (h + 1) * LANES] = values[r][
                                    part
                                ].astype(BF16)
            for r in range(4):
                raw[c, r] = jnp.dot(
                    lx[r], fwd_x[:, r * 2 * Q : (r + 1) * 2 * Q], preferred_element_type=F32
                )
            return carry

        lax.fori_loop(0, C, x_stage, 0)

        def filter_block(r, carry):
            for b in range(per // ROWS):
                for h in range(wide):
                    cols = slice(h * LANES, (h + 1) * LANES)
                    sins = slice(Q + h * LANES, Q + (h + 1) * LANES)

                    def spectrum(c, p):
                        re = slice(p * pair + b * ROWS, p * pair + (b + 1) * ROWS)
                        im = slice(p * pair + per + b * ROWS, p * pair + per + (b + 1) * ROWS)
                        real = raw[c, r, re, cols] + raw[c, r, im, sins]
                        imag = raw[c, r, im, cols] - raw[c, r, re, sins]
                        return real, imag

                    wrow = slice(b * ROWS, (b + 1) * ROWS)
                    ax = weights[r, 0, wrow, cols]
                    ay = weights[r, 1, wrow, cols]
                    az = weights[r, 2, wrow, cols]
                    (rx, sx), (ry, sy), (rz, sz) = [spectrum(c, 0) for c in range(3)]
                    (ux, vx), (uy, vy), (uz, vz) = [spectrum(c, 1) for c in range(3)]
                    result = (
                        (
                            (az * uy - ay * sz, ay * rz + az * vy),
                            (ay * vz + az * ry, az * sy - ay * uz),
                        ),
                        (
                            (ax * sz - az * ux, -(ax * rz + az * vx)),
                            (-(ax * vz + az * rx), ax * uz - az * sx),
                        ),
                        (
                            (ay * sx - ax * sy, ax * ry - ay * rx),
                            (ax * vy - ay * vx, ay * ux - ax * uy),
                        ),
                    )
                    for c in range(3):
                        for p in range(2):
                            for part in range(2):
                                row = p * pair + part * per + b * ROWS
                                filt[c, r, row : row + ROWS, cols] = result[c][p][part].astype(BF16)
            return carry

        lax.fori_loop(0, 4, filter_block, 0)

        def x_back(c, carry):
            for r in range(4):
                raw[c, r] = jnp.dot(
                    filt[c, r], inv_x[r * Q : (r + 1) * Q, :], preferred_element_type=F32
                )
            for p in range(2):
                for b in range(per // ROWS):
                    for h in range(wide):
                        cols = slice(h * LANES, (h + 1) * LANES)
                        sins = slice(Q + h * LANES, Q + (h + 1) * LANES)
                        re = slice(p * pair + b * ROWS, p * pair + (b + 1) * ROWS)
                        im = slice(p * pair + per + b * ROWS, p * pair + per + (b + 1) * ROWS)
                        real = [raw[c, r, re, cols] - raw[c, r, im, sins] for r in range(4)]
                        imag = [raw[c, r, re, sins] + raw[c, r, im, cols] for r in range(4)]
                        sr, dr, tr, er = real[0] + real[2], real[0] - real[2], real[1] + real[3], real[1] - real[3]
                        si, di, ti, ei = imag[0] + imag[2], imag[0] - imag[2], imag[1] + imag[3], imag[1] - imag[3]
                        values = (
                            (sr + tr, si + ti),
                            (dr - ei, di + er),
                            (sr - tr, si - ti),
                            (dr + ei, di - er),
                        )
                        for j in range(4):
                            for part in range(2):
                                row = part * per + b * ROWS
                                xb[c, p, j * wide + h, row : row + ROWS, :] = values[j][part].astype(BF16)

            dst = pl.ds(pl.multiple_of(mine * pair, pair), pair)

            def body(k, carry):
                t = lax.rem(mine + k, chunks)
                pltpu.make_async_remote_copy(
                    src_ref=xb.at[c, lax.rem(t, 2), t // 2],
                    dst_ref=yr.at[c, dst],
                    send_sem=send_sem.at[2, c],
                    recv_sem=recv_sem.at[2, c],
                    device_id=(t // 2, base + lax.rem(t, 2)),
                    device_id_type=MESH,
                ).start()
                return carry

            lax.fori_loop(1, chunks, body, 0)
            pltpu.make_async_copy(xb.at[c, core, gx], yr.at[c, dst], recv_sem.at[2, c]).start()
            return carry

        lax.fori_loop(0, C, x_back, 0)

        def y_back(c, carry):
            pltpu.make_async_copy(yr.at[c], yr.at[c], recv_sem.at[2, c]).wait()
            even = jnp.dot(inv_y[:, 0:half_y], yr[c, 0:half_y, :], preferred_element_type=F32)
            odd = jnp.dot(inv_y[:, half_y:Y], yr[c, half_y:Y, :], preferred_element_type=F32)
            sp[c, 0:half_y, :] = (even + odd).astype(BF16)
            sp[c, half_y:Y, :] = (even - odd).astype(BF16)

            def body(k, carry):
                dst = lax.rem(gy + k, NY)
                pltpu.make_async_remote_copy(
                    src_ref=sp.at[c, pl.ds(pl.multiple_of(dst * yl, yl), yl)],
                    dst_ref=zr.at[c, gy],
                    send_sem=send_sem.at[3, c],
                    recv_sem=recv_sem.at[3, c],
                    device_id=(gx, dst),
                    device_id_type=MESH,
                ).start()
                return carry

            lax.fori_loop(1, NY, body, 0)
            pltpu.make_async_copy(
                sp.at[c, pl.ds(pl.multiple_of(gy * yl, yl), yl)], zr.at[c, gy], recv_sem.at[3, c]
            ).start()
            return carry

        lax.fori_loop(0, C, y_back, 0)

        field_loads[2].wait()
        lane_block = lax.broadcasted_iota(jnp.int32, (ROWS, LANES), 1)
        stores = []
        for c in range(C):
            pltpu.make_async_copy(zr.at[c], zr.at[c], recv_sem.at[3, c]).wait()

            def body(b, carry, c=c):
                rows = pl.ds(pl.multiple_of(b * ROWS, ROWS), ROWS)
                values = depth_inverse(
                    [zr[c, k, rows, :].astype(F32) * scale for k in range(Z)], Z
                )
                acc = cols_f[rows, :] if c else jnp.zeros((ROWS, LANES), F32)
                for z in range(Z):
                    value = adj[c, z, rows, :] + values[z]
                    adj[c, z, rows, :] = value
                    index = c * Z + z
                    acc = jnp.where(lane_block // 2 == index, pltpu.roll(value, 2 * index + 1, 1), acc)
                cols_f[rows, :] = acc
                return carry

            lax.fori_loop(0, yl // ROWS, body, 0)
            stores.append(pltpu.make_async_copy(adj.at[c], adj_h.at[c], store_sem.at[c]))
            stores[-1].start()
            for z in range(Z):
                rows_f[0, 4 + c, z : z + 1, :] = adj[c, z, 0:1, :]
                rows_f[1, 4 + c, z : z + 1, :] = adj[c, z, yl - 1 : yl, :]
        cols_out[1] = cols_f[...].astype(BF16)
        rows_out[:, 4 : 4 + C] = rows_f[:, 4 : 4 + C].astype(BF16)
        halo_copies += send_halo(1, C)

        for c in range(C):
            sent = zb.at[c, 0 : NY - 1]
            pltpu.make_async_copy(sent, sent, send_sem.at[0, c]).wait()
            sent = ys.at[c, 0 : (chunks - 1) * pair]
            pltpu.make_async_copy(sent, sent, send_sem.at[1, c]).wait()
            sent = yr.at[c, 0 : (chunks - 1) * pair]
            pltpu.make_async_copy(sent, sent, send_sem.at[2, c]).wait()
            sent = sp.at[c, 0 : (NY - 1) * yl]
            pltpu.make_async_copy(sent, sent, send_sem.at[3, c]).wait()
        for copy in halo_copies:
            copy.wait()
        halo_rows[...] = rows_in[...].astype(F32)
        for stage in range(2):
            halo_cols[stage] = jnp.where(
                lane % 2 == 0, cols_in[0, stage].astype(F32), cols_in[1, stage].astype(F32)
            )
        for copy in stores:
            copy.wait()

    def vmem(shape, dtype=BF16):
        return pltpu.VMEM(shape, dtype)

    scratch = [
        vmem((C, Z, yl, LANES), F32),
        vmem((C, Z, yl, LANES), F32),
        vmem((C, Z, yl, LANES)),
        vmem((C, Z, yl, LANES)),
        vmem((2, 7, Z, LANES), F32),
        vmem((yl, LANES), F32),
        vmem((2, 7, Z, LANES)),
        vmem((2, yl, LANES)),
        vmem((2, 7, Z, LANES)),
        vmem((2, 2, yl, LANES)),
    ]
    scratch += [vmem(s.shape, F32) for s in seeds]
    scratch += [
        vmem((Y, half_y)),
        vmem((half_y, Y)),
        vmem((Q, 8 * Q)),
        vmem((4 * Q, 2 * Q)),
        vmem((4, 3, per, Q), F32),
        vmem((C, Z, yl, LANES)),
        vmem((C, Y, LANES)),
        vmem((C, Y, LANES)),
        vmem((C, 2, NX, pair, LANES)),
        vmem((4, 2 * pair, Q)),
        vmem((C, 4, 2 * pair, 2 * Q), F32),
        vmem((C, 4, 2 * pair, Q)),
        vmem((C, 2, NX, pair, LANES)),
        vmem((C, Y, LANES)),
        vmem((C, Y, LANES)),
        vmem((C, Z, yl, LANES)),
        pltpu.SemaphoreType.DMA((C + 3,)),
        pltpu.SemaphoreType.DMA((C,)),
        pltpu.SemaphoreType.DMA((4,)),
        pltpu.SemaphoreType.DMA((4, C)),
        pltpu.SemaphoreType.DMA((4, C)),
        pltpu.SemaphoreType.DMA((2, 4)),
        pltpu.SemaphoreType.DMA((2, 4)),
    ]
    call = pl.pallas_call(
        kernel,
        out_shape=(
            jax.ShapeDtypeStruct((C, Z, yl, LANES), F32),
            jax.ShapeDtypeStruct((2, 7, Z, LANES), F32),
            jax.ShapeDtypeStruct((2, yl, LANES), F32),
        ),
        in_specs=[pl.BlockSpec(memory_space=pl.ANY)] * 8,
        out_specs=(
            pl.BlockSpec(memory_space=pl.ANY),
            pl.BlockSpec(memory_space=pltpu.VMEM),
            pl.BlockSpec(memory_space=pltpu.VMEM),
        ),
        scratch_shapes=scratch,
        compiler_params=pltpu.CompilerParams(
            collective_id=0, has_side_effects=True, vmem_limit_bytes=56 << 20
        ),
        name="spectral",
    )

    def run(cot_vel, cot_vort, velocity, vorticity):
        return call(cot_vel, cot_vort, velocity, vorticity, *[jnp.asarray(s) for s in seeds])

    return run


def stretch(adjoint, velocity, vorticity, halo_rows, halo_cols):
    C, Z, yl, _ = adjoint.shape
    quarter = 0.5 * step_size

    def kernel(adj, ve, vo, rows, cols, grad_vort, grad_vel):
        z = pl.program_id(0)
        up, down = lax.rem(z + 1, Z), lax.rem(z + Z - 1, Z)
        lane = lax.broadcasted_iota(jnp.int32, (yl, LANES), 1)
        line = lax.broadcasted_iota(jnp.int32, (yl, LANES), 0)

        def columns(stage, index):
            return pltpu.roll(cols[stage], LANES - 1 - 2 * (index * Z + z), 1)

        def slope_x(f, edge):
            return pltpu.roll(jnp.where(lane == 0, edge, f), LANES - 1, 1) - pltpu.roll(
                jnp.where(lane == LANES - 1, edge, f), 1, 1
            )

        def slope_y(f, low, high):
            return jnp.where(line == yl - 1, high, pltpu.roll(f, yl - 1, 0)) - jnp.where(
                line == 0, low, pltpu.roll(f, 1, 0)
            )

        def edges(index):
            return rows[0, index, pl.ds(z, 1), :], rows[1, index, pl.ds(z, 1), :]

        a = [adj[i, z] for i in range(3)]
        totals = [None] * 3
        for i in range(3):
            v = ve[i, z].astype(F32)
            terms = (
                slope_x(v, columns(0, i)),
                slope_y(v, *edges(i)),
                ve[i, up].astype(F32) - ve[i, down].astype(F32),
            )
            for j in range(3):
                term = a[i] * terms[j]
                totals[j] = term if totals[j] is None else totals[j] + term
        for j in range(3):
            grad_vort[j, 0] = a[j] + quarter * totals[j]

        wx, wy = vo[0, z].astype(F32), vo[1, z].astype(F32)
        wz_up, wz_down = vo[2, up].astype(F32), vo[2, down].astype(F32)
        wx_edge = columns(0, 3)
        wy_low, wy_high = edges(3)
        for i in range(3):
            low, high = edges(4 + i)
            total = slope_x(wx * a[i], wx_edge * columns(1, i))
            total = total + slope_y(wy * a[i], wy_low * low, wy_high * high)
            total = total + (wz_up * adj[i, up] - wz_down * adj[i, down])
            grad_vel[i, 0] = -quarter * total

    whole = pl.BlockSpec(memory_space=pltpu.VMEM)
    layer = pl.BlockSpec((C, 1, yl, LANES), lambda z: (0, z, 0, 0))
    shape = jax.ShapeDtypeStruct((C, Z, yl, LANES), F32)
    return pl.pallas_call(
        kernel,
        grid=(Z,),
        out_shape=(shape, shape),
        in_specs=[whole] * 5,
        out_specs=(layer, layer),
        compiler_params=pltpu.CompilerParams(vmem_limit_bytes=32 << 20),
        name="stretch",
    )(adjoint, velocity, vorticity, halo_rows, halo_cols)


def local(cot_vort, cot_vel, vorticity, velocity):
    C, Z, yl, _ = cot_vel.shape
    spectral = make_spectral(C, Z, yl, lax.axis_size("gx"), lax.axis_size("gy"))
    adjoint, halo_rows, halo_cols = spectral(cot_vel, cot_vort, velocity, vorticity)
    return stretch(adjoint, velocity, vorticity, halo_rows, halo_cols)


def solution(mesh):
    return jax.shard_map(
        local,
        mesh=mesh,
        in_specs=(
            P(None, None, "gy", "gx"),
            P(None, None, "gy", "gx"),
            P(None, None, "gy", "gx"),
            P(None, None, "gy", "gx"),
        ),
        out_specs=(P(None, None, "gy", "gx"), P(None, None, "gy", "gx")),
        check_vma=False,
    )
```

```python
import math

import jax
import jax.numpy as jnp
import numpy as np
from jax import lax
from jax.experimental import pallas as pl
from jax.experimental.pallas import tpu as pltpu
from jax.sharding import PartitionSpec as P

step_size = 0.5
F32 = jnp.float32
BF16 = jnp.bfloat16
LANES = 128
ROWS = 16
MESH = pl.DeviceIdType.MESH


def seed(alpha, beta, length):
    turns = np.concatenate([beta, alpha], 0) % length
    angles = turns * (2.0 * np.pi / length)
    return np.stack([np.cos(angles), np.sin(angles)]).astype(np.float32)


def y_modes(Y, chunks):
    half = chunks // 2
    per = (Y // 2) // chunks
    row = np.arange(Y)
    chunk, part, index = row // (2 * per), (row // per) % 2, row % per
    return 2 * ((chunk % half) * per + index) + chunk // half, part


def tables(X, Y, chunks):
    modes, part = y_modes(Y, chunks)
    quarter = Y // 4
    yy = np.arange(Y // 2)
    start = np.arange(0, Y, ROWS)
    forward_y = seed(
        modes[start][:, None] * yy + quarter * part[start][:, None],
        2 * np.arange(ROWS)[:, None] * yy,
        Y,
    )
    block = np.arange(0, Y // 2, ROWS)
    inverse_y = seed(
        block[:, None] * modes + quarter * part, np.arange(ROWS)[:, None] * modes, Y
    )
    Q = X // 4
    k = np.arange(Q)
    freq = np.concatenate([4 * k + r for r in range(4) for _ in range(2)])
    shift = np.concatenate([np.full(Q, s * (X // 4)) for _ in range(4) for s in range(2)])
    block = np.arange(0, Q, ROWS)
    forward_x = seed(block[:, None] * freq - shift, np.arange(ROWS)[:, None] * freq, X)
    xx = np.concatenate([k, k])
    shift = np.concatenate([np.zeros(Q), np.full(Q, X // 4)]).astype(np.int64)
    first = np.concatenate([4 * block + r for r in range(4)])
    inverse_x = seed(first[:, None] * xx - shift, 4 * np.arange(ROWS)[:, None] * xx, X)
    return forward_y, inverse_y, forward_x, inverse_x


def combine(terms):
    total = None
    for factor, value in terms:
        if abs(factor) < 1e-12:
            continue
        if total is None:
            total = value if factor == 1.0 else (-value if factor == -1.0 else value * factor)
        elif factor == 1.0:
            total = total + value
        elif factor == -1.0:
            total = total - value
        else:
            total = total + value * factor
    return total


def trig(kind, product, Z):
    value = (math.cos if kind == "c" else math.sin)(2.0 * math.pi * (product % Z) / Z)
    nearest = round(value)
    return float(nearest) if abs(value - nearest) < 1e-12 else value


def depth_forward(f, Z):
    H = Z // 2
    even = [f[0]] + [f[z] + f[Z - z] for z in range(1, H)] + [f[H]]
    odd = [None] + [f[z] - f[Z - z] for z in range(1, H)]
    real, imag = [None] * H, [None] * H
    for k in range(H // 2 + 1):
        a = combine([(trig("c", k * z, Z), even[z]) for z in range(0, H + 1, 2)])
        b = combine([(trig("c", k * z, Z), even[z]) for z in range(1, H + 1, 2)])
        total = a if b is None else (b if a is None else a + b)
        real[k] = total
        if 0 < k < H - k:
            real[H - k] = a if b is None else (-b if a is None else a - b)
        if k == 0:
            continue
        a = combine([(trig("s", k * z, Z), odd[z]) for z in range(2, H, 2)])
        b = combine([(trig("s", k * z, Z), odd[z]) for z in range(1, H, 2)])
        imag[k] = -(a if b is None else (b if a is None else a + b))
        if k < H - k:
            imag[H - k] = -b if a is None else (a if b is None else a - b)
    planes = []
    for k in range(H):
        planes += [real[k], jnp.zeros_like(real[0]) if k == 0 else imag[k]]
    return planes


def depth_inverse(planes, Z):
    H = Z // 2
    s = [planes[2 * k] for k in range(H)]
    d = [planes[2 * k + 1] for k in range(H)]
    even, odd = [None] * (H + 1), [None] * (H + 1)
    for z in range(H // 2 + 1):
        a = combine([((1.0 if k == 0 else 2.0 * trig("c", k * z, Z)), s[k]) for k in range(0, H, 2)])
        b = combine([(2.0 * trig("c", k * z, Z), s[k]) for k in range(1, H, 2)])
        even[z] = a if b is None else a + b
        even[H - z] = a if b is None else a - b
        if z == 0:
            continue
        a = combine([(2.0 * trig("s", k * z, Z), d[k]) for k in range(2, H, 2)])
        b = combine([(2.0 * trig("s", k * z, Z), d[k]) for k in range(1, H, 2)])
        odd[z] = a if b is None else (b if a is None else a + b)
        odd[H - z] = -a if b is None else (b if a is None else b - a)
    out = [None] * Z
    out[0], out[H] = even[0], even[H]
    for z in range(1, H):
        out[z] = even[z] + odd[z]
        out[Z - z] = even[z] - odd[z]
    return out


def make_spectral(C, Z, yl, NX, NY):
    X, Y = NX * LANES, NY * yl
    assert NY == Z
    chunks = NX * 2
    per = (Y // 2) // chunks
    pair = 2 * per
    half_y = Y // 2
    Q = X // 4
    wide = Q // LANES
    scale = 2.0 / (X * Y * Z)
    seeds = tables(X, Y, chunks)

    def kernel(
        cv_h,
        cw_h,
        ve_h,
        vo_h,
        sfy_h,
        siy_h,
        sfx_h,
        six_h,
        grad_vort_h,
        grad_vel_h,
        cv,
        adj,
        ve,
        vo,
        grad_vel,
        vel_slope,
        rows_f,
        cols_f,
        rows_out,
        cols_out,
        rows_in,
        cols_in,
        sfy,
        siy,
        sfx,
        six,
        fwd_y,
        inv_y,
        fwd_x,
        inv_x,
        weights,
        zb,
        fy,
        ys,
        xr,
        lx,
        raw,
        filt,
        xb,
        yr,
        sp,
        zr,
        load_sem,
        store_sem,
        seed_sem,
        send_sem,
        recv_sem,
        halo_send,
        halo_recv,
    ):
        gx = lax.axis_index("gx")
        gy = lax.axis_index("gy")
        core = lax.rem(gy, 2)
        base = gy - core
        mine = gx * 2 + core

        cv_loads = []
        for c in range(C):
            cv_loads.append(pltpu.make_async_copy(cv_h.at[c], cv.at[c], load_sem.at[c]))
            cv_loads[-1].start()
        field_loads = []
        for i, (src, dst) in enumerate(((ve_h, ve), (vo_h, vo), (cw_h, adj))):
            field_loads.append(pltpu.make_async_copy(src, dst, load_sem.at[C + i]))
            field_loads[-1].start()

        barrier = pltpu.get_barrier_semaphore()
        right, left = (lax.rem(gx + 1, NX), gy), (lax.rem(gx + NX - 1, NX), gy)
        after, before = (gx, lax.rem(gy + 1, NY)), (gx, lax.rem(gy + NY - 1, NY))

        def greet_y(k, carry):
            pl.semaphore_signal(
                barrier, inc=1, device_id=(gx, lax.rem(gy + k, NY)), device_id_type=MESH
            )
            return carry

        lax.fori_loop(1, NY, greet_y, 0)

        def greet_x(k, carry):
            t = lax.rem(mine + k, chunks)
            pl.semaphore_signal(
                barrier, inc=1, device_id=(t // 2, base + lax.rem(t, 2)), device_id_type=MESH
            )
            return carry

        lax.fori_loop(1, chunks, greet_x, 0)

        loads = []
        for i, (src, dst) in enumerate(((sfy_h, sfy), (sfx_h, sfx), (siy_h, siy), (six_h, six))):
            loads.append(pltpu.make_async_copy(src, dst, seed_sem.at[i]))
            loads[-1].start()

        def z_block(c, b):
            rows = pl.ds(pl.multiple_of(b * ROWS, ROWS), ROWS)
            planes = depth_forward([cv[c, z, rows, :] for z in range(Z)], Z)
            for k in range(Z):
                zb[c, k, rows, :] = planes[k].astype(BF16)

        def send_planes(c):
            row = pl.ds(pl.multiple_of(gy * yl, yl), yl)

            def body(k, carry):
                dst = lax.rem(gy + k, NY)
                pltpu.make_async_remote_copy(
                    src_ref=zb.at[c, dst],
                    dst_ref=fy.at[c, row],
                    send_sem=send_sem.at[0, c],
                    recv_sem=recv_sem.at[0, c],
                    device_id=(gx, dst),
                    device_id_type=MESH,
                ).start()
                return carry

            lax.fori_loop(1, NY, body, 0)
            pltpu.make_async_copy(zb.at[c, gy], fy.at[c, row], recv_sem.at[0, c]).start()

        for c in range(C):
            cv_loads[c].wait()
            lax.fori_loop(0, yl // ROWS, lambda b, carry, c=c: (z_block(c, b), carry)[1], 0)
            if c == 0:
                pl.semaphore_wait(barrier, NY - 1 + chunks - 1)
            send_planes(c)

        lane = lax.broadcasted_iota(jnp.int32, (yl, LANES), 1)
        line = lax.broadcasted_iota(jnp.int32, (yl, LANES), 0)
        quarter = 0.5 * step_size

        def send_halo(stage, first, count):
            copies = []
            for i, (src, dst, device) in enumerate(
                (
                    (rows_out.at[1, first : first + count], rows_in.at[0, first : first + count], after),
                    (rows_out.at[0, first : first + count], rows_in.at[1, first : first + count], before),
                    (cols_out.at[stage], cols_in.at[0, stage], right),
                    (cols_out.at[stage], cols_in.at[1, stage], left),
                )
            ):
                copies.append(
                    pltpu.make_async_remote_copy(
                        src_ref=src,
                        dst_ref=dst,
                        send_sem=halo_send.at[stage, i],
                        recv_sem=halo_recv.at[stage, i],
                        device_id=device,
                        device_id_type=MESH,
                    )
                )
                copies[-1].start()
            return copies

        def take_halo(copies, stage, first, count):
            for copy in copies:
                copy.wait()
            rows_f[:, first : first + count] = rows_in[:, first : first + count].astype(F32)
            cols_f[stage] = jnp.where(
                lane % 2 == 0, cols_in[0, stage].astype(F32), cols_in[1, stage].astype(F32)
            )

        def columns(stage, index):
            return pltpu.roll(cols_f[stage], LANES - 1 - 2 * index, 1)

        def edges(index, z):
            return rows_f[0, index, pl.ds(z, 1), :], rows_f[1, index, pl.ds(z, 1), :]

        def slope_x(f, edge):
            return pltpu.roll(jnp.where(lane == 0, edge, f), LANES - 1, 1) - pltpu.roll(
                jnp.where(lane == LANES - 1, edge, f), 1, 1
            )

        def slope_y(f, low, high):
            return jnp.where(line == yl - 1, high, pltpu.roll(f, yl - 1, 0)) - jnp.where(
                line == 0, low, pltpu.roll(f, 1, 0)
            )

        field_loads[0].wait()
        field_loads[1].wait()

        def pack_plane(z, acc):
            for i in range(C + 1):
                plane = (ve[i, z] if i < C else vo[0, z]).astype(F32)
                acc = jnp.where(lane // 2 == i * Z + z, pltpu.roll(plane, 2 * (i * Z + z) + 1, 1), acc)
                edge = plane if i < C else vo[1, z].astype(F32)
                rows_f[0, i, pl.ds(z, 1), :] = edge[0:1]
                rows_f[1, i, pl.ds(z, 1), :] = edge[yl - 1 : yl]
            return acc

        cols_out[0] = lax.fori_loop(0, Z, pack_plane, jnp.zeros((yl, LANES), F32)).astype(BF16)
        rows_out[:, 0 : C + 1] = rows_f[:, 0 : C + 1].astype(BF16)
        field_halo = send_halo(0, 0, C + 1)

        def build(dst, table, count, width):
            def body(a, carry):
                row = pl.ds(ROWS + a, 1)
                value = table[0, 0:ROWS, :] * table[0, row, :] - table[1, 0:ROWS, :] * table[1, row, :]
                dst[pl.ds(pl.multiple_of(a * ROWS, ROWS), ROWS), :] = value.astype(BF16)
                return carry

            lax.fori_loop(0, count, body, 0)

        loads[0].wait()
        build(fwd_y, sfy, Y // ROWS, half_y)

        def y_stage(c, carry):
            pltpu.make_async_copy(fy.at[c], fy.at[c], recv_sem.at[0, c]).wait()
            low = fy[c, 0:half_y, :].astype(F32)
            high = fy[c, half_y:Y, :].astype(F32)
            ys[c, 0:half_y, :] = jnp.dot(
                fwd_y[0:half_y, :], (low + high).astype(BF16), preferred_element_type=F32
            ).astype(BF16)
            ys[c, half_y:Y, :] = jnp.dot(
                fwd_y[half_y:Y, :], (low - high).astype(BF16), preferred_element_type=F32
            ).astype(BF16)

            def body(k, carry):
                t = lax.rem(mine + k, chunks)
                pltpu.make_async_remote_copy(
                    src_ref=ys.at[c, pl.ds(pl.multiple_of(t * pair, pair), pair)],
                    dst_ref=xr.at[c, core, gx],
                    send_sem=send_sem.at[1, c],
                    recv_sem=recv_sem.at[1, c],
                    device_id=(t // 2, base + lax.rem(t, 2)),
                    device_id_type=MESH,
                ).start()
                return carry

            lax.fori_loop(1, chunks, body, 0)
            pltpu.make_async_copy(
                ys.at[c, pl.ds(pl.multiple_of(mine * pair, pair), pair)],
                xr.at[c, core, gx],
                recv_sem.at[1, c],
            ).start()
            return carry

        lax.fori_loop(0, C, y_stage, 0)

        loads[1].wait()
        build(fwd_x, sfx, Q // ROWS, 8 * Q)
        loads[2].wait()
        build(inv_y, siy, half_y // ROWS, Y)
        loads[3].wait()
        build(inv_x, six, 4 * Q // ROWS, 2 * Q)

        depth_wave = (gy // 2).astype(F32) * (2.0 * math.pi / Z)
        chunk_half = mine // (chunks // 2)
        first_mode = 2 * lax.rem(mine, chunks // 2) * per + chunk_half
        mode = first_mode + 2 * lax.broadcasted_iota(jnp.int32, (per, Q), 0)
        wave_y = mode.astype(F32) * (2.0 * math.pi / Y)
        for r in range(4):
            kx = 4 * lax.broadcasted_iota(jnp.int32, (per, Q), 1) + r
            wave_x = jnp.where(kx < X // 2, kx, kx - X).astype(F32) * (2.0 * math.pi / X)
            square = wave_x * wave_x + wave_y * wave_y + depth_wave * depth_wave
            weight = jnp.where(square > 0, 1.0 / jnp.where(square > 0, square, 1.0), 0.0)
            weight = jnp.where(kx == X // 2, 0.0, weight)
            weight = jnp.where(mode == 0, 0.5 * weight, weight)
            weights[r, 0] = weight * wave_x
            weights[r, 1] = weight * wave_y
            weights[r, 2] = weight * depth_wave

        def x_stage(c, carry):
            pltpu.make_async_copy(xr.at[c], xr.at[c], recv_sem.at[1, c]).wait()
            for p in range(2):
                for b in range(per // ROWS):
                    for h in range(wide):
                        a = []
                        for part in range(2):
                            rows = slice(part * per + b * ROWS, part * per + (b + 1) * ROWS)
                            a.append([xr[c, p, j * wide + h, rows, :].astype(F32) for j in range(4)])
                        (r0, r1, r2, r3), (i0, i1, i2, i3) = a
                        sr, dr, tr, er = r0 + r2, r0 - r2, r1 + r3, r1 - r3
                        si, di, ti, ei = i0 + i2, i0 - i2, i1 + i3, i1 - i3
                        values = (
                            (sr + tr, si + ti),
                            (dr + ei, di - er),
                            (sr - tr, si - ti),
                            (dr - ei, di + er),
                        )
                        for r in range(4):
                            for part in range(2):
                                row = p * pair + part * per + b * ROWS
                                lx[r, row : row + ROWS, h * LANES : (h + 1) * LANES] = values[r][
                                    part
                                ].astype(BF16)
            for r in range(4):
                raw[c, r] = jnp.dot(
                    lx[r], fwd_x[:, r * 2 * Q : (r + 1) * 2 * Q], preferred_element_type=F32
                )
            return carry

        lax.fori_loop(0, C, x_stage, 0)

        def filter_block(r, carry):
            for b in range(per // ROWS):
                for h in range(wide):
                    cols = slice(h * LANES, (h + 1) * LANES)
                    sins = slice(Q + h * LANES, Q + (h + 1) * LANES)

                    def spectrum(c, p):
                        re = slice(p * pair + b * ROWS, p * pair + (b + 1) * ROWS)
                        im = slice(p * pair + per + b * ROWS, p * pair + per + (b + 1) * ROWS)
                        real = raw[c, r, re, cols] + raw[c, r, im, sins]
                        imag = raw[c, r, im, cols] - raw[c, r, re, sins]
                        return real, imag

                    wrow = slice(b * ROWS, (b + 1) * ROWS)
                    ax = weights[r, 0, wrow, cols]
                    ay = weights[r, 1, wrow, cols]
                    az = weights[r, 2, wrow, cols]
                    (rx, sx), (ry, sy), (rz, sz) = [spectrum(c, 0) for c in range(3)]
                    (ux, vx), (uy, vy), (uz, vz) = [spectrum(c, 1) for c in range(3)]
                    result = (
                        (
                            (az * uy - ay * sz, ay * rz + az * vy),
                            (ay * vz + az * ry, az * sy - ay * uz),
                        ),
                        (
                            (ax * sz - az * ux, -(ax * rz + az * vx)),
                            (-(ax * vz + az * rx), ax * uz - az * sx),
                        ),
                        (
                            (ay * sx - ax * sy, ax * ry - ay * rx),
                            (ax * vy - ay * vx, ay * ux - ax * uy),
                        ),
                    )
                    for c in range(3):
                        for p in range(2):
                            for part in range(2):
                                row = p * pair + part * per + b * ROWS
                                filt[c, r, row : row + ROWS, cols] = result[c][p][part].astype(BF16)
            return carry

        lax.fori_loop(0, 4, filter_block, 0)

        def x_back(c, carry):
            for r in range(4):
                raw[c, r] = jnp.dot(
                    filt[c, r], inv_x[r * Q : (r + 1) * Q, :], preferred_element_type=F32
                )
            for p in range(2):
                for b in range(per // ROWS):
                    for h in range(wide):
                        cols = slice(h * LANES, (h + 1) * LANES)
                        sins = slice(Q + h * LANES, Q + (h + 1) * LANES)
                        re = slice(p * pair + b * ROWS, p * pair + (b + 1) * ROWS)
                        im = slice(p * pair + per + b * ROWS, p * pair + per + (b + 1) * ROWS)
                        real = [raw[c, r, re, cols] - raw[c, r, im, sins] for r in range(4)]
                        imag = [raw[c, r, re, sins] + raw[c, r, im, cols] for r in range(4)]
                        sr, dr, tr, er = real[0] + real[2], real[0] - real[2], real[1] + real[3], real[1] - real[3]
                        si, di, ti, ei = imag[0] + imag[2], imag[0] - imag[2], imag[1] + imag[3], imag[1] - imag[3]
                        values = (
                            (sr + tr, si + ti),
                            (dr - ei, di + er),
                            (sr - tr, si - ti),
                            (dr + ei, di - er),
                        )
                        for j in range(4):
                            for part in range(2):
                                row = part * per + b * ROWS
                                xb[c, p, j * wide + h, row : row + ROWS, :] = values[j][part].astype(BF16)

            dst = pl.ds(pl.multiple_of(mine * pair, pair), pair)

            def body(k, carry):
                t = lax.rem(mine + k, chunks)
                pltpu.make_async_remote_copy(
                    src_ref=xb.at[c, lax.rem(t, 2), t // 2],
                    dst_ref=yr.at[c, dst],
                    send_sem=send_sem.at[2, c],
                    recv_sem=recv_sem.at[2, c],
                    device_id=(t // 2, base + lax.rem(t, 2)),
                    device_id_type=MESH,
                ).start()
                return carry

            lax.fori_loop(1, chunks, body, 0)
            pltpu.make_async_copy(xb.at[c, core, gx], yr.at[c, dst], recv_sem.at[2, c]).start()
            return carry

        lax.fori_loop(0, C, x_back, 0)

        take_halo(field_halo, 0, 0, C + 1)

        def velocity_slopes(z, carry):
            up, down = lax.rem(z + 1, Z), lax.rem(z + Z - 1, Z)
            for i in range(C):
                v = ve[i, z].astype(F32)
                vel_slope[0, i, z] = quarter * slope_x(v, columns(0, i * Z + z))
                vel_slope[1, i, z] = quarter * slope_y(v, *edges(i, z))
                vel_slope[2, i, z] = quarter * (ve[i, up].astype(F32) - ve[i, down].astype(F32))
            return carry

        lax.fori_loop(0, Z, velocity_slopes, 0)

        def y_back(c, carry):
            pltpu.make_async_copy(yr.at[c], yr.at[c], recv_sem.at[2, c]).wait()
            even = jnp.dot(inv_y[:, 0:half_y], yr[c, 0:half_y, :], preferred_element_type=F32)
            odd = jnp.dot(inv_y[:, half_y:Y], yr[c, half_y:Y, :], preferred_element_type=F32)
            sp[c, 0:half_y, :] = (even + odd).astype(BF16)
            sp[c, half_y:Y, :] = (even - odd).astype(BF16)

            def body(k, carry):
                dst = lax.rem(gy + k, NY)
                pltpu.make_async_remote_copy(
                    src_ref=sp.at[c, pl.ds(pl.multiple_of(dst * yl, yl), yl)],
                    dst_ref=zr.at[c, gy],
                    send_sem=send_sem.at[3, c],
                    recv_sem=recv_sem.at[3, c],
                    device_id=(gx, dst),
                    device_id_type=MESH,
                ).start()
                return carry

            lax.fori_loop(1, NY, body, 0)
            pltpu.make_async_copy(
                sp.at[c, pl.ds(pl.multiple_of(gy * yl, yl), yl)], zr.at[c, gy], recv_sem.at[3, c]
            ).start()
            return carry

        lax.fori_loop(0, C, y_back, 0)

        field_loads[2].wait()
        lane_block = lax.broadcasted_iota(jnp.int32, (ROWS, LANES), 1)
        grad_vort = cv
        stores = []
        for c in range(C):
            pltpu.make_async_copy(zr.at[c], zr.at[c], recv_sem.at[3, c]).wait()

            def z_back(b, carry, c=c):
                rows = pl.ds(pl.multiple_of(b * ROWS, ROWS), ROWS)
                values = depth_inverse(
                    [zr[c, k, rows, :].astype(F32) * scale for k in range(Z)], Z
                )
                acc = jnp.zeros((ROWS, LANES), F32)
                for z in range(Z):
                    value = adj[c, z, rows, :] + values[z]
                    adj[c, z, rows, :] = value
                    acc = jnp.where(lane_block // 2 == z, pltpu.roll(value, 2 * z + 1, 1), acc)
                cols_out[1 + c, rows, :] = acc.astype(BF16)
                return carry

            lax.fori_loop(0, yl // ROWS, z_back, 0)
            for z in range(Z):
                rows_f[0, 4 + c, z : z + 1, :] = adj[c, z, 0:1, :]
                rows_f[1, 4 + c, z : z + 1, :] = adj[c, z, yl - 1 : yl, :]
            rows_out[:, 4 + c] = rows_f[:, 4 + c].astype(BF16)
            halo = send_halo(1 + c, 4 + c, 1)

            def vort_part(z, carry, c=c):
                a = adj[c, z]
                for j in range(3):
                    term = a * vel_slope[j, c, z]
                    if j == c:
                        term = term + a
                    grad_vort[j, z] = term if c == 0 else grad_vort[j, z] + term
                return carry

            lax.fori_loop(0, Z, vort_part, 0)
            if c == C - 1:
                stores.append(pltpu.make_async_copy(grad_vort, grad_vort_h, store_sem.at[C]))
                stores[-1].start()

            take_halo(halo, 1 + c, 4 + c, 1)

            def vel_part(z, carry, c=c):
                up, down = lax.rem(z + 1, Z), lax.rem(z + Z - 1, Z)
                a = adj[c, z]
                low, high = edges(4 + c, z)
                wy_low, wy_high = edges(C, z)
                total = slope_x(vo[0, z].astype(F32) * a, columns(0, C * Z + z) * columns(1 + c, z))
                total = total + slope_y(vo[1, z].astype(F32) * a, wy_low * low, wy_high * high)
                total = total + (
                    vo[2, up].astype(F32) * adj[c, up] - vo[2, down].astype(F32) * adj[c, down]
                )
                grad_vel[c, z] = -quarter * total
                return carry

            lax.fori_loop(0, Z, vel_part, 0)
            stores.append(pltpu.make_async_copy(grad_vel.at[c], grad_vel_h.at[c], store_sem.at[c]))
            stores[-1].start()

        for c in range(C):
            sent = zb.at[c, 0 : NY - 1]
            pltpu.make_async_copy(sent, sent, send_sem.at[0, c]).wait()
            sent = ys.at[c, 0 : (chunks - 1) * pair]
            pltpu.make_async_copy(sent, sent, send_sem.at[1, c]).wait()
            sent = yr.at[c, 0 : (chunks - 1) * pair]
            pltpu.make_async_copy(sent, sent, send_sem.at[2, c]).wait()
            sent = sp.at[c, 0 : (NY - 1) * yl]
            pltpu.make_async_copy(sent, sent, send_sem.at[3, c]).wait()
        for copy in stores:
            copy.wait()

    def vmem(shape, dtype=BF16):
        return pltpu.VMEM(shape, dtype)

    scratch = [
        vmem((C, Z, yl, LANES), F32),
        vmem((C, Z, yl, LANES), F32),
        vmem((C, Z, yl, LANES)),
        vmem((C, Z, yl, LANES)),
        vmem((C, Z, yl, LANES), F32),
        vmem((3, C, Z, yl, LANES), F32),
        vmem((2, 7, Z, LANES), F32),
        vmem((1 + C, yl, LANES), F32),
        vmem((2, 7, Z, LANES)),
        vmem((1 + C, yl, LANES)),
        vmem((2, 7, Z, LANES)),
        vmem((2, 1 + C, yl, LANES)),
    ]
    scratch += [vmem(s.shape, F32) for s in seeds]
    scratch += [
        vmem((Y, half_y)),
        vmem((half_y, Y)),
        vmem((Q, 8 * Q)),
        vmem((4 * Q, 2 * Q)),
        vmem((4, 3, per, Q), F32),
        vmem((C, Z, yl, LANES)),
        vmem((C, Y, LANES)),
        vmem((C, Y, LANES)),
        vmem((C, 2, NX, pair, LANES)),
        vmem((4, 2 * pair, Q)),
        vmem((C, 4, 2 * pair, 2 * Q), F32),
        vmem((C, 4, 2 * pair, Q)),
        vmem((C, 2, NX, pair, LANES)),
        vmem((C, Y, LANES)),
        vmem((C, Y, LANES)),
        vmem((C, Z, yl, LANES)),
        pltpu.SemaphoreType.DMA((C + 3,)),
        pltpu.SemaphoreType.DMA((C + 1,)),
        pltpu.SemaphoreType.DMA((4,)),
        pltpu.SemaphoreType.DMA((4, C)),
        pltpu.SemaphoreType.DMA((4, C)),
        pltpu.SemaphoreType.DMA((1 + C, 4)),
        pltpu.SemaphoreType.DMA((1 + C, 4)),
    ]
    call = pl.pallas_call(
        kernel,
        out_shape=(
            jax.ShapeDtypeStruct((C, Z, yl, LANES), F32),
            jax.ShapeDtypeStruct((C, Z, yl, LANES), F32),
        ),
        in_specs=[pl.BlockSpec(memory_space=pl.ANY)] * 8,
        out_specs=(pl.BlockSpec(memory_space=pl.ANY), pl.BlockSpec(memory_space=pl.ANY)),
        scratch_shapes=scratch,
        compiler_params=pltpu.CompilerParams(
            collective_id=0, has_side_effects=True, vmem_limit_bytes=56 << 20
        ),
        name="spectral",
    )

    def run(cot_vel, cot_vort, velocity, vorticity):
        return call(cot_vel, cot_vort, velocity, vorticity, *[jnp.asarray(s) for s in seeds])

    return run


def local(cot_vort, cot_vel, vorticity, velocity):
    C, Z, yl, _ = cot_vel.shape
    spectral = make_spectral(C, Z, yl, lax.axis_size("gx"), lax.axis_size("gy"))
    return spectral(cot_vel, cot_vort, velocity, vorticity)


def solution(mesh):
    return jax.shard_map(
        local,
        mesh=mesh,
        in_specs=(
            P(None, None, "gy", "gx"),
            P(None, None, "gy", "gx"),
            P(None, None, "gy", "gx"),
            P(None, None, "gy", "gx"),
        ),
        out_specs=(P(None, None, "gy", "gx"), P(None, None, "gy", "gx")),
        check_vma=False,
    )
```

```python
import math

import jax
import jax.numpy as jnp
import numpy as np
from jax import lax
from jax.experimental import pallas as pl
from jax.experimental.pallas import tpu as pltpu
from jax.sharding import PartitionSpec as P

step_size = 0.5
F32 = jnp.float32
BF16 = jnp.bfloat16
LANES = 128
ROWS = 16
MESH = pl.DeviceIdType.MESH
EMPTY = 1


def seed(alpha, beta, length):
    turns = np.concatenate([beta, alpha], 0) % length
    angles = turns * (2.0 * np.pi / length)
    return np.stack([np.cos(angles), np.sin(angles)]).astype(np.float32)


def y_modes(Y, chunks):
    half = chunks // 2
    per = (Y // 2) // chunks
    row = np.arange(Y)
    chunk, part, index = row // (2 * per), (row // per) % 2, row % per
    return 2 * ((chunk % half) * per + index) + chunk // half, part


def tables(X, Y, chunks):
    modes, part = y_modes(Y, chunks)
    quarter = Y // 4
    yy = np.arange(Y // 2)
    start = np.arange(0, Y, ROWS)
    forward_y = seed(
        modes[start][:, None] * yy + quarter * part[start][:, None],
        2 * np.arange(ROWS)[:, None] * yy,
        Y,
    )
    block = np.arange(0, Y // 2, ROWS)
    inverse_y = seed(
        block[:, None] * modes + quarter * part, np.arange(ROWS)[:, None] * modes, Y
    )
    Q = X // 4
    k = np.arange(Q)
    freq = np.concatenate([4 * k + r for r in range(4) for _ in range(2)])
    shift = np.concatenate([np.full(Q, s * (X // 4)) for _ in range(4) for s in range(2)])
    block = np.arange(0, Q, ROWS)
    forward_x = seed(block[:, None] * freq - shift, np.arange(ROWS)[:, None] * freq, X)
    xx = np.concatenate([k, k])
    shift = np.concatenate([np.zeros(Q), np.full(Q, X // 4)]).astype(np.int64)
    first = np.concatenate([4 * block + r for r in range(4)])
    inverse_x = seed(first[:, None] * xx - shift, 4 * np.arange(ROWS)[:, None] * xx, X)
    return forward_y, inverse_y, forward_x, inverse_x


def combine(terms):
    total = None
    for factor, value in terms:
        if abs(factor) < 1e-12:
            continue
        if total is None:
            total = value if factor == 1.0 else (-value if factor == -1.0 else value * factor)
        elif factor == 1.0:
            total = total + value
        elif factor == -1.0:
            total = total - value
        else:
            total = total + value * factor
    return total


def trig(kind, product, Z):
    value = (math.cos if kind == "c" else math.sin)(2.0 * math.pi * (product % Z) / Z)
    nearest = round(value)
    return float(nearest) if abs(value - nearest) < 1e-12 else value


def depth_forward(f, Z):
    H = Z // 2
    even = [f[0]] + [f[z] + f[Z - z] for z in range(1, H)] + [f[H]]
    odd = [None] + [f[z] - f[Z - z] for z in range(1, H)]
    real, imag = [None] * H, [None] * H
    for k in range(H // 2 + 1):
        a = combine([(trig("c", k * z, Z), even[z]) for z in range(0, H + 1, 2)])
        b = combine([(trig("c", k * z, Z), even[z]) for z in range(1, H + 1, 2)])
        total = a if b is None else (b if a is None else a + b)
        real[k] = total
        if 0 < k < H - k:
            real[H - k] = a if b is None else (-b if a is None else a - b)
        if k == 0:
            continue
        a = combine([(trig("s", k * z, Z), odd[z]) for z in range(2, H, 2)])
        b = combine([(trig("s", k * z, Z), odd[z]) for z in range(1, H, 2)])
        imag[k] = -(a if b is None else (b if a is None else a + b))
        if k < H - k:
            imag[H - k] = -b if a is None else (a if b is None else a - b)
    planes = []
    for k in range(H):
        planes += [real[k], jnp.zeros_like(real[0]) if k == 0 else imag[k]]
    return planes


def depth_inverse(planes, Z):
    H = Z // 2
    s = [planes[2 * k] for k in range(H)]
    d = [planes[2 * k + 1] for k in range(H)]
    even, odd = [None] * (H + 1), [None] * (H + 1)
    for z in range(H // 2 + 1):
        a = combine([((1.0 if k == 0 else 2.0 * trig("c", k * z, Z)), s[k]) for k in range(0, H, 2)])
        b = combine([(2.0 * trig("c", k * z, Z), s[k]) for k in range(1, H, 2)])
        even[z] = a if b is None else a + b
        even[H - z] = a if b is None else a - b
        if z == 0:
            continue
        a = combine([(2.0 * trig("s", k * z, Z), d[k]) for k in range(2, H, 2)])
        b = combine([(2.0 * trig("s", k * z, Z), d[k]) for k in range(1, H, 2)])
        odd[z] = a if b is None else (b if a is None else a + b)
        odd[H - z] = -a if b is None else (b if a is None else b - a)
    out = [None] * Z
    out[0], out[H] = even[0], even[H]
    for z in range(1, H):
        out[z] = even[z] + odd[z]
        out[Z - z] = even[z] - odd[z]
    return out


def make_spectral(C, Z, yl, NX, NY):
    X, Y = NX * LANES, NY * yl
    assert NY == Z
    chunks = NX * 2
    per = (Y // 2) // chunks
    pair = 2 * per
    half_y = Y // 2
    Q = X // 4
    wide = Q // LANES
    scale = 2.0 / (X * Y * Z)
    seeds = tables(X, Y, chunks)
    group = 4

    def kernel(
        cv_h,
        cw_h,
        ve_h,
        vo_h,
        sfy_h,
        siy_h,
        sfx_h,
        six_h,
        grad_vort_h,
        grad_vel_h,
        cv,
        adj,
        ve,
        vo,
        gv_out,
        gl_out,
        vel_slope,
        shift,
        px,
        yp,
        edge_rows,
        edge_cols,
        rows_f,
        cols_f,
        rows_out,
        cols_out,
        rows_in,
        cols_in,
        sfy,
        siy,
        sfx,
        six,
        fwd_y,
        inv_y,
        fwd_x,
        inv_x,
        weights,
        zb,
        fy,
        ys,
        xr,
        lx,
        raw,
        back,
        filt,
        xb,
        yr,
        sp,
        zr,
        load_sem,
        store_sem,
        seed_sem,
        send_sem,
        recv_sem,
        halo_send,
        halo_recv,
    ):
        gx = lax.axis_index("gx")
        gy = lax.axis_index("gy")
        core = lax.rem(gy, 2)
        base = gy - core
        mine = gx * 2 + core

        cv_loads = []
        for c in range(C):
            cv_loads.append(pltpu.make_async_copy(cv_h.at[c], cv.at[c], load_sem.at[c]))
            cv_loads[-1].start()
        field_loads = []
        for i, (src, dst) in enumerate(((ve_h, ve), (vo_h, vo), (cw_h, adj))):
            field_loads.append(pltpu.make_async_copy(src, dst, load_sem.at[C + i]))
            field_loads[-1].start()

        barrier = pltpu.get_barrier_semaphore()
        right, left = (lax.rem(gx + 1, NX), gy), (lax.rem(gx + NX - 1, NX), gy)
        after, before = (gx, lax.rem(gy + 1, NY)), (gx, lax.rem(gy + NY - 1, NY))

        def greet_y(k, carry):
            pl.semaphore_signal(
                barrier, inc=1, device_id=(gx, lax.rem(gy + k, NY)), device_id_type=MESH
            )
            return carry

        lax.fori_loop(1, NY, greet_y, 0)

        def greet_x(k, carry):
            t = lax.rem(mine + k, chunks)
            pl.semaphore_signal(
                barrier, inc=1, device_id=(t // 2, base + lax.rem(t, 2)), device_id_type=MESH
            )
            return carry

        lax.fori_loop(1, chunks, greet_x, 0)

        loads = []
        for i, (src, dst) in enumerate(((sfy_h, sfy), (sfx_h, sfx), (siy_h, siy), (six_h, six))):
            loads.append(pltpu.make_async_copy(src, dst, seed_sem.at[i]))
            loads[-1].start()

        def z_block(c, b):
            rows = pl.ds(pl.multiple_of(b * ROWS, ROWS), ROWS)
            planes = depth_forward([cv[c, z, rows, :] for z in range(Z)], Z)
            for k in range(Z):
                if k != EMPTY:
                    zb[c, k, rows, :] = planes[k].astype(BF16)

        def send_planes(c):
            row = pl.ds(pl.multiple_of(gy * yl, yl), yl)

            def body(k, carry):
                dst = lax.rem(gy + k, NY)

                @pl.when(dst != EMPTY)
                def _():
                    pltpu.make_async_remote_copy(
                        src_ref=zb.at[c, dst],
                        dst_ref=fy.at[c, row],
                        send_sem=send_sem.at[0, c],
                        recv_sem=recv_sem.at[0, c],
                        device_id=(gx, dst),
                        device_id_type=MESH,
                    ).start()

                return carry

            lax.fori_loop(1, NY, body, 0)

            @pl.when(gy != EMPTY)
            def _():
                pltpu.make_async_copy(zb.at[c, gy], fy.at[c, row], recv_sem.at[0, c]).start()

            @pl.when(gy == EMPTY)
            def _():
                fy[c] = jnp.zeros((Y, LANES), BF16)

        for c in (1, 2, 0):
            cv_loads[c].wait()
            lax.fori_loop(0, yl // ROWS, lambda b, carry, c=c: (z_block(c, b), carry)[1], 0)
            if c == 1:
                pl.semaphore_wait(barrier, NY - 1 + chunks - 1)
            send_planes(c)

        lane = lax.broadcasted_iota(jnp.int32, (yl, LANES), 1)
        line = lax.broadcasted_iota(jnp.int32, (yl, LANES), 0)
        quarter = 0.5 * step_size

        def send_halo(stage, first, count):
            copies = []
            for i, (src, dst, device) in enumerate(
                (
                    (rows_out.at[1, first : first + count], rows_in.at[0, first : first + count], after),
                    (rows_out.at[0, first : first + count], rows_in.at[1, first : first + count], before),
                    (cols_out.at[stage], cols_in.at[0, stage], right),
                    (cols_out.at[stage], cols_in.at[1, stage], left),
                )
            ):
                copies.append(
                    pltpu.make_async_remote_copy(
                        src_ref=src,
                        dst_ref=dst,
                        send_sem=halo_send.at[stage, i],
                        recv_sem=halo_recv.at[stage, i],
                        device_id=device,
                        device_id_type=MESH,
                    )
                )
                copies[-1].start()
            return copies

        def take_halo(copies, stage, first, count, factor):
            for copy in copies:
                copy.wait()
            rows_f[:, first : first + count] = rows_in[:, first : first + count].astype(F32)
            from_left = pltpu.roll(cols_in[0, stage].astype(F32), 2, 1)
            from_right = cols_in[1, stage].astype(F32)
            if factor is not None:
                from_left, from_right = -factor * from_left, factor * from_right
            cols_f[stage] = jnp.where(lane % 2 == 0, from_right, from_left)

        def at_edges(cols, index):
            moved = pltpu.roll(cols, LANES - 1 - 2 * index, 1)
            return jnp.where((lane == 0) | (lane == LANES - 1), moved, 0.0)

        def slope_y(slot, f, low, high):
            yp[slot, 8 : 8 + yl, :] = f
            yp[slot, 7:8, :] = low
            yp[slot, 8 + yl : 9 + yl, :] = high
            return yp[slot, 9 : 9 + yl, :] - yp[slot, 7 : 7 + yl, :]

        row_index = lax.broadcasted_iota(jnp.int32, (LANES, LANES), 0)
        col_index = lax.broadcasted_iota(jnp.int32, (LANES, LANES), 1)
        shift[...] = jnp.where(
            row_index == col_index + 1, quarter, jnp.where(row_index == col_index - 1, -quarter, 0.0)
        ).astype(BF16)

        field_loads[0].wait()
        field_loads[1].wait()

        slots = lax.rem(lane + 1, LANES) // 2

        def pack_plane(z, acc):
            for i in range(C + 1):
                plane = (ve[i, z] if i < C else vo[0, z]).astype(F32)
                acc = jnp.where(slots == i * Z + z, pltpu.roll(plane, 2 * (i * Z + z), 1), acc)
                edge = plane if i < C else vo[1, z].astype(F32)
                rows_f[0, i, pl.ds(z, 1), :] = edge[0:1]
                rows_f[1, i, pl.ds(z, 1), :] = edge[yl - 1 : yl]
            return acc

        cols_out[0] = lax.fori_loop(0, Z, pack_plane, jnp.zeros((yl, LANES), F32)).astype(BF16)
        rows_out[:, 0 : C + 1] = rows_f[:, 0 : C + 1].astype(BF16)
        field_halo = send_halo(0, 0, C + 1)

        def build(dst, table, count, width):
            def body(a, carry):
                row = pl.ds(ROWS + a, 1)
                value = table[0, 0:ROWS, :] * table[0, row, :] - table[1, 0:ROWS, :] * table[1, row, :]
                dst[pl.ds(pl.multiple_of(a * ROWS, ROWS), ROWS), :] = value.astype(BF16)
                return carry

            lax.fori_loop(0, count, body, 0)

        loads[0].wait()
        build(fwd_y, sfy, Y // ROWS, half_y)

        def y_stage(i, carry):
            c = lax.rem(i + 1, C)

            @pl.when(gy != EMPTY)
            def _():
                pltpu.make_async_copy(fy.at[c], fy.at[c], recv_sem.at[0, c]).wait()

            low = fy[c, 0:half_y, :].astype(F32)
            high = fy[c, half_y:Y, :].astype(F32)
            ys[c, 0:half_y, :] = jnp.dot(
                fwd_y[0:half_y, :], (low + high).astype(BF16), preferred_element_type=F32
            ).astype(BF16)
            ys[c, half_y:Y, :] = jnp.dot(
                fwd_y[half_y:Y, :], (low - high).astype(BF16), preferred_element_type=F32
            ).astype(BF16)

            def body(k, carry):
                t = lax.rem(mine + k, chunks)
                pltpu.make_async_remote_copy(
                    src_ref=ys.at[c, pl.ds(pl.multiple_of(t * pair, pair), pair)],
                    dst_ref=xr.at[c, core, gx],
                    send_sem=send_sem.at[1, c],
                    recv_sem=recv_sem.at[1, c],
                    device_id=(t // 2, base + lax.rem(t, 2)),
                    device_id_type=MESH,
                ).start()
                return carry

            lax.fori_loop(1, chunks, body, 0)
            pltpu.make_async_copy(
                ys.at[c, pl.ds(pl.multiple_of(mine * pair, pair), pair)],
                xr.at[c, core, gx],
                recv_sem.at[1, c],
            ).start()
            return carry

        lax.fori_loop(0, C, y_stage, 0)

        loads[1].wait()
        build(fwd_x, sfx, Q // ROWS, 8 * Q)
        loads[2].wait()
        build(inv_y, siy, half_y // ROWS, Y)
        loads[3].wait()
        build(inv_x, six, 4 * Q // ROWS, 2 * Q)

        depth_wave = (gy // 2).astype(F32) * (2.0 * math.pi / Z)
        chunk_half = mine // (chunks // 2)
        first_mode = 2 * lax.rem(mine, chunks // 2) * per + chunk_half
        mode = first_mode + 2 * lax.broadcasted_iota(jnp.int32, (per, Q), 0)
        wave_y = mode.astype(F32) * (2.0 * math.pi / Y)
        for r in range(4):
            kx = 4 * lax.broadcasted_iota(jnp.int32, (per, Q), 1) + r
            wave_x = jnp.where(kx < X // 2, kx, kx - X).astype(F32) * (2.0 * math.pi / X)
            square = wave_x * wave_x + wave_y * wave_y + depth_wave * depth_wave
            weight = jnp.where(square > 0, 1.0 / jnp.where(square > 0, square, 1.0), 0.0)
            weight = jnp.where(kx == X // 2, 0.0, weight)
            weight = jnp.where(mode == 0, 0.5 * weight, weight)
            weights[r, 0] = weight * wave_x
            weights[r, 1] = weight * wave_y
            weights[r, 2] = weight * depth_wave

        take_halo(field_halo, 0, 0, C + 1, quarter)
        edge_cols[...] = pltpu.roll(cols_f[0], LANES - 2 * C * Z, 1)

        def velocity_slopes(i, carry):
            flat = ve[i].reshape(Z * yl, LANES)
            vel_slope[0, i] = jnp.dot(flat, shift[...], preferred_element_type=F32).reshape(Z, yl, LANES)

            def layer(b, carry):
                for n in range(group):
                    z = b * group + n
                    up, down = lax.rem(z + 1, Z), lax.rem(z + Z - 1, Z)
                    vel_slope[0, i, z] = vel_slope[0, i, z] + at_edges(cols_f[0], i * Z + z)
                    vel_slope[1, i, z] = quarter * slope_y(
                        n, ve[i, z].astype(F32), rows_f[0, i, pl.ds(z, 1), :], rows_f[1, i, pl.ds(z, 1), :]
                    )
                    vel_slope[2, i, z] = quarter * (ve[i, up].astype(F32) - ve[i, down].astype(F32))
                return carry

            return lax.fori_loop(0, Z // group, layer, carry)

        lax.fori_loop(0, C, velocity_slopes, 0)

        def x_stage(c, carry):
            pltpu.make_async_copy(xr.at[c], xr.at[c], recv_sem.at[1, c]).wait()
            for p in range(2):
                for b in range(per // ROWS):
                    for h in range(wide):
                        a = []
                        for part in range(2):
                            rows = slice(part * per + b * ROWS, part * per + (b + 1) * ROWS)
                            a.append([xr[c, p, j * wide + h, rows, :].astype(F32) for j in range(4)])
                        (r0, r1, r2, r3), (i0, i1, i2, i3) = a
                        sr, dr, tr, er = r0 + r2, r0 - r2, r1 + r3, r1 - r3
                        si, di, ti, ei = i0 + i2, i0 - i2, i1 + i3, i1 - i3
                        values = (
                            (sr + tr, si + ti),
                            (dr + ei, di - er),
                            (sr - tr, si - ti),
                            (dr - ei, di + er),
                        )
                        for r in range(4):
                            for part in range(2):
                                row = p * pair + part * per + b * ROWS
                                lx[r, row : row + ROWS, h * LANES : (h + 1) * LANES] = values[r][
                                    part
                                ].astype(BF16)
            for r in range(4):
                raw[c, r] = jnp.dot(
                    lx[r], fwd_x[:, r * 2 * Q : (r + 1) * 2 * Q], preferred_element_type=F32
                )
            return carry

        lax.fori_loop(1, C, x_stage, 0)

        def filter_block(r, first):
            for b in range(per // ROWS):
                for h in range(wide):
                    cols = slice(h * LANES, (h + 1) * LANES)
                    sins = slice(Q + h * LANES, Q + (h + 1) * LANES)

                    def spectrum(c, p):
                        re = slice(p * pair + b * ROWS, p * pair + (b + 1) * ROWS)
                        im = slice(p * pair + per + b * ROWS, p * pair + per + (b + 1) * ROWS)
                        real = raw[c, r, re, cols] + raw[c, r, im, sins]
                        imag = raw[c, r, im, cols] - raw[c, r, re, sins]
                        return real, imag

                    wrow = slice(b * ROWS, (b + 1) * ROWS)
                    ax = weights[r, 0, wrow, cols]
                    ay = weights[r, 1, wrow, cols]
                    az = weights[r, 2, wrow, cols]
                    (ry, sy), (rz, sz) = [spectrum(c, 0) for c in (1, 2)]
                    (uy, vy), (uz, vz) = [spectrum(c, 1) for c in (1, 2)]
                    if first:
                        result = {
                            0: (
                                (az * uy - ay * sz, ay * rz + az * vy),
                                (ay * vz + az * ry, az * sy - ay * uz),
                            )
                        }
                    else:
                        (rx, sx), (ux, vx) = spectrum(0, 0), spectrum(0, 1)
                        result = {
                            1: (
                                (ax * sz - az * ux, -(ax * rz + az * vx)),
                                (-(ax * vz + az * rx), ax * uz - az * sx),
                            ),
                            2: (
                                (ay * sx - ax * sy, ax * ry - ay * rx),
                                (ax * vy - ay * vx, ay * ux - ax * uy),
                            ),
                        }
                    for c in result:
                        for p in range(2):
                            for part in range(2):
                                row = p * pair + part * per + b * ROWS
                                filt[c, r, row : row + ROWS, cols] = result[c][p][part].astype(BF16)

        def filter_all(first):
            def body(r, carry):
                filter_block(r, first)
                return carry

            lax.fori_loop(0, 4, body, 0)

        def x_back(c, carry):
            for r in range(4):
                back[r] = jnp.dot(
                    filt[c, r], inv_x[r * Q : (r + 1) * Q, :], preferred_element_type=F32
                )
            for p in range(2):
                for b in range(per // ROWS):
                    for h in range(wide):
                        cols = slice(h * LANES, (h + 1) * LANES)
                        sins = slice(Q + h * LANES, Q + (h + 1) * LANES)
                        re = slice(p * pair + b * ROWS, p * pair + (b + 1) * ROWS)
                        im = slice(p * pair + per + b * ROWS, p * pair + per + (b + 1) * ROWS)
                        real = [back[r, re, cols] - back[r, im, sins] for r in range(4)]
                        imag = [back[r, re, sins] + back[r, im, cols] for r in range(4)]
                        sr, dr, tr, er = real[0] + real[2], real[0] - real[2], real[1] + real[3], real[1] - real[3]
                        si, di, ti, ei = imag[0] + imag[2], imag[0] - imag[2], imag[1] + imag[3], imag[1] - imag[3]
                        values = (
                            (sr + tr, si + ti),
                            (dr - ei, di + er),
                            (sr - tr, si - ti),
                            (dr + ei, di - er),
                        )
                        for j in range(4):
                            for part in range(2):
                                row = part * per + b * ROWS
                                xb[c, p, j * wide + h, row : row + ROWS, :] = values[j][part].astype(BF16)

            dst = pl.ds(pl.multiple_of(mine * pair, pair), pair)

            def body(k, carry):
                t = lax.rem(mine + k, chunks)
                pltpu.make_async_remote_copy(
                    src_ref=xb.at[c, lax.rem(t, 2), t // 2],
                    dst_ref=yr.at[c, dst],
                    send_sem=send_sem.at[2, c],
                    recv_sem=recv_sem.at[2, c],
                    device_id=(t // 2, base + lax.rem(t, 2)),
                    device_id_type=MESH,
                ).start()
                return carry

            lax.fori_loop(1, chunks, body, 0)
            pltpu.make_async_copy(xb.at[c, core, gx], yr.at[c, dst], recv_sem.at[2, c]).start()
            return carry

        filter_all(True)
        lax.fori_loop(0, 1, x_back, 0)
        lax.fori_loop(0, 1, x_stage, 0)
        filter_all(False)
        lax.fori_loop(1, C, x_back, 0)

        def y_back(c, carry):
            pltpu.make_async_copy(yr.at[c], yr.at[c], recv_sem.at[2, c]).wait()
            even = jnp.dot(inv_y[:, 0:half_y], yr[c, 0:half_y, :], preferred_element_type=F32)
            odd = jnp.dot(inv_y[:, half_y:Y], yr[c, half_y:Y, :], preferred_element_type=F32)
            sp[c, 0:half_y, :] = (even + odd).astype(BF16)
            sp[c, half_y:Y, :] = (even - odd).astype(BF16)

            @pl.when(gy != EMPTY)
            def _():
                def body(k, carry):
                    dst = lax.rem(gy + k, NY)
                    pltpu.make_async_remote_copy(
                        src_ref=sp.at[c, pl.ds(pl.multiple_of(dst * yl, yl), yl)],
                        dst_ref=zr.at[c, gy],
                        send_sem=send_sem.at[3, c],
                        recv_sem=recv_sem.at[3, c],
                        device_id=(gx, dst),
                        device_id_type=MESH,
                    ).start()
                    return carry

                lax.fori_loop(1, NY, body, 0)
                pltpu.make_async_copy(
                    sp.at[c, pl.ds(pl.multiple_of(gy * yl, yl), yl)], zr.at[c, gy], recv_sem.at[3, c]
                ).start()

            return carry

        lax.fori_loop(0, C, y_back, 0)

        field_loads[2].wait()
        slots_block = slots[0:ROWS]
        grad_vort = cv
        stores = []
        halos = []

        def finish_velocity(c):
            take_halo(halos[c], 1 + c, 4 + c, 1, None)
            cols_f[1 + c] = cols_f[1 + c] * edge_cols[...]
            edge_rows[...] = rows_f[:, C] * rows_f[:, 4 + c]

            def vel_part(b, carry):
                for n in range(group):
                    z = b * group + n
                    px[n * yl : (n + 1) * yl, :] = (vo[0, z].astype(F32) * adj[c, z]).astype(BF16)
                slopes = jnp.dot(px[...], shift[...], preferred_element_type=F32)
                for n in range(group):
                    z = b * group + n
                    up, down = lax.rem(z + 1, Z), lax.rem(z + Z - 1, Z)
                    rest = slope_y(
                        n,
                        vo[1, z].astype(F32) * adj[c, z],
                        edge_rows[0, pl.ds(z, 1), :],
                        edge_rows[1, pl.ds(z, 1), :],
                    )
                    rest = rest + (
                        vo[2, up].astype(F32) * adj[c, up] - vo[2, down].astype(F32) * adj[c, down]
                    )
                    total = slopes[n * yl : (n + 1) * yl] + at_edges(cols_f[1 + c], z)
                    gl_out[c, z] = (-total - quarter * rest).astype(BF16)
                return carry

            lax.fori_loop(0, Z // group, vel_part, 0)
            stores.append(pltpu.make_async_copy(gl_out.at[c], grad_vel_h.at[c], store_sem.at[c]))
            stores[-1].start()

        for c in range(C):
            come = zr.at[c, 0 : Z - 1]
            pltpu.make_async_copy(come, come, recv_sem.at[3, c]).wait()

            def z_back(b, carry, c=c):
                rows = pl.ds(pl.multiple_of(b * ROWS, ROWS), ROWS)
                values = depth_inverse(
                    [None if k == EMPTY else zr[c, k, rows, :].astype(F32) * scale for k in range(Z)],
                    Z,
                )
                acc = jnp.zeros((ROWS, LANES), F32)
                for z in range(Z):
                    value = adj[c, z, rows, :] + values[z]
                    adj[c, z, rows, :] = value
                    acc = jnp.where(slots_block == z, pltpu.roll(value, 2 * z, 1) if z else value, acc)
                cols_out[1 + c, rows, :] = acc.astype(BF16)
                return carry

            lax.fori_loop(0, yl // ROWS, z_back, 0)
            for z in range(Z):
                rows_f[0, 4 + c, z : z + 1, :] = adj[c, z, 0:1, :]
                rows_f[1, 4 + c, z : z + 1, :] = adj[c, z, yl - 1 : yl, :]
            rows_out[:, 4 + c] = rows_f[:, 4 + c].astype(BF16)
            halos.append(send_halo(1 + c, 4 + c, 1))

            def vort_part(z, carry, c=c):
                a = adj[c, z]
                for j in range(3):
                    term = a * vel_slope[j, c, z]
                    if j == c:
                        term = term + a
                    if c:
                        term = grad_vort[j, z] + term
                    if c == C - 1:
                        gv_out[j, z] = term.astype(BF16)
                    else:
                        grad_vort[j, z] = term
                return carry

            lax.fori_loop(0, Z, vort_part, 0)
            if c:
                finish_velocity(c - 1)
        stores.append(pltpu.make_async_copy(gv_out, grad_vort_h, store_sem.at[C]))
        stores[-1].start()
        finish_velocity(C - 1)

        for c in range(C):
            sent = zb.at[c, 0 : NY - 2]
            pltpu.make_async_copy(sent, sent, send_sem.at[0, c]).wait()

            @pl.when(gy == EMPTY)
            def _():
                more = zb.at[c, 0]
                pltpu.make_async_copy(more, more, send_sem.at[0, c]).wait()

            sent = ys.at[c, 0 : (chunks - 1) * pair]
            pltpu.make_async_copy(sent, sent, send_sem.at[1, c]).wait()
            sent = yr.at[c, 0 : (chunks - 1) * pair]
            pltpu.make_async_copy(sent, sent, send_sem.at[2, c]).wait()

            @pl.when(gy != EMPTY)
            def _():
                last = sp.at[c, 0 : (NY - 1) * yl]
                pltpu.make_async_copy(last, last, send_sem.at[3, c]).wait()

        for copy in stores:
            copy.wait()

    def vmem(shape, dtype=BF16):
        return pltpu.VMEM(shape, dtype)

    scratch = [
        vmem((C, Z, yl, LANES), F32),
        vmem((C, Z, yl, LANES), F32),
        vmem((C, Z, yl, LANES)),
        vmem((C, Z, yl, LANES)),
        vmem((C, Z, yl, LANES)),
        vmem((C, Z, yl, LANES)),
        vmem((3, C, Z, yl, LANES), F32),
        vmem((LANES, LANES)),
        vmem((group * yl, LANES)),
        vmem((group, yl + 16, LANES), F32),
        vmem((2, Z, LANES), F32),
        vmem((yl, LANES), F32),
        vmem((2, 7, Z, LANES), F32),
        vmem((1 + C, yl, LANES), F32),
        vmem((2, 7, Z, LANES)),
        vmem((1 + C, yl, LANES)),
        vmem((2, 7, Z, LANES)),
        vmem((2, 1 + C, yl, LANES)),
    ]
    scratch += [vmem(s.shape, F32) for s in seeds]
    scratch += [
        vmem((Y, half_y)),
        vmem((half_y, Y)),
        vmem((Q, 8 * Q)),
        vmem((4 * Q, 2 * Q)),
        vmem((4, 3, per, Q), F32),
        vmem((C, Z, yl, LANES)),
        vmem((C, Y, LANES)),
        vmem((C, Y, LANES)),
        vmem((C, 2, NX, pair, LANES)),
        vmem((4, 2 * pair, Q)),
        vmem((C, 4, 2 * pair, 2 * Q), F32),
        vmem((4, 2 * pair, 2 * Q), F32),
        vmem((C, 4, 2 * pair, Q)),
        vmem((C, 2, NX, pair, LANES)),
        vmem((C, Y, LANES)),
        vmem((C, Y, LANES)),
        vmem((C, Z, yl, LANES)),
        pltpu.SemaphoreType.DMA((C + 3,)),
        pltpu.SemaphoreType.DMA((C + 1,)),
        pltpu.SemaphoreType.DMA((4,)),
        pltpu.SemaphoreType.DMA((4, C)),
        pltpu.SemaphoreType.DMA((4, C)),
        pltpu.SemaphoreType.DMA((1 + C, 4)),
        pltpu.SemaphoreType.DMA((1 + C, 4)),
    ]
    call = pl.pallas_call(
        kernel,
        out_shape=(
            jax.ShapeDtypeStruct((C, Z, yl, LANES), BF16),
            jax.ShapeDtypeStruct((C, Z, yl, LANES), BF16),
        ),
        in_specs=[pl.BlockSpec(memory_space=pltpu.HBM)] * 8,
        out_specs=(pl.BlockSpec(memory_space=pl.ANY), pl.BlockSpec(memory_space=pl.ANY)),
        scratch_shapes=scratch,
        compiler_params=pltpu.CompilerParams(
            collective_id=0, has_side_effects=True, vmem_limit_bytes=56 << 20
        ),
        name="spectral",
    )

    def run(cot_vel, cot_vort, velocity, vorticity):
        return call(cot_vel, cot_vort, velocity, vorticity, *[jnp.asarray(s) for s in seeds])

    return run


def widen(grad_vort, grad_vel):
    C, Z, yl, _ = grad_vort.shape

    def kernel(a_h, b_h, wide_a_h, wide_b_h, a, b, wide_a, wide_b, load_sem, store_sem):
        pieces = []
        for c in range(C):
            for i, refs in enumerate(((a_h, a, wide_a, wide_a_h), (b_h, b, wide_b, wide_b_h))):
                load = pltpu.make_async_copy(refs[0].at[c], refs[1].at[c], load_sem.at[i, c])
                load.start()
                pieces.append((c, i, refs, load))
        stores = []
        for c, i, (_, narrow, wide, out), load in pieces:
            load.wait()

            def body(z, carry):
                wide[c, z] = narrow[c, z].astype(F32)
                return carry

            lax.fori_loop(0, Z, body, 0)
            stores.append(pltpu.make_async_copy(wide.at[c], out.at[c], store_sem.at[i, c]))
            stores[-1].start()
        for store in stores:
            store.wait()

    hbm = pl.BlockSpec(memory_space=pltpu.HBM)
    shape = jax.ShapeDtypeStruct((C, Z, yl, LANES), F32)
    narrow = pltpu.VMEM((C, Z, yl, LANES), BF16)
    wide = pltpu.VMEM((C, Z, yl, LANES), F32)
    return pl.pallas_call(
        kernel,
        out_shape=(shape, shape),
        in_specs=[hbm, hbm],
        out_specs=(hbm, hbm),
        scratch_shapes=[narrow, narrow, wide, wide]
        + [pltpu.SemaphoreType.DMA((2, C)), pltpu.SemaphoreType.DMA((2, C))],
        compiler_params=pltpu.CompilerParams(vmem_limit_bytes=60 << 20),
        name="widen",
    )(grad_vort, grad_vel)


def local(cot_vort, cot_vel, vorticity, velocity):
    C, Z, yl, _ = cot_vel.shape
    spectral = make_spectral(C, Z, yl, lax.axis_size("gx"), lax.axis_size("gy"))
    return widen(*spectral(cot_vel, cot_vort, velocity, vorticity))


def solution(mesh):
    return jax.shard_map(
        local,
        mesh=mesh,
        in_specs=(
            P(None, None, "gy", "gx"),
            P(None, None, "gy", "gx"),
            P(None, None, "gy", "gx"),
            P(None, None, "gy", "gx"),
        ),
        out_specs=(P(None, None, "gy", "gx"), P(None, None, "gy", "gx")),
        check_vma=False,
    )
```

```python
import math

import jax
import jax.numpy as jnp
import numpy as np
from jax import lax
from jax.experimental import pallas as pl
from jax.experimental.pallas import tpu as pltpu
from jax.sharding import PartitionSpec as P

step_size = 0.5
F32 = jnp.float32
BF16 = jnp.bfloat16
LANES = 128
ROWS = 16
MESH = pl.DeviceIdType.MESH
EMPTY = 1


def seed(alpha, beta, length):
    turns = np.concatenate([beta, alpha], 0) % length
    angles = turns * (2.0 * np.pi / length)
    return np.stack([np.cos(angles), np.sin(angles)]).astype(np.float32)


def y_modes(Y, chunks):
    half = chunks // 2
    per = (Y // 2) // chunks
    row = np.arange(Y)
    chunk, part, index = row // (2 * per), (row // per) % 2, row % per
    return 2 * ((chunk % half) * per + index) + chunk // half, part


def tables(X, Y, chunks):
    modes, part = y_modes(Y, chunks)
    quarter = Y // 4
    yy = np.arange(Y // 2)
    start = np.arange(0, Y, ROWS)
    forward_y = seed(
        modes[start][:, None] * yy + quarter * part[start][:, None],
        2 * np.arange(ROWS)[:, None] * yy,
        Y,
    )
    block = np.arange(0, Y // 2, ROWS)
    inverse_y = seed(
        block[:, None] * modes + quarter * part, np.arange(ROWS)[:, None] * modes, Y
    )
    Q = X // 4
    k = np.arange(Q)
    freq = np.concatenate([4 * k + r for r in range(4) for _ in range(2)])
    shift = np.concatenate([np.full(Q, s * (X // 4)) for _ in range(4) for s in range(2)])
    block = np.arange(0, Q, ROWS)
    forward_x = seed(block[:, None] * freq - shift, np.arange(ROWS)[:, None] * freq, X)
    xx = np.concatenate([k, k])
    shift = np.concatenate([np.zeros(Q), np.full(Q, X // 4)]).astype(np.int64)
    first = np.concatenate([4 * block + r for r in range(4)])
    inverse_x = seed(first[:, None] * xx - shift, 4 * np.arange(ROWS)[:, None] * xx, X)
    return forward_y, inverse_y, forward_x, inverse_x


def combine(terms):
    total = None
    for factor, value in terms:
        if abs(factor) < 1e-12:
            continue
        if total is None:
            total = value if factor == 1.0 else (-value if factor == -1.0 else value * factor)
        elif factor == 1.0:
            total = total + value
        elif factor == -1.0:
            total = total - value
        else:
            total = total + value * factor
    return total


def trig(kind, product, Z):
    value = (math.cos if kind == "c" else math.sin)(2.0 * math.pi * (product % Z) / Z)
    nearest = round(value)
    return float(nearest) if abs(value - nearest) < 1e-12 else value


def depth_forward(f, Z):
    H = Z // 2
    even = [f[0]] + [f[z] + f[Z - z] for z in range(1, H)] + [f[H]]
    odd = [None] + [f[z] - f[Z - z] for z in range(1, H)]
    real, imag = [None] * H, [None] * H
    for k in range(H // 2 + 1):
        a = combine([(trig("c", k * z, Z), even[z]) for z in range(0, H + 1, 2)])
        b = combine([(trig("c", k * z, Z), even[z]) for z in range(1, H + 1, 2)])
        total = a if b is None else (b if a is None else a + b)
        real[k] = total
        if 0 < k < H - k:
            real[H - k] = a if b is None else (-b if a is None else a - b)
        if k == 0:
            continue
        a = combine([(trig("s", k * z, Z), odd[z]) for z in range(2, H, 2)])
        b = combine([(trig("s", k * z, Z), odd[z]) for z in range(1, H, 2)])
        imag[k] = -(a if b is None else (b if a is None else a + b))
        if k < H - k:
            imag[H - k] = -b if a is None else (a if b is None else a - b)
    planes = []
    for k in range(H):
        planes += [real[k], jnp.zeros_like(real[0]) if k == 0 else imag[k]]
    return planes


def depth_inverse(planes, Z):
    H = Z // 2
    s = [planes[2 * k] for k in range(H)]
    d = [planes[2 * k + 1] for k in range(H)]
    even, odd = [None] * (H + 1), [None] * (H + 1)
    for z in range(H // 2 + 1):
        a = combine([((1.0 if k == 0 else 2.0 * trig("c", k * z, Z)), s[k]) for k in range(0, H, 2)])
        b = combine([(2.0 * trig("c", k * z, Z), s[k]) for k in range(1, H, 2)])
        even[z] = a if b is None else a + b
        even[H - z] = a if b is None else a - b
        if z == 0:
            continue
        a = combine([(2.0 * trig("s", k * z, Z), d[k]) for k in range(2, H, 2)])
        b = combine([(2.0 * trig("s", k * z, Z), d[k]) for k in range(1, H, 2)])
        odd[z] = a if b is None else (b if a is None else a + b)
        odd[H - z] = -a if b is None else (b if a is None else b - a)
    out = [None] * Z
    out[0], out[H] = even[0], even[H]
    for z in range(1, H):
        out[z] = even[z] + odd[z]
        out[Z - z] = even[z] - odd[z]
    return out


def make_spectral(C, Z, yl, NX, NY):
    X, Y = NX * LANES, NY * yl
    assert NY == Z
    chunks = NX * 2
    per = (Y // 2) // chunks
    pair = 2 * per
    half_y = Y // 2
    Q = X // 4
    wide = Q // LANES
    scale = 2.0 / (X * Y * Z)
    seeds = tables(X, Y, chunks)
    group = 4

    def kernel(
        cv_h,
        cw_h,
        ve_h,
        vo_h,
        sfy_h,
        siy_h,
        sfx_h,
        six_h,
        gv_out,
        gl_out,
        cv,
        adj,
        ve,
        vo,
        vel_slope,
        shift,
        px,
        yp,
        edge_rows,
        edge_cols,
        rows_f,
        cols_f,
        rows_out,
        cols_out,
        rows_in,
        cols_in,
        sfy,
        siy,
        sfx,
        six,
        fwd_y,
        inv_y,
        fwd_x,
        inv_x,
        weights,
        zb,
        fy,
        ys,
        xr,
        lx,
        raw,
        back,
        filt,
        xb,
        yr,
        sp,
        zr,
        load_sem,
        seed_sem,
        send_sem,
        recv_sem,
        halo_send,
        halo_recv,
    ):
        gx = lax.axis_index("gx")
        gy = lax.axis_index("gy")
        core = lax.rem(gy, 2)
        base = gy - core
        mine = gx * 2 + core

        cv_loads = []
        for c in range(C):
            cv_loads.append(pltpu.make_async_copy(cv_h.at[c], cv.at[c], load_sem.at[c]))
            cv_loads[-1].start()
        field_loads = []
        for i, (src, dst) in enumerate(((ve_h, ve), (vo_h, vo), (cw_h, adj))):
            field_loads.append(pltpu.make_async_copy(src, dst, load_sem.at[C + i]))
            field_loads[-1].start()

        barrier = pltpu.get_barrier_semaphore()
        right, left = (lax.rem(gx + 1, NX), gy), (lax.rem(gx + NX - 1, NX), gy)
        after, before = (gx, lax.rem(gy + 1, NY)), (gx, lax.rem(gy + NY - 1, NY))

        def greet_y(k, carry):
            pl.semaphore_signal(
                barrier, inc=1, device_id=(gx, lax.rem(gy + k, NY)), device_id_type=MESH
            )
            return carry

        lax.fori_loop(1, NY, greet_y, 0)

        def greet_x(k, carry):
            t = lax.rem(mine + k, chunks)
            pl.semaphore_signal(
                barrier, inc=1, device_id=(t // 2, base + lax.rem(t, 2)), device_id_type=MESH
            )
            return carry

        lax.fori_loop(1, chunks, greet_x, 0)

        loads = []
        for i, (src, dst) in enumerate(((sfy_h, sfy), (sfx_h, sfx), (siy_h, siy), (six_h, six))):
            loads.append(pltpu.make_async_copy(src, dst, seed_sem.at[i]))
            loads[-1].start()

        def z_block(c, b):
            rows = pl.ds(pl.multiple_of(b * ROWS, ROWS), ROWS)
            planes = depth_forward([cv[c, z, rows, :] for z in range(Z)], Z)
            for k in range(Z):
                if k != EMPTY:
                    zb[c, k, rows, :] = planes[k].astype(BF16)

        def send_planes(c):
            row = pl.ds(pl.multiple_of(gy * yl, yl), yl)

            def body(k, carry):
                dst = lax.rem(gy + k, NY)

                @pl.when(dst != EMPTY)
                def _():
                    pltpu.make_async_remote_copy(
                        src_ref=zb.at[c, dst],
                        dst_ref=fy.at[c, row],
                        send_sem=send_sem.at[0, c],
                        recv_sem=recv_sem.at[0, c],
                        device_id=(gx, dst),
                        device_id_type=MESH,
                    ).start()

                return carry

            lax.fori_loop(1, NY, body, 0)

            @pl.when(gy != EMPTY)
            def _():
                pltpu.make_async_copy(zb.at[c, gy], fy.at[c, row], recv_sem.at[0, c]).start()

            @pl.when(gy == EMPTY)
            def _():
                fy[c] = jnp.zeros((Y, LANES), BF16)

        for c in (1, 2, 0):
            cv_loads[c].wait()
            lax.fori_loop(0, yl // ROWS, lambda b, carry, c=c: (z_block(c, b), carry)[1], 0)
            if c == 1:
                pl.semaphore_wait(barrier, NY - 1 + chunks - 1)
            send_planes(c)

        lane = lax.broadcasted_iota(jnp.int32, (yl, LANES), 1)
        line = lax.broadcasted_iota(jnp.int32, (yl, LANES), 0)
        quarter = 0.5 * step_size

        def send_halo(stage, first, count):
            copies = []
            for i, (src, dst, device) in enumerate(
                (
                    (rows_out.at[1, first : first + count], rows_in.at[0, first : first + count], after),
                    (rows_out.at[0, first : first + count], rows_in.at[1, first : first + count], before),
                    (cols_out.at[stage], cols_in.at[0, stage], right),
                    (cols_out.at[stage], cols_in.at[1, stage], left),
                )
            ):
                copies.append(
                    pltpu.make_async_remote_copy(
                        src_ref=src,
                        dst_ref=dst,
                        send_sem=halo_send.at[stage, i],
                        recv_sem=halo_recv.at[stage, i],
                        device_id=device,
                        device_id_type=MESH,
                    )
                )
                copies[-1].start()
            return copies

        def take_halo(copies, stage, first, count, factor):
            for copy in copies:
                copy.wait()
            rows_f[:, first : first + count] = rows_in[:, first : first + count].astype(F32)
            from_left = pltpu.roll(cols_in[0, stage].astype(F32), 2, 1)
            from_right = cols_in[1, stage].astype(F32)
            if factor is not None:
                from_left, from_right = -factor * from_left, factor * from_right
            cols_f[stage] = jnp.where(lane % 2 == 0, from_right, from_left)

        def at_edges(cols, index):
            moved = pltpu.roll(cols, LANES - 1 - 2 * index, 1)
            return jnp.where((lane == 0) | (lane == LANES - 1), moved, 0.0)

        def slope_y(slot, f, low, high):
            yp[slot, 8 : 8 + yl, :] = f
            yp[slot, 7:8, :] = low
            yp[slot, 8 + yl : 9 + yl, :] = high
            return yp[slot, 9 : 9 + yl, :] - yp[slot, 7 : 7 + yl, :]

        row_index = lax.broadcasted_iota(jnp.int32, (LANES, LANES), 0)
        col_index = lax.broadcasted_iota(jnp.int32, (LANES, LANES), 1)
        shift[...] = jnp.where(
            row_index == col_index + 1, quarter, jnp.where(row_index == col_index - 1, -quarter, 0.0)
        ).astype(BF16)

        field_loads[0].wait()
        field_loads[1].wait()

        slots = lax.rem(lane + 1, LANES) // 2

        def pack_plane(z, acc):
            for i in range(C + 1):
                plane = (ve[i, z] if i < C else vo[0, z]).astype(F32)
                acc = jnp.where(slots == i * Z + z, pltpu.roll(plane, 2 * (i * Z + z), 1), acc)
                edge = plane if i < C else vo[1, z].astype(F32)
                rows_f[0, i, pl.ds(z, 1), :] = edge[0:1]
                rows_f[1, i, pl.ds(z, 1), :] = edge[yl - 1 : yl]
            return acc

        cols_out[0] = lax.fori_loop(0, Z, pack_plane, jnp.zeros((yl, LANES), F32)).astype(BF16)
        rows_out[:, 0 : C + 1] = rows_f[:, 0 : C + 1].astype(BF16)
        field_halo = send_halo(0, 0, C + 1)

        def build(dst, table, count, width):
            def body(a, carry):
                row = pl.ds(ROWS + a, 1)
                value = table[0, 0:ROWS, :] * table[0, row, :] - table[1, 0:ROWS, :] * table[1, row, :]
                dst[pl.ds(pl.multiple_of(a * ROWS, ROWS), ROWS), :] = value.astype(BF16)
                return carry

            lax.fori_loop(0, count, body, 0)

        loads[0].wait()
        build(fwd_y, sfy, Y // ROWS, half_y)

        def y_stage(i, carry):
            c = lax.rem(i + 1, C)

            @pl.when(gy != EMPTY)
            def _():
                pltpu.make_async_copy(fy.at[c], fy.at[c], recv_sem.at[0, c]).wait()

            low = fy[c, 0:half_y, :].astype(F32)
            high = fy[c, half_y:Y, :].astype(F32)
            ys[c, 0:half_y, :] = jnp.dot(
                fwd_y[0:half_y, :], (low + high).astype(BF16), preferred_element_type=F32
            ).astype(BF16)
            ys[c, half_y:Y, :] = jnp.dot(
                fwd_y[half_y:Y, :], (low - high).astype(BF16), preferred_element_type=F32
            ).astype(BF16)

            def body(k, carry):
                t = lax.rem(mine + k, chunks)
                pltpu.make_async_remote_copy(
                    src_ref=ys.at[c, pl.ds(pl.multiple_of(t * pair, pair), pair)],
                    dst_ref=xr.at[c, core, gx],
                    send_sem=send_sem.at[1, c],
                    recv_sem=recv_sem.at[1, c],
                    device_id=(t // 2, base + lax.rem(t, 2)),
                    device_id_type=MESH,
                ).start()
                return carry

            lax.fori_loop(1, chunks, body, 0)
            pltpu.make_async_copy(
                ys.at[c, pl.ds(pl.multiple_of(mine * pair, pair), pair)],
                xr.at[c, core, gx],
                recv_sem.at[1, c],
            ).start()
            return carry

        lax.fori_loop(0, C, y_stage, 0)

        loads[1].wait()
        build(fwd_x, sfx, Q // ROWS, 8 * Q)
        loads[2].wait()
        build(inv_y, siy, half_y // ROWS, Y)
        loads[3].wait()
        build(inv_x, six, 4 * Q // ROWS, 2 * Q)

        depth_wave = (gy // 2).astype(F32) * (2.0 * math.pi / Z)
        chunk_half = mine // (chunks // 2)
        first_mode = 2 * lax.rem(mine, chunks // 2) * per + chunk_half
        mode = first_mode + 2 * lax.broadcasted_iota(jnp.int32, (per, Q), 0)
        wave_y = mode.astype(F32) * (2.0 * math.pi / Y)
        for r in range(4):
            kx = 4 * lax.broadcasted_iota(jnp.int32, (per, Q), 1) + r
            wave_x = jnp.where(kx < X // 2, kx, kx - X).astype(F32) * (2.0 * math.pi / X)
            square = wave_x * wave_x + wave_y * wave_y + depth_wave * depth_wave
            weight = jnp.where(square > 0, 1.0 / jnp.where(square > 0, square, 1.0), 0.0)
            weight = jnp.where(kx == X // 2, 0.0, weight)
            weight = jnp.where(mode == 0, 0.5 * weight, weight)
            weights[r, 0] = weight * wave_x
            weights[r, 1] = weight * wave_y
            weights[r, 2] = weight * depth_wave

        take_halo(field_halo, 0, 0, C + 1, quarter)
        edge_cols[...] = pltpu.roll(cols_f[0], LANES - 2 * C * Z, 1)

        def velocity_slopes(i, carry):
            flat = ve[i].reshape(Z * yl, LANES)
            vel_slope[0, i] = jnp.dot(flat, shift[...], preferred_element_type=F32).reshape(Z, yl, LANES)

            def layer(b, carry):
                for n in range(group):
                    z = b * group + n
                    up, down = lax.rem(z + 1, Z), lax.rem(z + Z - 1, Z)
                    vel_slope[0, i, z] = vel_slope[0, i, z] + at_edges(cols_f[0], i * Z + z)
                    vel_slope[1, i, z] = quarter * slope_y(
                        n, ve[i, z].astype(F32), rows_f[0, i, pl.ds(z, 1), :], rows_f[1, i, pl.ds(z, 1), :]
                    )
                    vel_slope[2, i, z] = quarter * (ve[i, up].astype(F32) - ve[i, down].astype(F32))
                return carry

            return lax.fori_loop(0, Z // group, layer, carry)

        lax.fori_loop(0, C, velocity_slopes, 0)

        def x_stage(c, carry):
            pltpu.make_async_copy(xr.at[c], xr.at[c], recv_sem.at[1, c]).wait()
            for p in range(2):
                for b in range(per // ROWS):
                    for h in range(wide):
                        a = []
                        for part in range(2):
                            rows = slice(part * per + b * ROWS, part * per + (b + 1) * ROWS)
                            a.append([xr[c, p, j * wide + h, rows, :].astype(F32) for j in range(4)])
                        (r0, r1, r2, r3), (i0, i1, i2, i3) = a
                        sr, dr, tr, er = r0 + r2, r0 - r2, r1 + r3, r1 - r3
                        si, di, ti, ei = i0 + i2, i0 - i2, i1 + i3, i1 - i3
                        values = (
                            (sr + tr, si + ti),
                            (dr + ei, di - er),
                            (sr - tr, si - ti),
                            (dr - ei, di + er),
                        )
                        for r in range(4):
                            for part in range(2):
                                row = p * pair + part * per + b * ROWS
                                lx[r, row : row + ROWS, h * LANES : (h + 1) * LANES] = values[r][
                                    part
                                ].astype(BF16)
            for r in range(4):
                raw[c, r] = jnp.dot(
                    lx[r], fwd_x[:, r * 2 * Q : (r + 1) * 2 * Q], preferred_element_type=F32
                )
            return carry

        lax.fori_loop(1, C, x_stage, 0)

        def filter_block(r, first):
            for b in range(per // ROWS):
                for h in range(wide):
                    cols = slice(h * LANES, (h + 1) * LANES)
                    sins = slice(Q + h * LANES, Q + (h + 1) * LANES)

                    def spectrum(c, p):
                        re = slice(p * pair + b * ROWS, p * pair + (b + 1) * ROWS)
                        im = slice(p * pair + per + b * ROWS, p * pair + per + (b + 1) * ROWS)
                        real = raw[c, r, re, cols] + raw[c, r, im, sins]
                        imag = raw[c, r, im, cols] - raw[c, r, re, sins]
                        return real, imag

                    wrow = slice(b * ROWS, (b + 1) * ROWS)
                    ax = weights[r, 0, wrow, cols]
                    ay = weights[r, 1, wrow, cols]
                    az = weights[r, 2, wrow, cols]
                    (ry, sy), (rz, sz) = [spectrum(c, 0) for c in (1, 2)]
                    (uy, vy), (uz, vz) = [spectrum(c, 1) for c in (1, 2)]
                    if first:
                        result = {
                            0: (
                                (az * uy - ay * sz, ay * rz + az * vy),
                                (ay * vz + az * ry, az * sy - ay * uz),
                            )
                        }
                    else:
                        (rx, sx), (ux, vx) = spectrum(0, 0), spectrum(0, 1)
                        result = {
                            1: (
                                (ax * sz - az * ux, -(ax * rz + az * vx)),
                                (-(ax * vz + az * rx), ax * uz - az * sx),
                            ),
                            2: (
                                (ay * sx - ax * sy, ax * ry - ay * rx),
                                (ax * vy - ay * vx, ay * ux - ax * uy),
                            ),
                        }
                    for c in result:
                        for p in range(2):
                            for part in range(2):
                                row = p * pair + part * per + b * ROWS
                                filt[c, r, row : row + ROWS, cols] = result[c][p][part].astype(BF16)

        def filter_all(first):
            def body(r, carry):
                filter_block(r, first)
                return carry

            lax.fori_loop(0, 4, body, 0)

        def x_back(c, carry):
            for r in range(4):
                back[r] = jnp.dot(
                    filt[c, r], inv_x[r * Q : (r + 1) * Q, :], preferred_element_type=F32
                )
            for p in range(2):
                for b in range(per // ROWS):
                    for h in range(wide):
                        cols = slice(h * LANES, (h + 1) * LANES)
                        sins = slice(Q + h * LANES, Q + (h + 1) * LANES)
                        re = slice(p * pair + b * ROWS, p * pair + (b + 1) * ROWS)
                        im = slice(p * pair + per + b * ROWS, p * pair + per + (b + 1) * ROWS)
                        real = [back[r, re, cols] - back[r, im, sins] for r in range(4)]
                        imag = [back[r, re, sins] + back[r, im, cols] for r in range(4)]
                        sr, dr, tr, er = real[0] + real[2], real[0] - real[2], real[1] + real[3], real[1] - real[3]
                        si, di, ti, ei = imag[0] + imag[2], imag[0] - imag[2], imag[1] + imag[3], imag[1] - imag[3]
                        values = (
                            (sr + tr, si + ti),
                            (dr - ei, di + er),
                            (sr - tr, si - ti),
                            (dr + ei, di - er),
                        )
                        for j in range(4):
                            for part in range(2):
                                row = part * per + b * ROWS
                                xb[c, p, j * wide + h, row : row + ROWS, :] = values[j][part].astype(BF16)

            dst = pl.ds(pl.multiple_of(mine * pair, pair), pair)

            def body(k, carry):
                t = lax.rem(mine + k, chunks)
                pltpu.make_async_remote_copy(
                    src_ref=xb.at[c, lax.rem(t, 2), t // 2],
                    dst_ref=yr.at[c, dst],
                    send_sem=send_sem.at[2, c],
                    recv_sem=recv_sem.at[2, c],
                    device_id=(t // 2, base + lax.rem(t, 2)),
                    device_id_type=MESH,
                ).start()
                return carry

            lax.fori_loop(1, chunks, body, 0)
            pltpu.make_async_copy(xb.at[c, core, gx], yr.at[c, dst], recv_sem.at[2, c]).start()
            return carry

        filter_all(True)
        lax.fori_loop(0, 1, x_back, 0)
        lax.fori_loop(0, 1, x_stage, 0)
        filter_all(False)
        lax.fori_loop(1, C, x_back, 0)

        def y_back(c, carry):
            pltpu.make_async_copy(yr.at[c], yr.at[c], recv_sem.at[2, c]).wait()
            even = jnp.dot(inv_y[:, 0:half_y], yr[c, 0:half_y, :], preferred_element_type=F32)
            odd = jnp.dot(inv_y[:, half_y:Y], yr[c, half_y:Y, :], preferred_element_type=F32)
            sp[c, 0:half_y, :] = (even + odd).astype(BF16)
            sp[c, half_y:Y, :] = (even - odd).astype(BF16)

            @pl.when(gy != EMPTY)
            def _():
                def body(k, carry):
                    dst = lax.rem(gy + k, NY)
                    pltpu.make_async_remote_copy(
                        src_ref=sp.at[c, pl.ds(pl.multiple_of(dst * yl, yl), yl)],
                        dst_ref=zr.at[c, gy],
                        send_sem=send_sem.at[3, c],
                        recv_sem=recv_sem.at[3, c],
                        device_id=(gx, dst),
                        device_id_type=MESH,
                    ).start()
                    return carry

                lax.fori_loop(1, NY, body, 0)
                pltpu.make_async_copy(
                    sp.at[c, pl.ds(pl.multiple_of(gy * yl, yl), yl)], zr.at[c, gy], recv_sem.at[3, c]
                ).start()

            return carry

        lax.fori_loop(0, C, y_back, 0)

        field_loads[2].wait()
        slots_block = slots[0:ROWS]
        grad_vort = cv
        halos = []

        def finish_velocity(c):
            take_halo(halos[c], 1 + c, 4 + c, 1, None)
            cols_f[1 + c] = cols_f[1 + c] * edge_cols[...]
            edge_rows[...] = rows_f[:, C] * rows_f[:, 4 + c]

            def vel_part(b, carry):
                for n in range(group):
                    z = b * group + n
                    px[n * yl : (n + 1) * yl, :] = (vo[0, z].astype(F32) * adj[c, z]).astype(BF16)
                slopes = jnp.dot(px[...], shift[...], preferred_element_type=F32)
                for n in range(group):
                    z = b * group + n
                    up, down = lax.rem(z + 1, Z), lax.rem(z + Z - 1, Z)
                    rest = slope_y(
                        n,
                        vo[1, z].astype(F32) * adj[c, z],
                        edge_rows[0, pl.ds(z, 1), :],
                        edge_rows[1, pl.ds(z, 1), :],
                    )
                    rest = rest + (
                        vo[2, up].astype(F32) * adj[c, up] - vo[2, down].astype(F32) * adj[c, down]
                    )
                    total = slopes[n * yl : (n + 1) * yl] + at_edges(cols_f[1 + c], z)
                    gl_out[c, z] = (-total - quarter * rest).astype(BF16)
                return carry

            lax.fori_loop(0, Z // group, vel_part, 0)

        for c in range(C):
            come = zr.at[c, 0 : Z - 1]
            pltpu.make_async_copy(come, come, recv_sem.at[3, c]).wait()

            def z_back(b, carry, c=c):
                rows = pl.ds(pl.multiple_of(b * ROWS, ROWS), ROWS)
                values = depth_inverse(
                    [None if k == EMPTY else zr[c, k, rows, :].astype(F32) * scale for k in range(Z)],
                    Z,
                )
                acc = jnp.zeros((ROWS, LANES), F32)
                for z in range(Z):
                    value = adj[c, z, rows, :] + values[z]
                    adj[c, z, rows, :] = value
                    acc = jnp.where(slots_block == z, pltpu.roll(value, 2 * z, 1) if z else value, acc)
                cols_out[1 + c, rows, :] = acc.astype(BF16)
                return carry

            lax.fori_loop(0, yl // ROWS, z_back, 0)
            for z in range(Z):
                rows_f[0, 4 + c, z : z + 1, :] = adj[c, z, 0:1, :]
                rows_f[1, 4 + c, z : z + 1, :] = adj[c, z, yl - 1 : yl, :]
            rows_out[:, 4 + c] = rows_f[:, 4 + c].astype(BF16)
            halos.append(send_halo(1 + c, 4 + c, 1))

            def vort_part(z, carry, c=c):
                a = adj[c, z]
                for j in range(3):
                    term = a * vel_slope[j, c, z]
                    if j == c:
                        term = term + a
                    if c:
                        term = grad_vort[j, z] + term
                    if c == C - 1:
                        gv_out[j, z] = term.astype(BF16)
                    else:
                        grad_vort[j, z] = term
                return carry

            lax.fori_loop(0, Z, vort_part, 0)
            if c:
                finish_velocity(c - 1)
        finish_velocity(C - 1)

        for c in range(C):
            sent = zb.at[c, 0 : NY - 2]
            pltpu.make_async_copy(sent, sent, send_sem.at[0, c]).wait()

            @pl.when(gy == EMPTY)
            def _():
                more = zb.at[c, 0]
                pltpu.make_async_copy(more, more, send_sem.at[0, c]).wait()

            sent = ys.at[c, 0 : (chunks - 1) * pair]
            pltpu.make_async_copy(sent, sent, send_sem.at[1, c]).wait()
            sent = yr.at[c, 0 : (chunks - 1) * pair]
            pltpu.make_async_copy(sent, sent, send_sem.at[2, c]).wait()

            @pl.when(gy != EMPTY)
            def _():
                last = sp.at[c, 0 : (NY - 1) * yl]
                pltpu.make_async_copy(last, last, send_sem.at[3, c]).wait()


    def vmem(shape, dtype=BF16):
        return pltpu.VMEM(shape, dtype)

    scratch = [
        vmem((C, Z, yl, LANES), F32),
        vmem((C, Z, yl, LANES), F32),
        vmem((C, Z, yl, LANES)),
        vmem((C, Z, yl, LANES)),
        vmem((3, C, Z, yl, LANES), F32),
        vmem((LANES, LANES)),
        vmem((group * yl, LANES)),
        vmem((group, yl + 16, LANES), F32),
        vmem((2, Z, LANES), F32),
        vmem((yl, LANES), F32),
        vmem((2, 7, Z, LANES), F32),
        vmem((1 + C, yl, LANES), F32),
        vmem((2, 7, Z, LANES)),
        vmem((1 + C, yl, LANES)),
        vmem((2, 7, Z, LANES)),
        vmem((2, 1 + C, yl, LANES)),
    ]
    scratch += [vmem(s.shape, F32) for s in seeds]
    scratch += [
        vmem((Y, half_y)),
        vmem((half_y, Y)),
        vmem((Q, 8 * Q)),
        vmem((4 * Q, 2 * Q)),
        vmem((4, 3, per, Q), F32),
        vmem((C, Z, yl, LANES)),
        vmem((C, Y, LANES)),
        vmem((C, Y, LANES)),
        vmem((C, 2, NX, pair, LANES)),
        vmem((4, 2 * pair, Q)),
        vmem((C, 4, 2 * pair, 2 * Q), F32),
        vmem((4, 2 * pair, 2 * Q), F32),
        vmem((C, 4, 2 * pair, Q)),
        vmem((C, 2, NX, pair, LANES)),
        vmem((C, Y, LANES)),
        vmem((C, Y, LANES)),
        vmem((C, Z, yl, LANES)),
        pltpu.SemaphoreType.DMA((C + 3,)),
        pltpu.SemaphoreType.DMA((4,)),
        pltpu.SemaphoreType.DMA((4, C)),
        pltpu.SemaphoreType.DMA((4, C)),
        pltpu.SemaphoreType.DMA((1 + C, 4)),
        pltpu.SemaphoreType.DMA((1 + C, 4)),
    ]
    call = pl.pallas_call(
        kernel,
        out_shape=(
            jax.ShapeDtypeStruct((C, Z, yl, LANES), BF16),
            jax.ShapeDtypeStruct((C, Z, yl, LANES), BF16),
        ),
        in_specs=[pl.BlockSpec(memory_space=pltpu.HBM)] * 8,
        out_specs=(pl.BlockSpec(memory_space=pltpu.VMEM), pl.BlockSpec(memory_space=pltpu.VMEM)),
        scratch_shapes=scratch,
        compiler_params=pltpu.CompilerParams(
            collective_id=0, has_side_effects=True, vmem_limit_bytes=49 << 20
        ),
        name="spectral",
    )

    def run(cot_vel, cot_vort, velocity, vorticity):
        operands = [cot_vel, cot_vort, velocity, vorticity] + [jnp.asarray(s) for s in seeds]
        return call(*[pltpu.with_memory_space_constraint(x, pltpu.HBM) for x in operands])

    return run


def widen(grad_vort, grad_vel):
    C, Z, yl, _ = grad_vort.shape

    def kernel(a, b, wide_a_h, wide_b_h, wide_a, wide_b, store_sem):
        stores = []
        for c in range(C):
            for i, (narrow, wide, out) in enumerate(((a, wide_a, wide_a_h), (b, wide_b, wide_b_h))):

                def body(z, carry):
                    wide[c, z] = narrow[c, z].astype(F32)
                    return carry

                lax.fori_loop(0, Z, body, 0)
                stores.append(pltpu.make_async_copy(wide.at[c], out.at[c], store_sem.at[i, c]))
                stores[-1].start()
        for store in stores:
            store.wait()

    vmem = pl.BlockSpec(memory_space=pltpu.VMEM)
    hbm = pl.BlockSpec(memory_space=pltpu.HBM)
    shape = jax.ShapeDtypeStruct((C, Z, yl, LANES), F32)
    wide = pltpu.VMEM((C, Z, yl, LANES), F32)
    return pl.pallas_call(
        kernel,
        out_shape=(shape, shape),
        in_specs=[vmem, vmem],
        out_specs=(hbm, hbm),
        scratch_shapes=[wide, wide, pltpu.SemaphoreType.DMA((2, C))],
        compiler_params=pltpu.CompilerParams(vmem_limit_bytes=16 << 20),
        name="widen",
    )(grad_vort, grad_vel)


def local(cot_vort, cot_vel, vorticity, velocity):
    C, Z, yl, _ = cot_vel.shape
    spectral = make_spectral(C, Z, yl, lax.axis_size("gx"), lax.axis_size("gy"))
    return widen(*spectral(cot_vel, cot_vort, velocity, vorticity))


def solution(mesh):
    return jax.shard_map(
        local,
        mesh=mesh,
        in_specs=(
            P(None, None, "gy", "gx"),
            P(None, None, "gy", "gx"),
            P(None, None, "gy", "gx"),
            P(None, None, "gy", "gx"),
        ),
        out_specs=(P(None, None, "gy", "gx"), P(None, None, "gy", "gx")),
        check_vma=False,
    )
```

```python
import math

import jax
import jax.numpy as jnp
import numpy as np
from jax import lax
from jax.experimental import pallas as pl
from jax.experimental.pallas import tpu as pltpu
from jax.sharding import PartitionSpec as P

step_size = 0.5
F32 = jnp.float32
BF16 = jnp.bfloat16
LANES = 128
ROWS = 16
MESH = pl.DeviceIdType.MESH
EMPTY = 1


def seed(alpha, beta, length):
    turns = np.concatenate([beta, alpha], 0) % length
    angles = turns * (2.0 * np.pi / length)
    return np.stack([np.cos(angles), np.sin(angles)]).astype(np.float32)


def y_modes(Y, chunks):
    half = chunks // 2
    per = (Y // 2) // chunks
    row = np.arange(Y)
    chunk, part, index = row // (2 * per), (row // per) % 2, row % per
    return 2 * ((chunk % half) * per + index) + chunk // half, part


def tables(X, Y, chunks):
    modes, part = y_modes(Y, chunks)
    quarter = Y // 4
    yy = np.arange(Y // 2)
    start = np.arange(0, Y, ROWS)
    forward_y = seed(
        modes[start][:, None] * yy + quarter * part[start][:, None],
        2 * np.arange(ROWS)[:, None] * yy,
        Y,
    )
    block = np.arange(0, Y // 2, ROWS)
    inverse_y = seed(
        block[:, None] * modes + quarter * part, np.arange(ROWS)[:, None] * modes, Y
    )
    Q = X // 4
    k = np.arange(Q)
    freq = np.concatenate([4 * k + r for r in range(4) for _ in range(2)])
    shift = np.concatenate([np.full(Q, s * (X // 4)) for _ in range(4) for s in range(2)])
    block = np.arange(0, Q, ROWS)
    forward_x = seed(block[:, None] * freq - shift, np.arange(ROWS)[:, None] * freq, X)
    xx = np.concatenate([k, k])
    shift = np.concatenate([np.zeros(Q), np.full(Q, X // 4)]).astype(np.int64)
    first = np.concatenate([4 * block + r for r in range(4)])
    inverse_x = seed(first[:, None] * xx - shift, 4 * np.arange(ROWS)[:, None] * xx, X)
    return forward_y, inverse_y, forward_x, inverse_x


def combine(terms):
    total = None
    for factor, value in terms:
        if abs(factor) < 1e-12:
            continue
        if total is None:
            total = value if factor == 1.0 else (-value if factor == -1.0 else value * factor)
        elif factor == 1.0:
            total = total + value
        elif factor == -1.0:
            total = total - value
        else:
            total = total + value * factor
    return total


def trig(kind, product, Z):
    value = (math.cos if kind == "c" else math.sin)(2.0 * math.pi * (product % Z) / Z)
    nearest = round(value)
    return float(nearest) if abs(value - nearest) < 1e-12 else value


def depth_forward(f, Z):
    H = Z // 2
    even = [f[0]] + [f[z] + f[Z - z] for z in range(1, H)] + [f[H]]
    odd = [None] + [f[z] - f[Z - z] for z in range(1, H)]
    real, imag = [None] * H, [None] * H
    for k in range(H // 2 + 1):
        a = combine([(trig("c", k * z, Z), even[z]) for z in range(0, H + 1, 2)])
        b = combine([(trig("c", k * z, Z), even[z]) for z in range(1, H + 1, 2)])
        total = a if b is None else (b if a is None else a + b)
        real[k] = total
        if 0 < k < H - k:
            real[H - k] = a if b is None else (-b if a is None else a - b)
        if k == 0:
            continue
        a = combine([(trig("s", k * z, Z), odd[z]) for z in range(2, H, 2)])
        b = combine([(trig("s", k * z, Z), odd[z]) for z in range(1, H, 2)])
        imag[k] = -(a if b is None else (b if a is None else a + b))
        if k < H - k:
            imag[H - k] = -b if a is None else (a if b is None else a - b)
    planes = []
    for k in range(H):
        planes += [real[k], jnp.zeros_like(real[0]) if k == 0 else imag[k]]
    return planes


def depth_inverse(planes, Z):
    H = Z // 2
    s = [planes[2 * k] for k in range(H)]
    d = [planes[2 * k + 1] for k in range(H)]
    even, odd = [None] * (H + 1), [None] * (H + 1)
    for z in range(H // 2 + 1):
        a = combine([((1.0 if k == 0 else 2.0 * trig("c", k * z, Z)), s[k]) for k in range(0, H, 2)])
        b = combine([(2.0 * trig("c", k * z, Z), s[k]) for k in range(1, H, 2)])
        even[z] = a if b is None else a + b
        even[H - z] = a if b is None else a - b
        if z == 0:
            continue
        a = combine([(2.0 * trig("s", k * z, Z), d[k]) for k in range(2, H, 2)])
        b = combine([(2.0 * trig("s", k * z, Z), d[k]) for k in range(1, H, 2)])
        odd[z] = a if b is None else (b if a is None else a + b)
        odd[H - z] = -a if b is None else (b if a is None else b - a)
    out = [None] * Z
    out[0], out[H] = even[0], even[H]
    for z in range(1, H):
        out[z] = even[z] + odd[z]
        out[Z - z] = even[z] - odd[z]
    return out


def make_spectral(C, Z, yl, NX, NY):
    X, Y = NX * LANES, NY * yl
    assert NY == Z
    chunks = NX * 2
    per = (Y // 2) // chunks
    pair = 2 * per
    half_y = Y // 2
    Q = X // 4
    wide = Q // LANES
    scale = 2.0 / (X * Y * Z)
    seeds = tables(X, Y, chunks)
    group = 4

    def kernel(
        cv_h,
        cw_h,
        ve_h,
        vo_h,
        sfy_h,
        siy_h,
        sfx_h,
        six_h,
        gv_out,
        gl_out,
        cv,
        adj,
        ve,
        vo,
        vel_slope,
        shift,
        px,
        yp,
        edge_rows,
        edge_cols,
        rows_f,
        cols_f,
        rows_out,
        cols_out,
        rows_in,
        cols_in,
        sfy,
        siy,
        sfx,
        six,
        fwd_y,
        inv_y,
        fwd_x,
        inv_x,
        weights,
        zb,
        fy,
        ys,
        xr,
        lx,
        raw,
        back,
        filt,
        xb,
        yr,
        sp,
        zr,
        load_sem,
        seed_sem,
        send_sem,
        recv_sem,
        halo_send,
        halo_recv,
    ):
        gx = lax.axis_index("gx")
        gy = lax.axis_index("gy")
        core = lax.rem(gy, 2)
        base = gy - core
        mine = gx * 2 + core

        cv_loads = []
        for c in range(C):
            cv_loads.append(pltpu.make_async_copy(cv_h.at[c], cv.at[c], load_sem.at[c]))
            cv_loads[-1].start()
        field_loads = []
        for i, (src, dst) in enumerate(((ve_h, ve), (vo_h, vo), (cw_h, adj))):
            field_loads.append(pltpu.make_async_copy(src, dst, load_sem.at[C + i]))
            field_loads[-1].start()

        barrier = pltpu.get_barrier_semaphore()
        right, left = (lax.rem(gx + 1, NX), gy), (lax.rem(gx + NX - 1, NX), gy)
        after, before = (gx, lax.rem(gy + 1, NY)), (gx, lax.rem(gy + NY - 1, NY))

        def greet_y(k, carry):
            pl.semaphore_signal(
                barrier, inc=1, device_id=(gx, lax.rem(gy + k, NY)), device_id_type=MESH
            )
            return carry

        lax.fori_loop(1, NY, greet_y, 0)

        def greet_x(k, carry):
            t = lax.rem(mine + k, chunks)
            pl.semaphore_signal(
                barrier, inc=1, device_id=(t // 2, base + lax.rem(t, 2)), device_id_type=MESH
            )
            return carry

        lax.fori_loop(1, chunks, greet_x, 0)

        loads = []
        for i, (src, dst) in enumerate(((sfy_h, sfy), (sfx_h, sfx), (siy_h, siy), (six_h, six))):
            loads.append(pltpu.make_async_copy(src, dst, seed_sem.at[i]))
            loads[-1].start()

        def z_block(c, b):
            rows = pl.ds(pl.multiple_of(b * ROWS, ROWS), ROWS)
            planes = depth_forward([cv[c, z, rows, :] for z in range(Z)], Z)
            for k in range(Z):
                if k != EMPTY:
                    zb[c, k, rows, :] = planes[k].astype(BF16)

        def send_planes(c):
            row = pl.ds(pl.multiple_of(gy * yl, yl), yl)

            def body(k, carry):
                dst = lax.rem(gy + k, NY)

                @pl.when(dst != EMPTY)
                def _():
                    pltpu.make_async_remote_copy(
                        src_ref=zb.at[c, dst],
                        dst_ref=fy.at[c, row],
                        send_sem=send_sem.at[0, c],
                        recv_sem=recv_sem.at[0, c],
                        device_id=(gx, dst),
                        device_id_type=MESH,
                    ).start()

                return carry

            lax.fori_loop(1, NY, body, 0)

            @pl.when(gy != EMPTY)
            def _():
                pltpu.make_async_copy(zb.at[c, gy], fy.at[c, row], recv_sem.at[0, c]).start()

            @pl.when(gy == EMPTY)
            def _():
                fy[c] = jnp.zeros((Y, LANES), BF16)

        for c in (1, 2, 0):
            cv_loads[c].wait()
            lax.fori_loop(0, yl // ROWS, lambda b, carry, c=c: (z_block(c, b), carry)[1], 0)
            if c == 1:
                pl.semaphore_wait(barrier, NY - 1 + chunks - 1)
            send_planes(c)

        lane = lax.broadcasted_iota(jnp.int32, (yl, LANES), 1)
        line = lax.broadcasted_iota(jnp.int32, (yl, LANES), 0)
        quarter = 0.5 * step_size

        def send_halo(stage, first, count):
            copies = []
            for i, (src, dst, device) in enumerate(
                (
                    (rows_out.at[1, first : first + count], rows_in.at[0, first : first + count], after),
                    (rows_out.at[0, first : first + count], rows_in.at[1, first : first + count], before),
                    (cols_out.at[stage], cols_in.at[0, stage], right),
                    (cols_out.at[stage], cols_in.at[1, stage], left),
                )
            ):
                copies.append(
                    pltpu.make_async_remote_copy(
                        src_ref=src,
                        dst_ref=dst,
                        send_sem=halo_send.at[stage, i],
                        recv_sem=halo_recv.at[stage, i],
                        device_id=device,
                        device_id_type=MESH,
                    )
                )
                copies[-1].start()
            return copies

        def take_halo(copies, stage, first, count, factor):
            for copy in copies:
                copy.wait()
            rows_f[:, first : first + count] = rows_in[:, first : first + count].astype(F32)
            from_left = pltpu.roll(cols_in[0, stage].astype(F32), 2, 1)
            from_right = cols_in[1, stage].astype(F32)
            if factor is not None:
                from_left, from_right = -factor * from_left, factor * from_right
            cols_f[stage] = jnp.where(lane % 2 == 0, from_right, from_left)

        def at_edges(cols, index):
            moved = pltpu.roll(cols, LANES - 1 - 2 * index, 1)
            return jnp.where((lane == 0) | (lane == LANES - 1), moved, 0.0)

        def slope_y(slot, f, low, high):
            yp[slot, 8 : 8 + yl, :] = f
            yp[slot, 7:8, :] = low
            yp[slot, 8 + yl : 9 + yl, :] = high
            return yp[slot, 9 : 9 + yl, :] - yp[slot, 7 : 7 + yl, :]

        row_index = lax.broadcasted_iota(jnp.int32, (LANES, LANES), 0)
        col_index = lax.broadcasted_iota(jnp.int32, (LANES, LANES), 1)
        shift[...] = jnp.where(
            row_index == col_index + 1, quarter, jnp.where(row_index == col_index - 1, -quarter, 0.0)
        ).astype(BF16)

        field_loads[0].wait()
        field_loads[1].wait()

        slots = lax.rem(lane + 1, LANES) // 2

        def pack_plane(z, acc):
            for i in range(C + 1):
                plane = (ve[i, z] if i < C else vo[0, z]).astype(F32)
                acc = jnp.where(slots == i * Z + z, pltpu.roll(plane, 2 * (i * Z + z), 1), acc)
                edge = plane if i < C else vo[1, z].astype(F32)
                rows_f[0, i, pl.ds(z, 1), :] = edge[0:1]
                rows_f[1, i, pl.ds(z, 1), :] = edge[yl - 1 : yl]
            return acc

        cols_out[0] = lax.fori_loop(0, Z, pack_plane, jnp.zeros((yl, LANES), F32)).astype(BF16)
        rows_out[:, 0 : C + 1] = rows_f[:, 0 : C + 1].astype(BF16)
        field_halo = send_halo(0, 0, C + 1)

        def build(dst, table, count, width):
            def body(a, carry):
                row = pl.ds(ROWS + a, 1)
                value = table[0, 0:ROWS, :] * table[0, row, :] - table[1, 0:ROWS, :] * table[1, row, :]
                dst[pl.ds(pl.multiple_of(a * ROWS, ROWS), ROWS), :] = value.astype(BF16)
                return carry

            lax.fori_loop(0, count, body, 0)

        loads[0].wait()
        build(fwd_y, sfy, Y // ROWS, half_y)

        def y_stage(i, carry):
            c = lax.rem(i + 1, C)

            @pl.when(gy != EMPTY)
            def _():
                pltpu.make_async_copy(fy.at[c], fy.at[c], recv_sem.at[0, c]).wait()

            low = fy[c, 0:half_y, :].astype(F32)
            high = fy[c, half_y:Y, :].astype(F32)
            ys[c, 0:half_y, :] = jnp.dot(
                fwd_y[0:half_y, :], (low + high).astype(BF16), preferred_element_type=F32
            ).astype(BF16)
            ys[c, half_y:Y, :] = jnp.dot(
                fwd_y[half_y:Y, :], (low - high).astype(BF16), preferred_element_type=F32
            ).astype(BF16)

            def body(k, carry):
                t = lax.rem(mine + k, chunks)
                pltpu.make_async_remote_copy(
                    src_ref=ys.at[c, pl.ds(pl.multiple_of(t * pair, pair), pair)],
                    dst_ref=xr.at[c, core, gx],
                    send_sem=send_sem.at[1, c],
                    recv_sem=recv_sem.at[1, c],
                    device_id=(t // 2, base + lax.rem(t, 2)),
                    device_id_type=MESH,
                ).start()
                return carry

            lax.fori_loop(1, chunks, body, 0)
            pltpu.make_async_copy(
                ys.at[c, pl.ds(pl.multiple_of(mine * pair, pair), pair)],
                xr.at[c, core, gx],
                recv_sem.at[1, c],
            ).start()
            return carry

        lax.fori_loop(0, C, y_stage, 0)

        loads[1].wait()
        build(fwd_x, sfx, Q // ROWS, 8 * Q)
        loads[2].wait()
        build(inv_y, siy, half_y // ROWS, Y)
        loads[3].wait()
        build(inv_x, six, 4 * Q // ROWS, 2 * Q)

        depth_wave = (gy // 2).astype(F32) * (2.0 * math.pi / Z)
        chunk_half = mine // (chunks // 2)
        first_mode = 2 * lax.rem(mine, chunks // 2) * per + chunk_half
        mode = first_mode + 2 * lax.broadcasted_iota(jnp.int32, (per, Q), 0)
        wave_y = mode.astype(F32) * (2.0 * math.pi / Y)
        for r in range(4):
            kx = 4 * lax.broadcasted_iota(jnp.int32, (per, Q), 1) + r
            wave_x = jnp.where(kx < X // 2, kx, kx - X).astype(F32) * (2.0 * math.pi / X)
            square = wave_x * wave_x + wave_y * wave_y + depth_wave * depth_wave
            weight = jnp.where(square > 0, 1.0 / jnp.where(square > 0, square, 1.0), 0.0)
            weight = jnp.where(kx == X // 2, 0.0, weight)
            weight = jnp.where(mode == 0, 0.5 * weight, weight)
            weights[r, 0] = weight * wave_x
            weights[r, 1] = weight * wave_y
            weights[r, 2] = weight * depth_wave

        take_halo(field_halo, 0, 0, C + 1, quarter)
        edge_cols[...] = pltpu.roll(cols_f[0], LANES - 2 * C * Z, 1)

        def velocity_slopes(i, carry):
            flat = ve[i].reshape(Z * yl, LANES)
            vel_slope[0, i] = jnp.dot(flat, shift[...], preferred_element_type=F32).reshape(Z, yl, LANES)

            def layer(b, carry):
                for n in range(group):
                    z = b * group + n
                    up, down = lax.rem(z + 1, Z), lax.rem(z + Z - 1, Z)
                    vel_slope[0, i, z] = vel_slope[0, i, z] + at_edges(cols_f[0], i * Z + z)
                    vel_slope[1, i, z] = quarter * slope_y(
                        n, ve[i, z].astype(F32), rows_f[0, i, pl.ds(z, 1), :], rows_f[1, i, pl.ds(z, 1), :]
                    )
                    vel_slope[2, i, z] = quarter * (ve[i, up].astype(F32) - ve[i, down].astype(F32))
                return carry

            return lax.fori_loop(0, Z // group, layer, carry)

        lax.fori_loop(0, C, velocity_slopes, 0)

        def x_stage(c, carry):
            pltpu.make_async_copy(xr.at[c], xr.at[c], recv_sem.at[1, c]).wait()
            for p in range(2):
                for b in range(per // ROWS):
                    for h in range(wide):
                        a = []
                        for part in range(2):
                            rows = slice(part * per + b * ROWS, part * per + (b + 1) * ROWS)
                            a.append([xr[c, p, j * wide + h, rows, :].astype(F32) for j in range(4)])
                        (r0, r1, r2, r3), (i0, i1, i2, i3) = a
                        sr, dr, tr, er = r0 + r2, r0 - r2, r1 + r3, r1 - r3
                        si, di, ti, ei = i0 + i2, i0 - i2, i1 + i3, i1 - i3
                        values = (
                            (sr + tr, si + ti),
                            (dr + ei, di - er),
                            (sr - tr, si - ti),
                            (dr - ei, di + er),
                        )
                        for r in range(4):
                            for part in range(2):
                                row = p * pair + part * per + b * ROWS
                                lx[r, row : row + ROWS, h * LANES : (h + 1) * LANES] = values[r][
                                    part
                                ].astype(BF16)
            for r in range(4):
                raw[c, r] = jnp.dot(
                    lx[r], fwd_x[:, r * 2 * Q : (r + 1) * 2 * Q], preferred_element_type=F32
                )
            return carry

        lax.fori_loop(1, C, x_stage, 0)

        def filter_block(r, first):
            for b in range(per // ROWS):
                for h in range(wide):
                    cols = slice(h * LANES, (h + 1) * LANES)
                    sins = slice(Q + h * LANES, Q + (h + 1) * LANES)

                    def spectrum(c, p):
                        re = slice(p * pair + b * ROWS, p * pair + (b + 1) * ROWS)
                        im = slice(p * pair + per + b * ROWS, p * pair + per + (b + 1) * ROWS)
                        real = raw[c, r, re, cols] + raw[c, r, im, sins]
                        imag = raw[c, r, im, cols] - raw[c, r, re, sins]
                        return real, imag

                    wrow = slice(b * ROWS, (b + 1) * ROWS)
                    ax = weights[r, 0, wrow, cols]
                    ay = weights[r, 1, wrow, cols]
                    az = weights[r, 2, wrow, cols]
                    (ry, sy), (rz, sz) = [spectrum(c, 0) for c in (1, 2)]
                    (uy, vy), (uz, vz) = [spectrum(c, 1) for c in (1, 2)]
                    if first:
                        result = {
                            0: (
                                (az * uy - ay * sz, ay * rz + az * vy),
                                (ay * vz + az * ry, az * sy - ay * uz),
                            )
                        }
                    else:
                        (rx, sx), (ux, vx) = spectrum(0, 0), spectrum(0, 1)
                        result = {
                            1: (
                                (ax * sz - az * ux, -(ax * rz + az * vx)),
                                (-(ax * vz + az * rx), ax * uz - az * sx),
                            ),
                            2: (
                                (ay * sx - ax * sy, ax * ry - ay * rx),
                                (ax * vy - ay * vx, ay * ux - ax * uy),
                            ),
                        }
                    for c in result:
                        for p in range(2):
                            for part in range(2):
                                row = p * pair + part * per + b * ROWS
                                filt[c, r, row : row + ROWS, cols] = result[c][p][part].astype(BF16)

        def filter_all(first):
            def body(r, carry):
                filter_block(r, first)
                return carry

            lax.fori_loop(0, 4, body, 0)

        def x_back(c, carry):
            for r in range(4):
                back[r] = jnp.dot(
                    filt[c, r], inv_x[r * Q : (r + 1) * Q, :], preferred_element_type=F32
                )
            for p in range(2):
                for b in range(per // ROWS):
                    for h in range(wide):
                        cols = slice(h * LANES, (h + 1) * LANES)
                        sins = slice(Q + h * LANES, Q + (h + 1) * LANES)
                        re = slice(p * pair + b * ROWS, p * pair + (b + 1) * ROWS)
                        im = slice(p * pair + per + b * ROWS, p * pair + per + (b + 1) * ROWS)
                        real = [back[r, re, cols] - back[r, im, sins] for r in range(4)]
                        imag = [back[r, re, sins] + back[r, im, cols] for r in range(4)]
                        sr, dr, tr, er = real[0] + real[2], real[0] - real[2], real[1] + real[3], real[1] - real[3]
                        si, di, ti, ei = imag[0] + imag[2], imag[0] - imag[2], imag[1] + imag[3], imag[1] - imag[3]
                        values = (
                            (sr + tr, si + ti),
                            (dr - ei, di + er),
                            (sr - tr, si - ti),
                            (dr + ei, di - er),
                        )
                        for j in range(4):
                            for part in range(2):
                                row = part * per + b * ROWS
                                xb[c, p, j * wide + h, row : row + ROWS, :] = values[j][part].astype(BF16)

            dst = pl.ds(pl.multiple_of(mine * pair, pair), pair)

            def body(k, carry):
                t = lax.rem(mine + k, chunks)
                pltpu.make_async_remote_copy(
                    src_ref=xb.at[c, lax.rem(t, 2), t // 2],
                    dst_ref=yr.at[c, dst],
                    send_sem=send_sem.at[2, c],
                    recv_sem=recv_sem.at[2, c],
                    device_id=(t // 2, base + lax.rem(t, 2)),
                    device_id_type=MESH,
                ).start()
                return carry

            lax.fori_loop(1, chunks, body, 0)
            pltpu.make_async_copy(xb.at[c, core, gx], yr.at[c, dst], recv_sem.at[2, c]).start()
            return carry

        filter_all(True)
        lax.fori_loop(0, 1, x_back, 0)
        lax.fori_loop(0, 1, x_stage, 0)
        filter_all(False)
        lax.fori_loop(1, C, x_back, 0)

        def y_back(c, carry):
            pltpu.make_async_copy(yr.at[c], yr.at[c], recv_sem.at[2, c]).wait()
            even = jnp.dot(inv_y[:, 0:half_y], yr[c, 0:half_y, :], preferred_element_type=F32)
            odd = jnp.dot(inv_y[:, half_y:Y], yr[c, half_y:Y, :], preferred_element_type=F32)
            sp[c, 0:half_y, :] = (even + odd).astype(BF16)
            sp[c, half_y:Y, :] = (even - odd).astype(BF16)

            @pl.when(gy != EMPTY)
            def _():
                def body(k, carry):
                    dst = lax.rem(gy + k, NY)
                    pltpu.make_async_remote_copy(
                        src_ref=sp.at[c, pl.ds(pl.multiple_of(dst * yl, yl), yl)],
                        dst_ref=zr.at[c, gy],
                        send_sem=send_sem.at[3, c],
                        recv_sem=recv_sem.at[3, c],
                        device_id=(gx, dst),
                        device_id_type=MESH,
                    ).start()
                    return carry

                lax.fori_loop(1, NY, body, 0)
                pltpu.make_async_copy(
                    sp.at[c, pl.ds(pl.multiple_of(gy * yl, yl), yl)], zr.at[c, gy], recv_sem.at[3, c]
                ).start()

            return carry

        lax.fori_loop(0, C, y_back, 0)

        field_loads[2].wait()
        slots_block = slots[0:ROWS]
        halos = []

        def finish_velocity(c):
            take_halo(halos[c], 1 + c, 4 + c, 1, None)
            cols_f[1 + c] = cols_f[1 + c] * edge_cols[...]
            edge_rows[...] = rows_f[:, C] * rows_f[:, 4 + c]

            def vel_part(b, carry):
                for n in range(group):
                    z = b * group + n
                    px[n * yl : (n + 1) * yl, :] = (vo[0, z].astype(F32) * adj[c, z]).astype(BF16)
                slopes = jnp.dot(px[...], shift[...], preferred_element_type=F32)
                for n in range(group):
                    z = b * group + n
                    up, down = lax.rem(z + 1, Z), lax.rem(z + Z - 1, Z)
                    rest = slope_y(
                        n,
                        vo[1, z].astype(F32) * adj[c, z],
                        edge_rows[0, pl.ds(z, 1), :],
                        edge_rows[1, pl.ds(z, 1), :],
                    )
                    rest = rest + (
                        vo[2, up].astype(F32) * adj[c, up] - vo[2, down].astype(F32) * adj[c, down]
                    )
                    total = slopes[n * yl : (n + 1) * yl] + at_edges(cols_f[1 + c], z)
                    gl_out[c, z] = (-total - quarter * rest).astype(BF16)
                return carry

            lax.fori_loop(0, Z // group, vel_part, 0)

        for c in range(C):
            come = zr.at[c, 0 : Z - 1]
            pltpu.make_async_copy(come, come, recv_sem.at[3, c]).wait()

            def z_back(b, carry, c=c):
                rows = pl.ds(pl.multiple_of(b * ROWS, ROWS), ROWS)
                values = depth_inverse(
                    [None if k == EMPTY else zr[c, k, rows, :].astype(F32) * scale for k in range(Z)],
                    Z,
                )
                acc = jnp.zeros((ROWS, LANES), F32)
                for z in range(Z):
                    value = adj[c, z, rows, :] + values[z]
                    adj[c, z, rows, :] = value
                    acc = jnp.where(slots_block == z, pltpu.roll(value, 2 * z, 1) if z else value, acc)
                cols_out[1 + c, rows, :] = acc.astype(BF16)
                return carry

            lax.fori_loop(0, yl // ROWS, z_back, 0)
            for z in range(Z):
                rows_f[0, 4 + c, z : z + 1, :] = adj[c, z, 0:1, :]
                rows_f[1, 4 + c, z : z + 1, :] = adj[c, z, yl - 1 : yl, :]
            rows_out[:, 4 + c] = rows_f[:, 4 + c].astype(BF16)
            halos.append(send_halo(1 + c, 4 + c, 1))

        def vort_part(z, carry):
            a = [adj[i, z] for i in range(C)]
            for j in range(3):
                total = a[j]
                for i in range(C):
                    total = total + a[i] * vel_slope[j, i, z]
                gv_out[j, z] = total.astype(BF16)
            return carry

        lax.fori_loop(0, Z, vort_part, 0)
        for c in range(C):
            finish_velocity(c)

        for c in range(C):
            sent = zb.at[c, 0 : NY - 2]
            pltpu.make_async_copy(sent, sent, send_sem.at[0, c]).wait()

            @pl.when(gy == EMPTY)
            def _():
                more = zb.at[c, 0]
                pltpu.make_async_copy(more, more, send_sem.at[0, c]).wait()

            sent = ys.at[c, 0 : (chunks - 1) * pair]
            pltpu.make_async_copy(sent, sent, send_sem.at[1, c]).wait()
            sent = yr.at[c, 0 : (chunks - 1) * pair]
            pltpu.make_async_copy(sent, sent, send_sem.at[2, c]).wait()

            @pl.when(gy != EMPTY)
            def _():
                last = sp.at[c, 0 : (NY - 1) * yl]
                pltpu.make_async_copy(last, last, send_sem.at[3, c]).wait()


    def vmem(shape, dtype=BF16):
        return pltpu.VMEM(shape, dtype)

    scratch = [
        vmem((C, Z, yl, LANES), F32),
        vmem((C, Z, yl, LANES), F32),
        vmem((C, Z, yl, LANES)),
        vmem((C, Z, yl, LANES)),
        vmem((3, C, Z, yl, LANES), F32),
        vmem((LANES, LANES)),
        vmem((group * yl, LANES)),
        vmem((group, yl + 16, LANES), F32),
        vmem((2, Z, LANES), F32),
        vmem((yl, LANES), F32),
        vmem((2, 7, Z, LANES), F32),
        vmem((1 + C, yl, LANES), F32),
        vmem((2, 7, Z, LANES)),
        vmem((1 + C, yl, LANES)),
        vmem((2, 7, Z, LANES)),
        vmem((2, 1 + C, yl, LANES)),
    ]
    scratch += [vmem(s.shape, F32) for s in seeds]
    scratch += [
        vmem((Y, half_y)),
        vmem((half_y, Y)),
        vmem((Q, 8 * Q)),
        vmem((4 * Q, 2 * Q)),
        vmem((4, 3, per, Q), F32),
        vmem((C, Z, yl, LANES)),
        vmem((C, Y, LANES)),
        vmem((C, Y, LANES)),
        vmem((C, 2, NX, pair, LANES)),
        vmem((4, 2 * pair, Q)),
        vmem((C, 4, 2 * pair, 2 * Q), F32),
        vmem((4, 2 * pair, 2 * Q), F32),
        vmem((C, 4, 2 * pair, Q)),
        vmem((C, 2, NX, pair, LANES)),
        vmem((C, Y, LANES)),
        vmem((C, Y, LANES)),
        vmem((C, Z, yl, LANES)),
        pltpu.SemaphoreType.DMA((C + 3,)),
        pltpu.SemaphoreType.DMA((4,)),
        pltpu.SemaphoreType.DMA((4, C)),
        pltpu.SemaphoreType.DMA((4, C)),
        pltpu.SemaphoreType.DMA((1 + C, 4)),
        pltpu.SemaphoreType.DMA((1 + C, 4)),
    ]
    call = pl.pallas_call(
        kernel,
        out_shape=(
            jax.ShapeDtypeStruct((C, Z, yl, LANES), BF16),
            jax.ShapeDtypeStruct((C, Z, yl, LANES), BF16),
        ),
        in_specs=[pl.BlockSpec(memory_space=pltpu.HBM)] * 8,
        out_specs=(pl.BlockSpec(memory_space=pltpu.VMEM), pl.BlockSpec(memory_space=pltpu.VMEM)),
        scratch_shapes=scratch,
        compiler_params=pltpu.CompilerParams(
            collective_id=0, has_side_effects=True, vmem_limit_bytes=49 << 20
        ),
        name="spectral",
    )

    def run(cot_vel, cot_vort, velocity, vorticity):
        operands = [cot_vel, cot_vort, velocity, vorticity] + [jnp.asarray(s) for s in seeds]
        return call(*[pltpu.with_memory_space_constraint(x, pltpu.HBM) for x in operands])

    return run


def widen(grad_vort, grad_vel):
    C, Z, yl, _ = grad_vort.shape

    def kernel(a, b, wide_a_h, wide_b_h, wide_a, wide_b, store_sem):
        stores = []
        for c in range(C):
            for i, (narrow, wide, out) in enumerate(((a, wide_a, wide_a_h), (b, wide_b, wide_b_h))):

                def body(z, carry):
                    wide[c, z] = narrow[c, z].astype(F32)
                    return carry

                lax.fori_loop(0, Z, body, 0)
                stores.append(pltpu.make_async_copy(wide.at[c], out.at[c], store_sem.at[i, c]))
                stores[-1].start()
        for store in stores:
            store.wait()

    vmem = pl.BlockSpec(memory_space=pltpu.VMEM)
    hbm = pl.BlockSpec(memory_space=pltpu.HBM)
    shape = jax.ShapeDtypeStruct((C, Z, yl, LANES), F32)
    wide = pltpu.VMEM((C, Z, yl, LANES), F32)
    return pl.pallas_call(
        kernel,
        out_shape=(shape, shape),
        in_specs=[vmem, vmem],
        out_specs=(hbm, hbm),
        scratch_shapes=[wide, wide, pltpu.SemaphoreType.DMA((2, C))],
        compiler_params=pltpu.CompilerParams(vmem_limit_bytes=16 << 20),
        name="widen",
    )(grad_vort, grad_vel)


def local(cot_vort, cot_vel, vorticity, velocity):
    C, Z, yl, _ = cot_vel.shape
    spectral = make_spectral(C, Z, yl, lax.axis_size("gx"), lax.axis_size("gy"))
    return widen(*spectral(cot_vel, cot_vort, velocity, vorticity))


def solution(mesh):
    return jax.shard_map(
        local,
        mesh=mesh,
        in_specs=(
            P(None, None, "gy", "gx"),
            P(None, None, "gy", "gx"),
            P(None, None, "gy", "gx"),
            P(None, None, "gy", "gx"),
        ),
        out_specs=(P(None, None, "gy", "gx"), P(None, None, "gy", "gx")),
        check_vma=False,
    )
```

```python
import math

import jax
import jax.numpy as jnp
import numpy as np
from jax import lax
from jax.experimental import pallas as pl
from jax.experimental.pallas import tpu as pltpu
from jax.sharding import PartitionSpec as P

step_size = 0.5
F32 = jnp.float32
BF16 = jnp.bfloat16
LANES = 128
ROWS = 16
MESH = pl.DeviceIdType.MESH
EMPTY = 1


def seed(alpha, beta, length):
    turns = np.concatenate([beta, alpha], 0) % length
    angles = turns * (2.0 * np.pi / length)
    return np.stack([np.cos(angles), np.sin(angles)]).astype(np.float32)


def y_modes(Y, chunks):
    half = chunks // 2
    per = (Y // 2) // chunks
    row = np.arange(Y)
    chunk, part, index = row // (2 * per), (row // per) % 2, row % per
    return 2 * ((chunk % half) * per + index) + chunk // half, part


def tables(X, Y, chunks):
    modes, part = y_modes(Y, chunks)
    quarter = Y // 4
    yy = np.arange(Y // 2)
    start = np.arange(0, Y, ROWS)
    forward_y = seed(
        modes[start][:, None] * yy + quarter * part[start][:, None],
        2 * np.arange(ROWS)[:, None] * yy,
        Y,
    )
    block = np.arange(0, Y // 2, ROWS)
    inverse_y = seed(
        block[:, None] * modes + quarter * part, np.arange(ROWS)[:, None] * modes, Y
    )
    Q = X // 4
    k = np.arange(Q)
    freq = np.concatenate([4 * k + r for r in range(4) for _ in range(2)])
    shift = np.concatenate([np.full(Q, s * (X // 4)) for _ in range(4) for s in range(2)])
    block = np.arange(0, Q, ROWS)
    forward_x = seed(block[:, None] * freq - shift, np.arange(ROWS)[:, None] * freq, X)
    xx = np.concatenate([k, k])
    shift = np.concatenate([np.zeros(Q), np.full(Q, X // 4)]).astype(np.int64)
    first = np.concatenate([4 * block + r for r in range(4)])
    inverse_x = seed(first[:, None] * xx - shift, 4 * np.arange(ROWS)[:, None] * xx, X)
    return forward_y, inverse_y, forward_x, inverse_x


def combine(terms):
    total = None
    for factor, value in terms:
        if abs(factor) < 1e-12:
            continue
        if total is None:
            total = value if factor == 1.0 else (-value if factor == -1.0 else value * factor)
        elif factor == 1.0:
            total = total + value
        elif factor == -1.0:
            total = total - value
        else:
            total = total + value * factor
    return total


def trig(kind, product, Z):
    value = (math.cos if kind == "c" else math.sin)(2.0 * math.pi * (product % Z) / Z)
    nearest = round(value)
    return float(nearest) if abs(value - nearest) < 1e-12 else value


def depth_forward(f, Z):
    H = Z // 2
    even = [f[0]] + [f[z] + f[Z - z] for z in range(1, H)] + [f[H]]
    odd = [None] + [f[z] - f[Z - z] for z in range(1, H)]
    real, imag = [None] * H, [None] * H
    for k in range(H // 2 + 1):
        a = combine([(trig("c", k * z, Z), even[z]) for z in range(0, H + 1, 2)])
        b = combine([(trig("c", k * z, Z), even[z]) for z in range(1, H + 1, 2)])
        total = a if b is None else (b if a is None else a + b)
        real[k] = total
        if 0 < k < H - k:
            real[H - k] = a if b is None else (-b if a is None else a - b)
        if k == 0:
            continue
        a = combine([(trig("s", k * z, Z), odd[z]) for z in range(2, H, 2)])
        b = combine([(trig("s", k * z, Z), odd[z]) for z in range(1, H, 2)])
        imag[k] = -(a if b is None else (b if a is None else a + b))
        if k < H - k:
            imag[H - k] = -b if a is None else (a if b is None else a - b)
    planes = []
    for k in range(H):
        planes += [real[k], jnp.zeros_like(real[0]) if k == 0 else imag[k]]
    return planes


def depth_inverse(planes, Z):
    H = Z // 2
    s = [planes[2 * k] for k in range(H)]
    d = [planes[2 * k + 1] for k in range(H)]
    even, odd = [None] * (H + 1), [None] * (H + 1)
    for z in range(H // 2 + 1):
        a = combine([((1.0 if k == 0 else 2.0 * trig("c", k * z, Z)), s[k]) for k in range(0, H, 2)])
        b = combine([(2.0 * trig("c", k * z, Z), s[k]) for k in range(1, H, 2)])
        even[z] = a if b is None else a + b
        even[H - z] = a if b is None else a - b
        if z == 0:
            continue
        a = combine([(2.0 * trig("s", k * z, Z), d[k]) for k in range(2, H, 2)])
        b = combine([(2.0 * trig("s", k * z, Z), d[k]) for k in range(1, H, 2)])
        odd[z] = a if b is None else (b if a is None else a + b)
        odd[H - z] = -a if b is None else (b if a is None else b - a)
    out = [None] * Z
    out[0], out[H] = even[0], even[H]
    for z in range(1, H):
        out[z] = even[z] + odd[z]
        out[Z - z] = even[z] - odd[z]
    return out


def make_spectral(C, Z, yl, NX, NY):
    X, Y = NX * LANES, NY * yl
    assert NY == Z
    chunks = NX * 2
    per = (Y // 2) // chunks
    pair = 2 * per
    half_y = Y // 2
    Q = X // 4
    wide = Q // LANES
    scale = 2.0 / (X * Y * Z)
    seeds = tables(X, Y, chunks)
    group = 4

    def kernel(
        cv_h,
        cw_h,
        ve_h,
        vo_h,
        sfy_h,
        siy_h,
        sfx_h,
        six_h,
        gv_out,
        gl_out,
        cv,
        adj,
        ve,
        vo,
        vel_slope,
        shift,
        px,
        yp,
        edge_rows,
        edge_cols,
        rows_f,
        cols_f,
        rows_out,
        cols_out,
        rows_in,
        cols_in,
        sfy,
        siy,
        sfx,
        six,
        fwd_y,
        inv_y,
        fwd_x,
        inv_x,
        weights,
        zb,
        fy,
        ys,
        xr,
        lx,
        raw,
        back,
        filt,
        xb,
        yr,
        sp,
        zr,
        load_sem,
        seed_sem,
        send_sem,
        recv_sem,
        halo_send,
        halo_recv,
    ):
        gx = lax.axis_index("gx")
        gy = lax.axis_index("gy")
        core = lax.rem(gy, 2)
        base = gy - core
        mine = gx * 2 + core

        cv_loads = []
        for c in range(C):
            cv_loads.append(pltpu.make_async_copy(cv_h.at[c], cv.at[c], load_sem.at[c]))
            cv_loads[-1].start()
        field_loads = []
        for i, (src, dst) in enumerate(((ve_h, ve), (vo_h, vo), (cw_h, adj))):
            field_loads.append(pltpu.make_async_copy(src, dst, load_sem.at[C + i]))
            field_loads[-1].start()

        barrier = pltpu.get_barrier_semaphore()
        right, left = (lax.rem(gx + 1, NX), gy), (lax.rem(gx + NX - 1, NX), gy)
        after, before = (gx, lax.rem(gy + 1, NY)), (gx, lax.rem(gy + NY - 1, NY))

        def greet_y(k, carry):
            pl.semaphore_signal(
                barrier, inc=1, device_id=(gx, lax.rem(gy + k, NY)), device_id_type=MESH
            )
            return carry

        lax.fori_loop(1, NY, greet_y, 0)

        def greet_x(k, carry):
            t = lax.rem(mine + k, chunks)
            pl.semaphore_signal(
                barrier, inc=1, device_id=(t // 2, base + lax.rem(t, 2)), device_id_type=MESH
            )
            return carry

        lax.fori_loop(1, chunks, greet_x, 0)

        loads = []
        for i, (src, dst) in enumerate(((sfy_h, sfy), (sfx_h, sfx), (siy_h, siy), (six_h, six))):
            loads.append(pltpu.make_async_copy(src, dst, seed_sem.at[i]))
            loads[-1].start()

        def z_block(c, b):
            rows = pl.ds(pl.multiple_of(b * ROWS, ROWS), ROWS)
            planes = depth_forward([cv[c, z, rows, :] for z in range(Z)], Z)
            for k in range(Z):
                if k != EMPTY:
                    zb[c, k, rows, :] = planes[k].astype(BF16)

        def send_planes(c):
            row = pl.ds(pl.multiple_of(gy * yl, yl), yl)

            def body(k, carry):
                dst = lax.rem(gy + k, NY)

                @pl.when(dst != EMPTY)
                def _():
                    pltpu.make_async_remote_copy(
                        src_ref=zb.at[c, dst],
                        dst_ref=fy.at[c, row],
                        send_sem=send_sem.at[0, c],
                        recv_sem=recv_sem.at[0, c],
                        device_id=(gx, dst),
                        device_id_type=MESH,
                    ).start()

                return carry

            lax.fori_loop(1, NY, body, 0)

            @pl.when(gy != EMPTY)
            def _():
                pltpu.make_async_copy(zb.at[c, gy], fy.at[c, row], recv_sem.at[0, c]).start()

            @pl.when(gy == EMPTY)
            def _():
                fy[c] = jnp.zeros((Y, LANES), BF16)

        for c in (1, 2, 0):
            cv_loads[c].wait()
            lax.fori_loop(0, yl // ROWS, lambda b, carry, c=c: (z_block(c, b), carry)[1], 0)
            if c == 1:
                pl.semaphore_wait(barrier, NY - 1 + chunks - 1)
            send_planes(c)

        lane = lax.broadcasted_iota(jnp.int32, (yl, LANES), 1)
        line = lax.broadcasted_iota(jnp.int32, (yl, LANES), 0)
        quarter = 0.5 * step_size

        def send_halo(stage, first, count):
            copies = []
            for i, (src, dst, device) in enumerate(
                (
                    (rows_out.at[1, first : first + count], rows_in.at[0, first : first + count], after),
                    (rows_out.at[0, first : first + count], rows_in.at[1, first : first + count], before),
                    (cols_out.at[stage], cols_in.at[0, stage], right),
                    (cols_out.at[stage], cols_in.at[1, stage], left),
                )
            ):
                copies.append(
                    pltpu.make_async_remote_copy(
                        src_ref=src,
                        dst_ref=dst,
                        send_sem=halo_send.at[stage, i],
                        recv_sem=halo_recv.at[stage, i],
                        device_id=device,
                        device_id_type=MESH,
                    )
                )
                copies[-1].start()
            return copies

        def take_halo(copies, stage, first, count, factor):
            for copy in copies:
                copy.wait()
            rows_f[:, first : first + count] = rows_in[:, first : first + count].astype(F32)
            from_left = pltpu.roll(cols_in[0, stage].astype(F32), 2, 1)
            from_right = cols_in[1, stage].astype(F32)
            if factor is not None:
                from_left, from_right = -factor * from_left, factor * from_right
            cols_f[stage] = jnp.where(lane % 2 == 0, from_right, from_left)

        def at_edges(cols, index):
            moved = pltpu.roll(cols, LANES - 1 - 2 * index, 1)
            return jnp.where((lane == 0) | (lane == LANES - 1), moved, 0.0)

        def slope_y(slot, f, low, high):
            yp[slot, 8 : 8 + yl, :] = f
            yp[slot, 7:8, :] = low
            yp[slot, 8 + yl : 9 + yl, :] = high
            return yp[slot, 9 : 9 + yl, :] - yp[slot, 7 : 7 + yl, :]

        row_index = lax.broadcasted_iota(jnp.int32, (LANES, LANES), 0)
        col_index = lax.broadcasted_iota(jnp.int32, (LANES, LANES), 1)
        shift[...] = jnp.where(
            row_index == col_index + 1, quarter, jnp.where(row_index == col_index - 1, -quarter, 0.0)
        ).astype(BF16)

        field_loads[0].wait()
        field_loads[1].wait()

        slots = lax.rem(lane + 1, LANES) // 2

        def pack_plane(z, acc):
            for i in range(C + 1):
                plane = (ve[i, z] if i < C else vo[0, z]).astype(F32)
                acc = jnp.where(slots == i * Z + z, pltpu.roll(plane, 2 * (i * Z + z), 1), acc)
                edge = plane if i < C else vo[1, z].astype(F32)
                rows_f[0, i, pl.ds(z, 1), :] = edge[0:1]
                rows_f[1, i, pl.ds(z, 1), :] = edge[yl - 1 : yl]
            return acc

        cols_out[0] = lax.fori_loop(0, Z, pack_plane, jnp.zeros((yl, LANES), F32)).astype(BF16)
        rows_out[:, 0 : C + 1] = rows_f[:, 0 : C + 1].astype(BF16)
        field_halo = send_halo(0, 0, C + 1)

        def build(dst, table, count, width):
            def body(a, carry):
                row = pl.ds(ROWS + a, 1)
                value = table[0, 0:ROWS, :] * table[0, row, :] - table[1, 0:ROWS, :] * table[1, row, :]
                dst[pl.ds(pl.multiple_of(a * ROWS, ROWS), ROWS), :] = value.astype(BF16)
                return carry

            lax.fori_loop(0, count, body, 0)

        loads[0].wait()
        build(fwd_y, sfy, Y // ROWS, half_y)

        def y_stage(i, carry):
            c = lax.rem(i + 1, C)

            @pl.when(gy != EMPTY)
            def _():
                pltpu.make_async_copy(fy.at[c], fy.at[c], recv_sem.at[0, c]).wait()

            low = fy[c, 0:half_y, :].astype(F32)
            high = fy[c, half_y:Y, :].astype(F32)
            ys[c, 0:half_y, :] = jnp.dot(
                fwd_y[0:half_y, :], (low + high).astype(BF16), preferred_element_type=F32
            ).astype(BF16)
            ys[c, half_y:Y, :] = jnp.dot(
                fwd_y[half_y:Y, :], (low - high).astype(BF16), preferred_element_type=F32
            ).astype(BF16)

            def body(k, carry):
                t = lax.rem(mine + k, chunks)
                pltpu.make_async_remote_copy(
                    src_ref=ys.at[c, pl.ds(pl.multiple_of(t * pair, pair), pair)],
                    dst_ref=xr.at[c, core, gx],
                    send_sem=send_sem.at[1, c],
                    recv_sem=recv_sem.at[1, c],
                    device_id=(t // 2, base + lax.rem(t, 2)),
                    device_id_type=MESH,
                ).start()
                return carry

            lax.fori_loop(1, chunks, body, 0)
            pltpu.make_async_copy(
                ys.at[c, pl.ds(pl.multiple_of(mine * pair, pair), pair)],
                xr.at[c, core, gx],
                recv_sem.at[1, c],
            ).start()
            return carry

        lax.fori_loop(0, C, y_stage, 0)

        loads[1].wait()
        build(fwd_x, sfx, Q // ROWS, 8 * Q)
        loads[2].wait()
        build(inv_y, siy, half_y // ROWS, Y)
        loads[3].wait()
        build(inv_x, six, 4 * Q // ROWS, 2 * Q)

        depth_wave = (gy // 2).astype(F32) * (2.0 * math.pi / Z)
        chunk_half = mine // (chunks // 2)
        first_mode = 2 * lax.rem(mine, chunks // 2) * per + chunk_half
        mode = first_mode + 2 * lax.broadcasted_iota(jnp.int32, (per, Q), 0)
        wave_y = mode.astype(F32) * (2.0 * math.pi / Y)
        for r in range(4):
            kx = 4 * lax.broadcasted_iota(jnp.int32, (per, Q), 1) + r
            wave_x = jnp.where(kx < X // 2, kx, kx - X).astype(F32) * (2.0 * math.pi / X)
            square = wave_x * wave_x + wave_y * wave_y + depth_wave * depth_wave
            weight = jnp.where(square > 0, 1.0 / jnp.where(square > 0, square, 1.0), 0.0)
            weight = jnp.where(kx == X // 2, 0.0, weight)
            weight = scale * jnp.where(mode == 0, 0.5 * weight, weight)
            weights[r, 0] = weight * wave_x
            weights[r, 1] = weight * wave_y
            weights[r, 2] = weight * depth_wave

        take_halo(field_halo, 0, 0, C + 1, quarter)
        edge_cols[...] = pltpu.roll(cols_f[0], LANES - 2 * C * Z, 1)

        def velocity_slopes(i, carry):
            flat = ve[i].reshape(Z * yl, LANES)
            vel_slope[0, i] = jnp.dot(flat, shift[...], preferred_element_type=F32).reshape(Z, yl, LANES)

            def layer(b, carry):
                for n in range(group):
                    z = b * group + n
                    up, down = lax.rem(z + 1, Z), lax.rem(z + Z - 1, Z)
                    vel_slope[0, i, z] = vel_slope[0, i, z] + at_edges(cols_f[0], i * Z + z)
                    vel_slope[1, i, z] = quarter * slope_y(
                        n, ve[i, z].astype(F32), rows_f[0, i, pl.ds(z, 1), :], rows_f[1, i, pl.ds(z, 1), :]
                    )
                    vel_slope[2, i, z] = quarter * (ve[i, up].astype(F32) - ve[i, down].astype(F32))
                return carry

            return lax.fori_loop(0, Z // group, layer, carry)

        lax.fori_loop(0, C, velocity_slopes, 0)

        def x_stage(c, carry):
            pltpu.make_async_copy(xr.at[c], xr.at[c], recv_sem.at[1, c]).wait()
            for p in range(2):
                for b in range(per // ROWS):
                    for h in range(wide):
                        a = []
                        for part in range(2):
                            rows = slice(part * per + b * ROWS, part * per + (b + 1) * ROWS)
                            a.append([xr[c, p, j * wide + h, rows, :].astype(F32) for j in range(4)])
                        (r0, r1, r2, r3), (i0, i1, i2, i3) = a
                        sr, dr, tr, er = r0 + r2, r0 - r2, r1 + r3, r1 - r3
                        si, di, ti, ei = i0 + i2, i0 - i2, i1 + i3, i1 - i3
                        values = (
                            (sr + tr, si + ti),
                            (dr + ei, di - er),
                            (sr - tr, si - ti),
                            (dr - ei, di + er),
                        )
                        for r in range(4):
                            for part in range(2):
                                row = p * pair + part * per + b * ROWS
                                lx[r, row : row + ROWS, h * LANES : (h + 1) * LANES] = values[r][
                                    part
                                ].astype(BF16)
            for r in range(4):
                raw[c, r] = jnp.dot(
                    lx[r], fwd_x[:, r * 2 * Q : (r + 1) * 2 * Q], preferred_element_type=F32
                )
            return carry

        lax.fori_loop(1, C, x_stage, 0)

        def filter_block(r, first):
            for b in range(per // ROWS):
                for h in range(wide):
                    cols = slice(h * LANES, (h + 1) * LANES)
                    sins = slice(Q + h * LANES, Q + (h + 1) * LANES)

                    def spectrum(c, p):
                        re = slice(p * pair + b * ROWS, p * pair + (b + 1) * ROWS)
                        im = slice(p * pair + per + b * ROWS, p * pair + per + (b + 1) * ROWS)
                        real = raw[c, r, re, cols] + raw[c, r, im, sins]
                        imag = raw[c, r, im, cols] - raw[c, r, re, sins]
                        return real, imag

                    wrow = slice(b * ROWS, (b + 1) * ROWS)
                    ax = weights[r, 0, wrow, cols]
                    ay = weights[r, 1, wrow, cols]
                    az = weights[r, 2, wrow, cols]
                    (ry, sy), (rz, sz) = [spectrum(c, 0) for c in (1, 2)]
                    (uy, vy), (uz, vz) = [spectrum(c, 1) for c in (1, 2)]
                    if first:
                        result = {
                            0: (
                                (az * uy - ay * sz, ay * rz + az * vy),
                                (ay * vz + az * ry, az * sy - ay * uz),
                            )
                        }
                    else:
                        (rx, sx), (ux, vx) = spectrum(0, 0), spectrum(0, 1)
                        result = {
                            1: (
                                (ax * sz - az * ux, -(ax * rz + az * vx)),
                                (-(ax * vz + az * rx), ax * uz - az * sx),
                            ),
                            2: (
                                (ay * sx - ax * sy, ax * ry - ay * rx),
                                (ax * vy - ay * vx, ay * ux - ax * uy),
                            ),
                        }
                    for c in result:
                        for p in range(2):
                            for part in range(2):
                                row = p * pair + part * per + b * ROWS
                                filt[c, r, row : row + ROWS, cols] = result[c][p][part].astype(BF16)

        def filter_all(first):
            def body(r, carry):
                filter_block(r, first)
                return carry

            lax.fori_loop(0, 4, body, 0)

        def x_back(c, carry):
            for r in range(4):
                back[r] = jnp.dot(
                    filt[c, r], inv_x[r * Q : (r + 1) * Q, :], preferred_element_type=F32
                )
            for p in range(2):
                for b in range(per // ROWS):
                    for h in range(wide):
                        cols = slice(h * LANES, (h + 1) * LANES)
                        sins = slice(Q + h * LANES, Q + (h + 1) * LANES)
                        re = slice(p * pair + b * ROWS, p * pair + (b + 1) * ROWS)
                        im = slice(p * pair + per + b * ROWS, p * pair + per + (b + 1) * ROWS)
                        real = [back[r, re, cols] - back[r, im, sins] for r in range(4)]
                        imag = [back[r, re, sins] + back[r, im, cols] for r in range(4)]
                        sr, dr, tr, er = real[0] + real[2], real[0] - real[2], real[1] + real[3], real[1] - real[3]
                        si, di, ti, ei = imag[0] + imag[2], imag[0] - imag[2], imag[1] + imag[3], imag[1] - imag[3]
                        values = (
                            (sr + tr, si + ti),
                            (dr - ei, di + er),
                            (sr - tr, si - ti),
                            (dr + ei, di - er),
                        )
                        for j in range(4):
                            for part in range(2):
                                row = part * per + b * ROWS
                                xb[c, p, j * wide + h, row : row + ROWS, :] = values[j][part].astype(BF16)

            dst = pl.ds(pl.multiple_of(mine * pair, pair), pair)

            def body(k, carry):
                t = lax.rem(mine + k, chunks)
                pltpu.make_async_remote_copy(
                    src_ref=xb.at[c, lax.rem(t, 2), t // 2],
                    dst_ref=yr.at[c, dst],
                    send_sem=send_sem.at[2, c],
                    recv_sem=recv_sem.at[2, c],
                    device_id=(t // 2, base + lax.rem(t, 2)),
                    device_id_type=MESH,
                ).start()
                return carry

            lax.fori_loop(1, chunks, body, 0)
            pltpu.make_async_copy(xb.at[c, core, gx], yr.at[c, dst], recv_sem.at[2, c]).start()
            return carry

        filter_all(True)
        lax.fori_loop(0, 1, x_back, 0)
        lax.fori_loop(0, 1, x_stage, 0)
        filter_all(False)
        lax.fori_loop(1, C, x_back, 0)

        def y_back(c, carry):
            pltpu.make_async_copy(yr.at[c], yr.at[c], recv_sem.at[2, c]).wait()
            even = jnp.dot(inv_y[:, 0:half_y], yr[c, 0:half_y, :], preferred_element_type=F32)
            odd = jnp.dot(inv_y[:, half_y:Y], yr[c, half_y:Y, :], preferred_element_type=F32)
            sp[c, 0:half_y, :] = (even + odd).astype(BF16)
            sp[c, half_y:Y, :] = (even - odd).astype(BF16)

            @pl.when(gy != EMPTY)
            def _():
                def body(k, carry):
                    dst = lax.rem(gy + k, NY)
                    pltpu.make_async_remote_copy(
                        src_ref=sp.at[c, pl.ds(pl.multiple_of(dst * yl, yl), yl)],
                        dst_ref=zr.at[c, gy],
                        send_sem=send_sem.at[3, c],
                        recv_sem=recv_sem.at[3, c],
                        device_id=(gx, dst),
                        device_id_type=MESH,
                    ).start()
                    return carry

                lax.fori_loop(1, NY, body, 0)
                pltpu.make_async_copy(
                    sp.at[c, pl.ds(pl.multiple_of(gy * yl, yl), yl)], zr.at[c, gy], recv_sem.at[3, c]
                ).start()

            return carry

        lax.fori_loop(0, C, y_back, 0)

        field_loads[2].wait()
        slots_block = slots[0:ROWS]
        halos = []

        def finish_velocity(c):
            take_halo(halos[c], 1 + c, 4 + c, 1, None)
            cols_f[1 + c] = cols_f[1 + c] * edge_cols[...]
            edge_rows[...] = rows_f[:, C] * rows_f[:, 4 + c]

            def vel_part(b, carry):
                for n in range(group):
                    z = b * group + n
                    px[n * yl : (n + 1) * yl, :] = (vo[0, z].astype(F32) * adj[c, z]).astype(BF16)
                ring = [lax.rem(b * group + n + Z - 1, Z) for n in range(group + 2)]
                along = [vo[2, z].astype(F32) * adj[c, z] for z in ring]
                slopes = jnp.dot(px[...], shift[...], preferred_element_type=F32)
                for n in range(group):
                    z = b * group + n
                    rest = slope_y(
                        n,
                        vo[1, z].astype(F32) * adj[c, z],
                        edge_rows[0, pl.ds(z, 1), :],
                        edge_rows[1, pl.ds(z, 1), :],
                    )
                    rest = rest + (along[n + 2] - along[n])
                    total = slopes[n * yl : (n + 1) * yl] + at_edges(cols_f[1 + c], z)
                    gl_out[c, z] = (-total - quarter * rest).astype(BF16)
                return carry

            lax.fori_loop(0, Z // group, vel_part, 0)

        for c in range(C):
            come = zr.at[c, 0 : Z - 1]
            pltpu.make_async_copy(come, come, recv_sem.at[3, c]).wait()

            def z_back(b, carry, c=c):
                rows = pl.ds(pl.multiple_of(b * ROWS, ROWS), ROWS)
                values = depth_inverse(
                    [None if k == EMPTY else zr[c, k, rows, :].astype(F32) for k in range(Z)],
                    Z,
                )
                acc = jnp.zeros((ROWS, LANES), F32)
                for z in range(Z):
                    value = adj[c, z, rows, :] + values[z]
                    adj[c, z, rows, :] = value
                    acc = jnp.where(slots_block == z, pltpu.roll(value, 2 * z, 1) if z else value, acc)
                cols_out[1 + c, rows, :] = acc.astype(BF16)
                return carry

            lax.fori_loop(0, yl // ROWS, z_back, 0, unroll=2)
            for z in range(Z):
                rows_f[0, 4 + c, z : z + 1, :] = adj[c, z, 0:1, :]
                rows_f[1, 4 + c, z : z + 1, :] = adj[c, z, yl - 1 : yl, :]
            rows_out[:, 4 + c] = rows_f[:, 4 + c].astype(BF16)
            halos.append(send_halo(1 + c, 4 + c, 1))

        def vort_part(z, carry):
            a = [adj[i, z] for i in range(C)]
            for j in range(3):
                total = a[j]
                for i in range(C):
                    total = total + a[i] * vel_slope[j, i, z]
                gv_out[j, z] = total.astype(BF16)
            return carry

        lax.fori_loop(0, Z, vort_part, 0)
        for c in range(C):
            finish_velocity(c)

        for c in range(C):
            sent = zb.at[c, 0 : NY - 2]
            pltpu.make_async_copy(sent, sent, send_sem.at[0, c]).wait()

            @pl.when(gy == EMPTY)
            def _():
                more = zb.at[c, 0]
                pltpu.make_async_copy(more, more, send_sem.at[0, c]).wait()

            sent = ys.at[c, 0 : (chunks - 1) * pair]
            pltpu.make_async_copy(sent, sent, send_sem.at[1, c]).wait()
            sent = yr.at[c, 0 : (chunks - 1) * pair]
            pltpu.make_async_copy(sent, sent, send_sem.at[2, c]).wait()

            @pl.when(gy != EMPTY)
            def _():
                last = sp.at[c, 0 : (NY - 1) * yl]
                pltpu.make_async_copy(last, last, send_sem.at[3, c]).wait()


    def vmem(shape, dtype=BF16):
        return pltpu.VMEM(shape, dtype)

    scratch = [
        vmem((C, Z, yl, LANES), F32),
        vmem((C, Z, yl, LANES), F32),
        vmem((C, Z, yl, LANES)),
        vmem((C, Z, yl, LANES)),
        vmem((3, C, Z, yl, LANES), F32),
        vmem((LANES, LANES)),
        vmem((group * yl, LANES)),
        vmem((group, yl + 16, LANES), F32),
        vmem((2, Z, LANES), F32),
        vmem((yl, LANES), F32),
        vmem((2, 7, Z, LANES), F32),
        vmem((1 + C, yl, LANES), F32),
        vmem((2, 7, Z, LANES)),
        vmem((1 + C, yl, LANES)),
        vmem((2, 7, Z, LANES)),
        vmem((2, 1 + C, yl, LANES)),
    ]
    scratch += [vmem(s.shape, F32) for s in seeds]
    scratch += [
        vmem((Y, half_y)),
        vmem((half_y, Y)),
        vmem((Q, 8 * Q)),
        vmem((4 * Q, 2 * Q)),
        vmem((4, 3, per, Q), F32),
        vmem((C, Z, yl, LANES)),
        vmem((C, Y, LANES)),
        vmem((C, Y, LANES)),
        vmem((C, 2, NX, pair, LANES)),
        vmem((4, 2 * pair, Q)),
        vmem((C, 4, 2 * pair, 2 * Q), F32),
        vmem((4, 2 * pair, 2 * Q), F32),
        vmem((C, 4, 2 * pair, Q)),
        vmem((C, 2, NX, pair, LANES)),
        vmem((C, Y, LANES)),
        vmem((C, Y, LANES)),
        vmem((C, Z, yl, LANES)),
        pltpu.SemaphoreType.DMA((C + 3,)),
        pltpu.SemaphoreType.DMA((4,)),
        pltpu.SemaphoreType.DMA((4, C)),
        pltpu.SemaphoreType.DMA((4, C)),
        pltpu.SemaphoreType.DMA((1 + C, 4)),
        pltpu.SemaphoreType.DMA((1 + C, 4)),
    ]
    call = pl.pallas_call(
        kernel,
        out_shape=(
            jax.ShapeDtypeStruct((C, Z, yl, LANES), BF16),
            jax.ShapeDtypeStruct((C, Z, yl, LANES), BF16),
        ),
        in_specs=[pl.BlockSpec(memory_space=pltpu.HBM)] * 8,
        out_specs=(pl.BlockSpec(memory_space=pltpu.VMEM), pl.BlockSpec(memory_space=pltpu.VMEM)),
        scratch_shapes=scratch,
        compiler_params=pltpu.CompilerParams(
            collective_id=0, has_side_effects=True, vmem_limit_bytes=49 << 20
        ),
        name="spectral",
    )

    def run(cot_vel, cot_vort, velocity, vorticity):
        operands = [cot_vel, cot_vort, velocity, vorticity] + [jnp.asarray(s) for s in seeds]
        return call(*[pltpu.with_memory_space_constraint(x, pltpu.HBM) for x in operands])

    return run


def widen(grad_vort, grad_vel):
    C, Z, yl, _ = grad_vort.shape

    def kernel(a, b, wide_a_h, wide_b_h, wide_a, wide_b, store_sem):
        stores = []
        for c in range(C):
            for i, (narrow, wide, out) in enumerate(((a, wide_a, wide_a_h), (b, wide_b, wide_b_h))):

                def body(z, carry):
                    wide[c, z] = narrow[c, z].astype(F32)
                    return carry

                lax.fori_loop(0, Z, body, 0)
                stores.append(pltpu.make_async_copy(wide.at[c], out.at[c], store_sem.at[i, c]))
                stores[-1].start()
        for store in stores:
            store.wait()

    vmem = pl.BlockSpec(memory_space=pltpu.VMEM)
    hbm = pl.BlockSpec(memory_space=pltpu.HBM)
    shape = jax.ShapeDtypeStruct((C, Z, yl, LANES), F32)
    wide = pltpu.VMEM((C, Z, yl, LANES), F32)
    return pl.pallas_call(
        kernel,
        out_shape=(shape, shape),
        in_specs=[vmem, vmem],
        out_specs=(hbm, hbm),
        scratch_shapes=[wide, wide, pltpu.SemaphoreType.DMA((2, C))],
        compiler_params=pltpu.CompilerParams(vmem_limit_bytes=16 << 20),
        name="widen",
    )(grad_vort, grad_vel)


def local(cot_vort, cot_vel, vorticity, velocity):
    C, Z, yl, _ = cot_vel.shape
    spectral = make_spectral(C, Z, yl, lax.axis_size("gx"), lax.axis_size("gy"))
    return widen(*spectral(cot_vel, cot_vort, velocity, vorticity))


def solution(mesh):
    return jax.shard_map(
        local,
        mesh=mesh,
        in_specs=(
            P(None, None, "gy", "gx"),
            P(None, None, "gy", "gx"),
            P(None, None, "gy", "gx"),
            P(None, None, "gy", "gx"),
        ),
        out_specs=(P(None, None, "gy", "gx"), P(None, None, "gy", "gx")),
        check_vma=False,
    )
```

```python
import math

import jax
import jax.numpy as jnp
import numpy as np
from jax import lax
from jax.experimental import pallas as pl
from jax.experimental.pallas import tpu as pltpu
from jax.sharding import PartitionSpec as P

step_size = 0.5
F32 = jnp.float32
BF16 = jnp.bfloat16
LANES = 128
ROWS = 16
MESH = pl.DeviceIdType.MESH
EMPTY = 1


def seed(alpha, beta, length):
    turns = np.concatenate([beta, alpha], 0) % length
    angles = turns * (2.0 * np.pi / length)
    return np.stack([np.cos(angles), np.sin(angles)]).astype(np.float32)


def y_modes(Y, chunks):
    half = chunks // 2
    per = (Y // 2) // chunks
    row = np.arange(Y)
    chunk, part, index = row // (2 * per), (row // per) % 2, row % per
    return 2 * ((chunk % half) * per + index) + chunk // half, part


def tables(X, Y, chunks):
    modes, part = y_modes(Y, chunks)
    quarter = Y // 4
    yy = np.arange(Y // 2)
    start = np.arange(0, Y, ROWS)
    forward_y = seed(
        modes[start][:, None] * yy + quarter * part[start][:, None],
        2 * np.arange(ROWS)[:, None] * yy,
        Y,
    )
    block = np.arange(0, Y // 2, ROWS)
    inverse_y = seed(
        block[:, None] * modes + quarter * part, np.arange(ROWS)[:, None] * modes, Y
    )
    Q = X // 4
    k = np.arange(Q)
    freq = np.concatenate([4 * k + r for r in range(4) for _ in range(2)])
    shift = np.concatenate([np.full(Q, s * (X // 4)) for _ in range(4) for s in range(2)])
    block = np.arange(0, Q, ROWS)
    forward_x = seed(block[:, None] * freq - shift, np.arange(ROWS)[:, None] * freq, X)
    xx = np.concatenate([k, k])
    shift = np.concatenate([np.zeros(Q), np.full(Q, X // 4)]).astype(np.int64)
    first = np.concatenate([4 * block + r for r in range(4)])
    inverse_x = seed(first[:, None] * xx - shift, 4 * np.arange(ROWS)[:, None] * xx, X)
    return forward_y, inverse_y, forward_x, inverse_x


def combine(terms):
    total = None
    for factor, value in terms:
        if abs(factor) < 1e-12:
            continue
        if total is None:
            total = value if factor == 1.0 else (-value if factor == -1.0 else value * factor)
        elif factor == 1.0:
            total = total + value
        elif factor == -1.0:
            total = total - value
        else:
            total = total + value * factor
    return total


def trig(kind, product, Z):
    value = (math.cos if kind == "c" else math.sin)(2.0 * math.pi * (product % Z) / Z)
    nearest = round(value)
    return float(nearest) if abs(value - nearest) < 1e-12 else value


def depth_forward(f, Z):
    H = Z // 2
    even = [f[0]] + [f[z] + f[Z - z] for z in range(1, H)] + [f[H]]
    odd = [None] + [f[z] - f[Z - z] for z in range(1, H)]
    real, imag = [None] * H, [None] * H
    for k in range(H // 2 + 1):
        a = combine([(trig("c", k * z, Z), even[z]) for z in range(0, H + 1, 2)])
        b = combine([(trig("c", k * z, Z), even[z]) for z in range(1, H + 1, 2)])
        total = a if b is None else (b if a is None else a + b)
        real[k] = total
        if 0 < k < H - k:
            real[H - k] = a if b is None else (-b if a is None else a - b)
        if k == 0:
            continue
        a = combine([(trig("s", k * z, Z), odd[z]) for z in range(2, H, 2)])
        b = combine([(trig("s", k * z, Z), odd[z]) for z in range(1, H, 2)])
        imag[k] = -(a if b is None else (b if a is None else a + b))
        if k < H - k:
            imag[H - k] = -b if a is None else (a if b is None else a - b)
    planes = []
    for k in range(H):
        planes += [real[k], jnp.zeros_like(real[0]) if k == 0 else imag[k]]
    return planes


def depth_inverse(planes, Z):
    H = Z // 2
    s = [planes[2 * k] for k in range(H)]
    d = [planes[2 * k + 1] for k in range(H)]
    even, odd = [None] * (H + 1), [None] * (H + 1)
    for z in range(H // 2 + 1):
        a = combine([((1.0 if k == 0 else 2.0 * trig("c", k * z, Z)), s[k]) for k in range(0, H, 2)])
        b = combine([(2.0 * trig("c", k * z, Z), s[k]) for k in range(1, H, 2)])
        even[z] = a if b is None else a + b
        even[H - z] = a if b is None else a - b
        if z == 0:
            continue
        a = combine([(2.0 * trig("s", k * z, Z), d[k]) for k in range(2, H, 2)])
        b = combine([(2.0 * trig("s", k * z, Z), d[k]) for k in range(1, H, 2)])
        odd[z] = a if b is None else (b if a is None else a + b)
        odd[H - z] = -a if b is None else (b if a is None else b - a)
    out = [None] * Z
    out[0], out[H] = even[0], even[H]
    for z in range(1, H):
        out[z] = even[z] + odd[z]
        out[Z - z] = even[z] - odd[z]
    return out


def make_spectral(C, Z, yl, NX, NY):
    X, Y = NX * LANES, NY * yl
    assert NY == Z
    chunks = NX * 2
    per = (Y // 2) // chunks
    pair = 2 * per
    half_y = Y // 2
    Q = X // 4
    wide = Q // LANES
    scale = 2.0 / (X * Y * Z)
    seeds = tables(X, Y, chunks)
    group = 4

    def kernel(
        cv_h,
        cw_h,
        ve_h,
        vo_h,
        sfy_h,
        siy_h,
        sfx_h,
        six_h,
        gv_out,
        gl_out,
        cv,
        adj,
        ve,
        vo,
        vel_slope,
        shift,
        px,
        yp,
        edge_rows,
        edge_cols,
        rows_f,
        cols_f,
        rows_out,
        cols_out,
        rows_in,
        cols_in,
        sfy,
        siy,
        sfx,
        six,
        fwd_y,
        inv_y,
        fwd_x,
        inv_x,
        weights,
        zb,
        fy,
        ys,
        xr,
        lx,
        raw,
        back,
        filt,
        xb,
        yr,
        sp,
        zr,
        load_sem,
        seed_sem,
        send_sem,
        recv_sem,
        halo_send,
        halo_recv,
    ):
        gx = lax.axis_index("gx")
        gy = lax.axis_index("gy")
        core = lax.rem(gy, 2)
        base = gy - core
        mine = gx * 2 + core

        cv_loads = []
        for c in range(C):
            cv_loads.append(pltpu.make_async_copy(cv_h.at[c], cv.at[c], load_sem.at[c]))
            cv_loads[-1].start()
        field_loads = []
        for i, (src, dst) in enumerate(((ve_h, ve), (vo_h, vo), (cw_h, adj))):
            field_loads.append(pltpu.make_async_copy(src, dst, load_sem.at[C + i]))
            field_loads[-1].start()

        barrier = pltpu.get_barrier_semaphore()
        right, left = (lax.rem(gx + 1, NX), gy), (lax.rem(gx + NX - 1, NX), gy)
        after, before = (gx, lax.rem(gy + 1, NY)), (gx, lax.rem(gy + NY - 1, NY))

        def greet_y(k, carry):
            pl.semaphore_signal(
                barrier, inc=1, device_id=(gx, lax.rem(gy + k, NY)), device_id_type=MESH
            )
            return carry

        lax.fori_loop(1, NY, greet_y, 0)

        def greet_x(k, carry):
            t = lax.rem(mine + k, chunks)
            pl.semaphore_signal(
                barrier, inc=1, device_id=(t // 2, base + lax.rem(t, 2)), device_id_type=MESH
            )
            return carry

        lax.fori_loop(1, chunks, greet_x, 0)

        loads = []
        for i, (src, dst) in enumerate(((sfy_h, sfy), (sfx_h, sfx), (siy_h, siy), (six_h, six))):
            loads.append(pltpu.make_async_copy(src, dst, seed_sem.at[i]))
            loads[-1].start()

        def across(k):
            half = NY // 2
            step = k + k // half
            side = lax.rem(gy // half + 1 - step // half, 2)
            return side * half + lax.rem(lax.rem(gy, half) + lax.rem(step, half), half)

        def z_block(c, b):
            rows = pl.ds(pl.multiple_of(b * ROWS, ROWS), ROWS)
            planes = depth_forward([cv[c, z, rows, :] for z in range(Z)], Z)
            for k in range(Z):
                if k != EMPTY:
                    zb[c, k, rows, :] = planes[k].astype(BF16)

        def send_planes(c):
            row = pl.ds(pl.multiple_of(gy * yl, yl), yl)

            def body(k, carry):
                dst = across(k)

                @pl.when(dst != EMPTY)
                def _():
                    pltpu.make_async_remote_copy(
                        src_ref=zb.at[c, dst],
                        dst_ref=fy.at[c, row],
                        send_sem=send_sem.at[0, c],
                        recv_sem=recv_sem.at[0, c],
                        device_id=(gx, dst),
                        device_id_type=MESH,
                    ).start()

                return carry

            lax.fori_loop(0, NY - 1, body, 0)

            @pl.when(gy != EMPTY)
            def _():
                pltpu.make_async_copy(zb.at[c, gy], fy.at[c, row], recv_sem.at[0, c]).start()

            @pl.when(gy == EMPTY)
            def _():
                fy[c] = jnp.zeros((Y, LANES), BF16)

        for c in (1, 2, 0):
            cv_loads[c].wait()
            lax.fori_loop(0, yl // ROWS, lambda b, carry, c=c: (z_block(c, b), carry)[1], 0)
            if c == 1:
                pl.semaphore_wait(barrier, NY - 1 + chunks - 1)
            send_planes(c)

        lane = lax.broadcasted_iota(jnp.int32, (yl, LANES), 1)
        line = lax.broadcasted_iota(jnp.int32, (yl, LANES), 0)
        quarter = 0.5 * step_size

        def send_halo(stage, first, count):
            copies = []
            for i, (src, dst, device) in enumerate(
                (
                    (rows_out.at[1, first : first + count], rows_in.at[0, first : first + count], after),
                    (rows_out.at[0, first : first + count], rows_in.at[1, first : first + count], before),
                    (cols_out.at[stage], cols_in.at[0, stage], right),
                    (cols_out.at[stage], cols_in.at[1, stage], left),
                )
            ):
                copies.append(
                    pltpu.make_async_remote_copy(
                        src_ref=src,
                        dst_ref=dst,
                        send_sem=halo_send.at[stage, i],
                        recv_sem=halo_recv.at[stage, i],
                        device_id=device,
                        device_id_type=MESH,
                    )
                )
                copies[-1].start()
            return copies

        def take_halo(copies, stage, first, count, factor):
            for copy in copies:
                copy.wait()
            rows_f[:, first : first + count] = rows_in[:, first : first + count].astype(F32)
            from_left = pltpu.roll(cols_in[0, stage].astype(F32), 2, 1)
            from_right = cols_in[1, stage].astype(F32)
            if factor is not None:
                from_left, from_right = -factor * from_left, factor * from_right
            cols_f[stage] = jnp.where(lane % 2 == 0, from_right, from_left)

        def at_edges(cols, index):
            moved = pltpu.roll(cols, LANES - 1 - 2 * index, 1)
            return jnp.where((lane == 0) | (lane == LANES - 1), moved, 0.0)

        def slope_y(slot, f, low, high):
            yp[slot, 8 : 8 + yl, :] = f
            yp[slot, 7:8, :] = low
            yp[slot, 8 + yl : 9 + yl, :] = high
            return yp[slot, 9 : 9 + yl, :] - yp[slot, 7 : 7 + yl, :]

        row_index = lax.broadcasted_iota(jnp.int32, (LANES, LANES), 0)
        col_index = lax.broadcasted_iota(jnp.int32, (LANES, LANES), 1)
        shift[...] = jnp.where(
            row_index == col_index + 1, quarter, jnp.where(row_index == col_index - 1, -quarter, 0.0)
        ).astype(BF16)

        field_loads[0].wait()
        field_loads[1].wait()

        slots = lax.rem(lane + 1, LANES) // 2

        def pack_plane(z, acc):
            for i in range(C + 1):
                plane = (ve[i, z] if i < C else vo[0, z]).astype(F32)
                acc = jnp.where(slots == i * Z + z, pltpu.roll(plane, 2 * (i * Z + z), 1), acc)
                edge = plane if i < C else vo[1, z].astype(F32)
                rows_f[0, i, pl.ds(z, 1), :] = edge[0:1]
                rows_f[1, i, pl.ds(z, 1), :] = edge[yl - 1 : yl]
            return acc

        cols_out[0] = lax.fori_loop(0, Z, pack_plane, jnp.zeros((yl, LANES), F32)).astype(BF16)
        rows_out[:, 0 : C + 1] = rows_f[:, 0 : C + 1].astype(BF16)
        field_halo = send_halo(0, 0, C + 1)

        def build(dst, table, count, width):
            def body(a, carry):
                row = pl.ds(ROWS + a, 1)
                value = table[0, 0:ROWS, :] * table[0, row, :] - table[1, 0:ROWS, :] * table[1, row, :]
                dst[pl.ds(pl.multiple_of(a * ROWS, ROWS), ROWS), :] = value.astype(BF16)
                return carry

            lax.fori_loop(0, count, body, 0)

        loads[0].wait()
        build(fwd_y, sfy, Y // ROWS, half_y)

        def y_stage(i, carry):
            c = lax.rem(i + 1, C)

            @pl.when(gy != EMPTY)
            def _():
                pltpu.make_async_copy(fy.at[c], fy.at[c], recv_sem.at[0, c]).wait()

            low = fy[c, 0:half_y, :].astype(F32)
            high = fy[c, half_y:Y, :].astype(F32)
            ys[c, 0:half_y, :] = jnp.dot(
                fwd_y[0:half_y, :], (low + high).astype(BF16), preferred_element_type=F32
            ).astype(BF16)
            ys[c, half_y:Y, :] = jnp.dot(
                fwd_y[half_y:Y, :], (low - high).astype(BF16), preferred_element_type=F32
            ).astype(BF16)

            def body(k, carry):
                t = lax.rem(mine + k, chunks)
                pltpu.make_async_remote_copy(
                    src_ref=ys.at[c, pl.ds(pl.multiple_of(t * pair, pair), pair)],
                    dst_ref=xr.at[c, core, gx],
                    send_sem=send_sem.at[1, c],
                    recv_sem=recv_sem.at[1, c],
                    device_id=(t // 2, base + lax.rem(t, 2)),
                    device_id_type=MESH,
                ).start()
                return carry

            lax.fori_loop(1, chunks, body, 0)
            pltpu.make_async_copy(
                ys.at[c, pl.ds(pl.multiple_of(mine * pair, pair), pair)],
                xr.at[c, core, gx],
                recv_sem.at[1, c],
            ).start()
            return carry

        lax.fori_loop(0, C, y_stage, 0)

        loads[1].wait()
        build(fwd_x, sfx, Q // ROWS, 8 * Q)
        loads[2].wait()
        build(inv_y, siy, half_y // ROWS, Y)
        loads[3].wait()
        build(inv_x, six, 4 * Q // ROWS, 2 * Q)

        depth_wave = (gy // 2).astype(F32) * (2.0 * math.pi / Z)
        chunk_half = mine // (chunks // 2)
        first_mode = 2 * lax.rem(mine, chunks // 2) * per + chunk_half
        mode = first_mode + 2 * lax.broadcasted_iota(jnp.int32, (per, Q), 0)
        wave_y = mode.astype(F32) * (2.0 * math.pi / Y)
        for r in range(4):
            kx = 4 * lax.broadcasted_iota(jnp.int32, (per, Q), 1) + r
            wave_x = jnp.where(kx < X // 2, kx, kx - X).astype(F32) * (2.0 * math.pi / X)
            square = wave_x * wave_x + wave_y * wave_y + depth_wave * depth_wave
            weight = jnp.where(square > 0, 1.0 / jnp.where(square > 0, square, 1.0), 0.0)
            weight = jnp.where(kx == X // 2, 0.0, weight)
            weight = scale * jnp.where(mode == 0, 0.5 * weight, weight)
            weights[r, 0] = weight * wave_x
            weights[r, 1] = weight * wave_y
            weights[r, 2] = weight * depth_wave

        take_halo(field_halo, 0, 0, C + 1, quarter)
        edge_cols[...] = pltpu.roll(cols_f[0], LANES - 2 * C * Z, 1)

        def velocity_slopes(i, carry):
            flat = ve[i].reshape(Z * yl, LANES)
            vel_slope[0, i] = jnp.dot(flat, shift[...], preferred_element_type=F32).reshape(Z, yl, LANES)

            def layer(b, carry):
                for n in range(group):
                    z = b * group + n
                    up, down = lax.rem(z + 1, Z), lax.rem(z + Z - 1, Z)
                    vel_slope[0, i, z] = vel_slope[0, i, z] + at_edges(cols_f[0], i * Z + z)
                    vel_slope[1, i, z] = quarter * slope_y(
                        n, ve[i, z].astype(F32), rows_f[0, i, pl.ds(z, 1), :], rows_f[1, i, pl.ds(z, 1), :]
                    )
                    vel_slope[2, i, z] = quarter * (ve[i, up].astype(F32) - ve[i, down].astype(F32))
                return carry

            return lax.fori_loop(0, Z // group, layer, carry)

        lax.fori_loop(0, C, velocity_slopes, 0)

        def x_stage(c, carry):
            pltpu.make_async_copy(xr.at[c], xr.at[c], recv_sem.at[1, c]).wait()
            for p in range(2):
                for b in range(per // ROWS):
                    for h in range(wide):
                        a = []
                        for part in range(2):
                            rows = slice(part * per + b * ROWS, part * per + (b + 1) * ROWS)
                            a.append([xr[c, p, j * wide + h, rows, :].astype(F32) for j in range(4)])
                        (r0, r1, r2, r3), (i0, i1, i2, i3) = a
                        sr, dr, tr, er = r0 + r2, r0 - r2, r1 + r3, r1 - r3
                        si, di, ti, ei = i0 + i2, i0 - i2, i1 + i3, i1 - i3
                        values = (
                            (sr + tr, si + ti),
                            (dr + ei, di - er),
                            (sr - tr, si - ti),
                            (dr - ei, di + er),
                        )
                        for r in range(4):
                            for part in range(2):
                                row = p * pair + part * per + b * ROWS
                                lx[r, row : row + ROWS, h * LANES : (h + 1) * LANES] = values[r][
                                    part
                                ].astype(BF16)
            for r in range(4):
                raw[c, r] = jnp.dot(
                    lx[r], fwd_x[:, r * 2 * Q : (r + 1) * 2 * Q], preferred_element_type=F32
                )
            return carry

        lax.fori_loop(1, C, x_stage, 0)

        def filter_block(r, first):
            for b in range(per // ROWS):
                for h in range(wide):
                    cols = slice(h * LANES, (h + 1) * LANES)
                    sins = slice(Q + h * LANES, Q + (h + 1) * LANES)

                    def spectrum(c, p):
                        re = slice(p * pair + b * ROWS, p * pair + (b + 1) * ROWS)
                        im = slice(p * pair + per + b * ROWS, p * pair + per + (b + 1) * ROWS)
                        real = raw[c, r, re, cols] + raw[c, r, im, sins]
                        imag = raw[c, r, im, cols] - raw[c, r, re, sins]
                        return real, imag

                    wrow = slice(b * ROWS, (b + 1) * ROWS)
                    ax = weights[r, 0, wrow, cols]
                    ay = weights[r, 1, wrow, cols]
                    az = weights[r, 2, wrow, cols]
                    (ry, sy), (rz, sz) = [spectrum(c, 0) for c in (1, 2)]
                    (uy, vy), (uz, vz) = [spectrum(c, 1) for c in (1, 2)]
                    if first:
                        result = {
                            0: (
                                (az * uy - ay * sz, ay * rz + az * vy),
                                (ay * vz + az * ry, az * sy - ay * uz),
                            )
                        }
                    else:
                        (rx, sx), (ux, vx) = spectrum(0, 0), spectrum(0, 1)
                        result = {
                            1: (
                                (ax * sz - az * ux, -(ax * rz + az * vx)),
                                (-(ax * vz + az * rx), ax * uz - az * sx),
                            ),
                            2: (
                                (ay * sx - ax * sy, ax * ry - ay * rx),
                                (ax * vy - ay * vx, ay * ux - ax * uy),
                            ),
                        }
                    for c in result:
                        for p in range(2):
                            for part in range(2):
                                row = p * pair + part * per + b * ROWS
                                filt[c, r, row : row + ROWS, cols] = result[c][p][part].astype(BF16)

        def filter_all(first):
            def body(r, carry):
                filter_block(r, first)
                return carry

            lax.fori_loop(0, 4, body, 0)

        def x_back(c, carry):
            for r in range(4):
                back[r] = jnp.dot(
                    filt[c, r], inv_x[r * Q : (r + 1) * Q, :], preferred_element_type=F32
                )
            for p in range(2):
                for b in range(per // ROWS):
                    for h in range(wide):
                        cols = slice(h * LANES, (h + 1) * LANES)
                        sins = slice(Q + h * LANES, Q + (h + 1) * LANES)
                        re = slice(p * pair + b * ROWS, p * pair + (b + 1) * ROWS)
                        im = slice(p * pair + per + b * ROWS, p * pair + per + (b + 1) * ROWS)
                        real = [back[r, re, cols] - back[r, im, sins] for r in range(4)]
                        imag = [back[r, re, sins] + back[r, im, cols] for r in range(4)]
                        sr, dr, tr, er = real[0] + real[2], real[0] - real[2], real[1] + real[3], real[1] - real[3]
                        si, di, ti, ei = imag[0] + imag[2], imag[0] - imag[2], imag[1] + imag[3], imag[1] - imag[3]
                        values = (
                            (sr + tr, si + ti),
                            (dr - ei, di + er),
                            (sr - tr, si - ti),
                            (dr + ei, di - er),
                        )
                        for j in range(4):
                            for part in range(2):
                                row = part * per + b * ROWS
                                xb[c, p, j * wide + h, row : row + ROWS, :] = values[j][part].astype(BF16)

            dst = pl.ds(pl.multiple_of(mine * pair, pair), pair)

            def body(k, carry):
                t = lax.rem(mine + k, chunks)
                pltpu.make_async_remote_copy(
                    src_ref=xb.at[c, lax.rem(t, 2), t // 2],
                    dst_ref=yr.at[c, dst],
                    send_sem=send_sem.at[2, c],
                    recv_sem=recv_sem.at[2, c],
                    device_id=(t // 2, base + lax.rem(t, 2)),
                    device_id_type=MESH,
                ).start()
                return carry

            lax.fori_loop(1, chunks, body, 0)
            pltpu.make_async_copy(xb.at[c, core, gx], yr.at[c, dst], recv_sem.at[2, c]).start()
            return carry

        filter_all(True)
        lax.fori_loop(0, 1, x_back, 0)
        lax.fori_loop(0, 1, x_stage, 0)
        filter_all(False)
        lax.fori_loop(1, C, x_back, 0)

        def y_back(c, carry):
            pltpu.make_async_copy(yr.at[c], yr.at[c], recv_sem.at[2, c]).wait()
            even = jnp.dot(inv_y[:, 0:half_y], yr[c, 0:half_y, :], preferred_element_type=F32)
            odd = jnp.dot(inv_y[:, half_y:Y], yr[c, half_y:Y, :], preferred_element_type=F32)
            sp[c, 0:half_y, :] = (even + odd).astype(BF16)
            sp[c, half_y:Y, :] = (even - odd).astype(BF16)

            @pl.when(gy != EMPTY)
            def _():
                def body(k, carry):
                    dst = across(k)
                    pltpu.make_async_remote_copy(
                        src_ref=sp.at[c, pl.ds(pl.multiple_of(dst * yl, yl), yl)],
                        dst_ref=zr.at[c, gy],
                        send_sem=send_sem.at[3, c],
                        recv_sem=recv_sem.at[3, c],
                        device_id=(gx, dst),
                        device_id_type=MESH,
                    ).start()
                    return carry

                lax.fori_loop(0, NY - 1, body, 0)
                pltpu.make_async_copy(
                    sp.at[c, pl.ds(pl.multiple_of(gy * yl, yl), yl)], zr.at[c, gy], recv_sem.at[3, c]
                ).start()

            return carry

        lax.fori_loop(0, C, y_back, 0)

        field_loads[2].wait()
        slots_block = slots[0:ROWS]
        halos = []

        def finish_velocity(c):
            take_halo(halos[c], 1 + c, 4 + c, 1, None)
            cols_f[1 + c] = cols_f[1 + c] * edge_cols[...]
            edge_rows[...] = rows_f[:, C] * rows_f[:, 4 + c]

            def vel_part(b, carry):
                for n in range(group):
                    z = b * group + n
                    px[n * yl : (n + 1) * yl, :] = (vo[0, z].astype(F32) * adj[c, z]).astype(BF16)
                ring = [lax.rem(b * group + n + Z - 1, Z) for n in range(group + 2)]
                along = [vo[2, z].astype(F32) * adj[c, z] for z in ring]
                slopes = jnp.dot(px[...], shift[...], preferred_element_type=F32)
                for n in range(group):
                    z = b * group + n
                    rest = slope_y(
                        n,
                        vo[1, z].astype(F32) * adj[c, z],
                        edge_rows[0, pl.ds(z, 1), :],
                        edge_rows[1, pl.ds(z, 1), :],
                    )
                    rest = rest + (along[n + 2] - along[n])
                    total = slopes[n * yl : (n + 1) * yl] + at_edges(cols_f[1 + c], z)
                    gl_out[c, z] = (-total - quarter * rest).astype(BF16)
                return carry

            lax.fori_loop(0, Z // group, vel_part, 0)

        for c in range(C):
            come = zr.at[c, 0 : Z - 1]
            pltpu.make_async_copy(come, come, recv_sem.at[3, c]).wait()

            def z_back(b, carry, c=c):
                rows = pl.ds(pl.multiple_of(b * ROWS, ROWS), ROWS)
                values = depth_inverse(
                    [None if k == EMPTY else zr[c, k, rows, :].astype(F32) for k in range(Z)],
                    Z,
                )
                acc = jnp.zeros((ROWS, LANES), F32)
                for z in range(Z):
                    value = adj[c, z, rows, :] + values[z]
                    adj[c, z, rows, :] = value
                    acc = jnp.where(slots_block == z, pltpu.roll(value, 2 * z, 1) if z else value, acc)
                cols_out[1 + c, rows, :] = acc.astype(BF16)
                return carry

            lax.fori_loop(0, yl // ROWS, z_back, 0, unroll=2)
            for z in range(Z):
                rows_f[0, 4 + c, z : z + 1, :] = adj[c, z, 0:1, :]
                rows_f[1, 4 + c, z : z + 1, :] = adj[c, z, yl - 1 : yl, :]
            rows_out[:, 4 + c] = rows_f[:, 4 + c].astype(BF16)
            halos.append(send_halo(1 + c, 4 + c, 1))

        def vort_part(z, carry):
            a = [adj[i, z] for i in range(C)]
            for j in range(3):
                total = a[j]
                for i in range(C):
                    total = total + a[i] * vel_slope[j, i, z]
                gv_out[j, z] = total.astype(BF16)
            return carry

        lax.fori_loop(0, Z, vort_part, 0)
        for c in range(C):
            finish_velocity(c)

        for c in range(C):
            sent = zb.at[c, 0 : NY - 2]
            pltpu.make_async_copy(sent, sent, send_sem.at[0, c]).wait()

            @pl.when(gy == EMPTY)
            def _():
                more = zb.at[c, 0]
                pltpu.make_async_copy(more, more, send_sem.at[0, c]).wait()

            sent = ys.at[c, 0 : (chunks - 1) * pair]
            pltpu.make_async_copy(sent, sent, send_sem.at[1, c]).wait()
            sent = yr.at[c, 0 : (chunks - 1) * pair]
            pltpu.make_async_copy(sent, sent, send_sem.at[2, c]).wait()

            @pl.when(gy != EMPTY)
            def _():
                last = sp.at[c, 0 : (NY - 1) * yl]
                pltpu.make_async_copy(last, last, send_sem.at[3, c]).wait()


    def vmem(shape, dtype=BF16):
        return pltpu.VMEM(shape, dtype)

    scratch = [
        vmem((C, Z, yl, LANES), F32),
        vmem((C, Z, yl, LANES), F32),
        vmem((C, Z, yl, LANES)),
        vmem((C, Z, yl, LANES)),
        vmem((3, C, Z, yl, LANES), F32),
        vmem((LANES, LANES)),
        vmem((group * yl, LANES)),
        vmem((group, yl + 16, LANES), F32),
        vmem((2, Z, LANES), F32),
        vmem((yl, LANES), F32),
        vmem((2, 7, Z, LANES), F32),
        vmem((1 + C, yl, LANES), F32),
        vmem((2, 7, Z, LANES)),
        vmem((1 + C, yl, LANES)),
        vmem((2, 7, Z, LANES)),
        vmem((2, 1 + C, yl, LANES)),
    ]
    scratch += [vmem(s.shape, F32) for s in seeds]
    scratch += [
        vmem((Y, half_y)),
        vmem((half_y, Y)),
        vmem((Q, 8 * Q)),
        vmem((4 * Q, 2 * Q)),
        vmem((4, 3, per, Q), F32),
        vmem((C, Z, yl, LANES)),
        vmem((C, Y, LANES)),
        vmem((C, Y, LANES)),
        vmem((C, 2, NX, pair, LANES)),
        vmem((4, 2 * pair, Q)),
        vmem((C, 4, 2 * pair, 2 * Q), F32),
        vmem((4, 2 * pair, 2 * Q), F32),
        vmem((C, 4, 2 * pair, Q)),
        vmem((C, 2, NX, pair, LANES)),
        vmem((C, Y, LANES)),
        vmem((C, Y, LANES)),
        vmem((C, Z, yl, LANES)),
        pltpu.SemaphoreType.DMA((C + 3,)),
        pltpu.SemaphoreType.DMA((4,)),
        pltpu.SemaphoreType.DMA((4, C)),
        pltpu.SemaphoreType.DMA((4, C)),
        pltpu.SemaphoreType.DMA((1 + C, 4)),
        pltpu.SemaphoreType.DMA((1 + C, 4)),
    ]
    call = pl.pallas_call(
        kernel,
        out_shape=(
            jax.ShapeDtypeStruct((C, Z, yl, LANES), BF16),
            jax.ShapeDtypeStruct((C, Z, yl, LANES), BF16),
        ),
        in_specs=[pl.BlockSpec(memory_space=pltpu.HBM)] * 8,
        out_specs=(pl.BlockSpec(memory_space=pltpu.VMEM), pl.BlockSpec(memory_space=pltpu.VMEM)),
        scratch_shapes=scratch,
        compiler_params=pltpu.CompilerParams(
            collective_id=0, has_side_effects=True, vmem_limit_bytes=49 << 20
        ),
        name="spectral",
    )

    def run(cot_vel, cot_vort, velocity, vorticity):
        operands = [cot_vel, cot_vort, velocity, vorticity] + [jnp.asarray(s) for s in seeds]
        return call(*[pltpu.with_memory_space_constraint(x, pltpu.HBM) for x in operands])

    return run


def widen(grad_vort, grad_vel):
    C, Z, yl, _ = grad_vort.shape

    def kernel(a, b, wide_a_h, wide_b_h, wide_a, wide_b, store_sem):
        stores = []
        for c in range(C):
            for i, (narrow, wide, out) in enumerate(((a, wide_a, wide_a_h), (b, wide_b, wide_b_h))):

                def body(z, carry):
                    wide[c, z] = narrow[c, z].astype(F32)
                    return carry

                lax.fori_loop(0, Z, body, 0)
                stores.append(pltpu.make_async_copy(wide.at[c], out.at[c], store_sem.at[i, c]))
                stores[-1].start()
        for store in stores:
            store.wait()

    vmem = pl.BlockSpec(memory_space=pltpu.VMEM)
    hbm = pl.BlockSpec(memory_space=pltpu.HBM)
    shape = jax.ShapeDtypeStruct((C, Z, yl, LANES), F32)
    wide = pltpu.VMEM((C, Z, yl, LANES), F32)
    return pl.pallas_call(
        kernel,
        out_shape=(shape, shape),
        in_specs=[vmem, vmem],
        out_specs=(hbm, hbm),
        scratch_shapes=[wide, wide, pltpu.SemaphoreType.DMA((2, C))],
        compiler_params=pltpu.CompilerParams(vmem_limit_bytes=16 << 20),
        name="widen",
    )(grad_vort, grad_vel)


def local(cot_vort, cot_vel, vorticity, velocity):
    C, Z, yl, _ = cot_vel.shape
    spectral = make_spectral(C, Z, yl, lax.axis_size("gx"), lax.axis_size("gy"))
    return widen(*spectral(cot_vel, cot_vort, velocity, vorticity))


def solution(mesh):
    return jax.shard_map(
        local,
        mesh=mesh,
        in_specs=(
            P(None, None, "gy", "gx"),
            P(None, None, "gy", "gx"),
            P(None, None, "gy", "gx"),
            P(None, None, "gy", "gx"),
        ),
        out_specs=(P(None, None, "gy", "gx"), P(None, None, "gy", "gx")),
        check_vma=False,
    )
```
